32 devices in a mesh: groups: 2 (over y), ctx: 4 (over z), head: 2 (over x), rep: 2 (over core).
Axes of the slice: x: 2, y: 2, z: 4, core: 2. Of those that a mesh axis runs over, the one named last changes fastest.
Arguments:
- queries: bfloat16 [8192, 16, 2, 128], P(('groups', 'ctx'), 'head', 'rep'), parts along dimension 0, may hold values from -10 to 10
- keys_values: bfloat16 [2, 8192, 16, 128], P('rep', ('groups', 'ctx'), 'head'), parts along dimension 1, may hold values from -6 to 6
- far_list: int32 [64, 16], P('groups'), parts along dimension 0, may hold values from 0 to 31, as said below
- far_count: int32 [64], P('groups'), parts along dimension 0, may hold values from 0 to 8
Outputs:
- attended: bfloat16 [8192, 16, 2, 128], P(('groups', 'ctx'), 'head', 'rep'), parts along dimension 0
The draws below stay inside these ranges and needn't reach their ends.
There are 2 independent parts, one for each index of `groups`. The reference program is written for one: setup_inputs(seed, part) draws one part's arguments, and reference() takes and returns one part's arrays. A program takes and returns all parts, laid end to end along the dimension named above; each array names one. Nothing has to cross between parts.
Inputs may be any that keep to these rules, and one draw needn't show every extreme that they name: `far_list`: for query block c, the entries j < far_count[c] are distinct block numbers no later than c - 4; entries from far_count[c] on are arbitrary and not read. Taken over all query blocks of one span of 1024 tokens, the counted entries name at most 2 distinct blocks of any one span, and some span's query blocks name exactly 2 of some span in every draw.
All inputs are finite; a program needn't handle non-finite values.
Results may differ from the reference program's by a relative error of at most 0.003.
Values may be sent and summed in bfloat16 or wider, within the bound.
A program may use at most 128 MiB of HBM per device.

```python
import jax
import jax.numpy as jnp
from jax import lax

DH = 128
KVH = 16
GQA = 2
BLK = 128
WB = 4
FSEL = 16
CAP = 2
L_DEV = 1024
SEQ = 4096


def draw_queries(key, part):
    own_key = jax.random.fold_in(key, 23)
    drawn = jnp.clip(2.5 * jax.random.normal(own_key, (SEQ, KVH, GQA, DH), jnp.float32), -10.0, 10.0)
    return drawn.astype(jnp.bfloat16)


def draw_keys_values(key, part):
    own_key = jax.random.fold_in(key, 29)
    drawn = jnp.clip(jax.random.normal(own_key, (2, SEQ, KVH, DH), jnp.float32), -6.0, 6.0)
    return drawn.astype(jnp.bfloat16)


def far_tables(key):
    base_key = jax.random.fold_in(key, 5)
    pool_key, order_key, jitter_key, filler_key = jax.random.split(base_key, 4)
    span_blocks = L_DEV // BLK
    span_total = SEQ // L_DEV
    all_blocks = span_blocks * span_total
    local_ids = jnp.arange(span_blocks, dtype=jnp.int32)
    span_ids = jnp.arange(span_total, dtype=jnp.int32)
    raw_scores = jax.random.randint(pool_key, (span_total, span_total, span_blocks), 0, 1 << 20, dtype=jnp.int32)
    too_late = (span_ids[None, :, None] == span_ids[:, None, None]) & (local_ids[None, None, :] >= span_blocks - WB)
    pool_score = raw_scores * span_blocks + local_ids[None, None, :] + too_late.astype(jnp.int32) * (1 << 26)
    pool_order = jnp.argsort(pool_score, axis=-1)[:, :, :CAP].astype(jnp.int32)
    pool_blocks = pool_order + span_ids[None, :, None] * span_blocks
    pool_ok = jnp.broadcast_to(span_ids[None, :, None] <= span_ids[:, None, None], pool_blocks.shape)
    block_ids = jnp.arange(all_blocks, dtype=jnp.int32)
    span_of = block_ids // span_blocks
    pool_width = span_total * CAP
    candidates = pool_blocks[span_of].reshape(all_blocks, pool_width)
    eligible = pool_ok[span_of].reshape(all_blocks, pool_width) & (candidates <= block_ids[:, None] - WB)
    owner_draw = jax.random.randint(order_key, (all_blocks, span_total), 0, 1 << 20, dtype=jnp.int32) * span_total + span_ids[None, :]
    owner_rank = jnp.argsort(jnp.argsort(owner_draw, axis=1), axis=1).astype(jnp.int32)
    slot_key = (owner_rank[:, :, None] * CAP + jnp.arange(CAP, dtype=jnp.int32)[None, None, :]).reshape(all_blocks, pool_width)
    sort_key = jnp.where(eligible, slot_key, slot_key + pool_width)
    picked = jnp.argsort(sort_key, axis=1)
    listed = jnp.take_along_axis(candidates, picked, axis=1).astype(jnp.int32)
    available = jnp.sum(eligible.astype(jnp.int32), axis=1)
    jitter = jax.random.randint(jitter_key, (all_blocks,), 0, 2, dtype=jnp.int32)
    jitter = jnp.where(block_ids == all_blocks - 1, 0, jitter)
    target = FSEL * (span_of + 1) // span_total - jitter
    counts = jnp.clip(jnp.minimum(target, available), 0, FSEL).astype(jnp.int32)
    if pool_width >= FSEL:
        listed = listed[:, :FSEL]
    else:
        listed = jnp.concatenate([listed, jnp.zeros((all_blocks, FSEL - pool_width), jnp.int32)], axis=1)
    filler = jax.random.randint(filler_key, (all_blocks, FSEL), 0, all_blocks, dtype=jnp.int32)
    listed = jnp.where(jnp.arange(FSEL, dtype=jnp.int32)[None, :] < counts[:, None], listed, filler)
    return (listed, counts)


def draw_far_list(key, part):
    return far_tables(key)[0]


def draw_far_count(key, part):
    return far_tables(key)[1]


def setup_inputs(seed: int = 0, part: int = 0) -> dict:
    streams_of = jax.random.split(jax.random.key(seed), 5)
    part_splits = jax.random.split(jax.random.fold_in(streams_of[4], part), 5)
    return {
        "queries": draw_queries(jax.random.fold_in(jax.random.fold_in(streams_of[4], part), 71), part),
        "keys_values": draw_keys_values(jax.random.fold_in(jax.random.fold_in(streams_of[4], part), 71), part),
        "far_list": draw_far_list(jax.random.fold_in(jax.random.fold_in(streams_of[4], part), 71), part),
        "far_count": draw_far_count(jax.random.fold_in(jax.random.fold_in(streams_of[4], part), 71), part),
    }


floor_score = -1.0e30
score_scale = 1.0 / 12.0


def group_weights(scores, usable):
    masked = jnp.where(usable, scores, floor_score)
    summit = jnp.max(masked, axis=-1, keepdims=True)
    weights = jnp.where(usable, jnp.exp(masked - summit), 0.0)
    return summit, weights, jnp.sum(weights, axis=-1, keepdims=True)


def attend(query_tile, keys_tile, values_tile, usable):
    scores = jnp.einsum("qhgd,khd->hgqk", query_tile.astype(jnp.float32), keys_tile.astype(jnp.float32), precision=lax.Precision.HIGHEST) * score_scale
    summit, weights, weight_sum = group_weights(scores, usable)
    light_weights = lax.optimization_barrier(weights.astype(jnp.bfloat16)).astype(jnp.float32)
    mixed_out = jnp.einsum("hgqk,khd->hgqd", light_weights, values_tile.astype(jnp.float32), precision=lax.Precision.HIGHEST)
    return summit, mixed_out, weight_sum


def reference(queries, keys_values, far_list, far_count):
    all_blocks = SEQ // BLK
    query_blocks = queries.reshape(all_blocks, BLK, KVH, GQA, DH)
    key_blocks = keys_values[0].reshape(all_blocks, BLK, KVH, DH)
    value_blocks = keys_values[1].reshape(all_blocks, BLK, KVH, DH)
    inside = jnp.arange(BLK, dtype=jnp.int32)
    window_pos = (jnp.arange(WB, dtype=jnp.int32)[:, None] * BLK + inside[None, :]).reshape(-1)
    slot_range = jnp.arange(FSEL, dtype=jnp.int32)

    def one_block(block_id):
        query_tile = query_blocks[block_id]
        window_ids = block_id - WB + 1 + jnp.arange(WB, dtype=jnp.int32)
        window_ok = jnp.repeat(window_ids >= 0, BLK)
        clipped = jnp.maximum(window_ids, 0).astype(jnp.int32)
        near_keys = key_blocks[clipped].reshape(WB * BLK, KVH, DH)
        near_values = value_blocks[clipped].reshape(WB * BLK, KVH, DH)
        query_pos = (WB - 1) * BLK + inside
        near_usable = (window_pos[None, :] <= query_pos[:, None]) & window_ok[None, :]
        near_top, near_out, near_sum = attend(query_tile, near_keys, near_values, near_usable)
        picked = far_list[block_id].astype(jnp.int32)
        far_keys = key_blocks[picked].reshape(FSEL * BLK, KVH, DH)
        far_values = value_blocks[picked].reshape(FSEL * BLK, KVH, DH)
        far_usable = jnp.repeat(slot_range < far_count[block_id], BLK)[None, :]
        far_top, far_out, far_sum = attend(query_tile, far_keys, far_values, far_usable)
        summit = jnp.maximum(near_top, far_top)
        near_scale = jnp.exp(near_top - summit)
        far_scale = jnp.exp(far_top - summit)
        result = (near_scale * near_out + far_scale * far_out) / (near_scale * near_sum + far_scale * far_sum)
        return jnp.transpose(result, (2, 0, 1, 3)).astype(jnp.bfloat16)

    outputs = lax.map(one_block, jnp.arange(all_blocks, dtype=jnp.int32))
    return outputs.reshape(SEQ, KVH, GQA, DH)
```

```python
import functools
import math

import jax
import jax.numpy as jnp
from jax import lax
from jax.experimental import pallas as pl
from jax.experimental.pallas import tpu as pltpu
from jax.sharding import PartitionSpec as P

BLK = 128
WB = 4
FSEL = 16
CAP = 2

LANES = 128
MASKED = -1e30
SCALE = math.log2(math.e) / 12.0
NT = (((1,), (1,)), ((), ()))


CHAIN = 4
BIG = 1 << 30


def pair_names(spans):
    return [(dst, src) for dst in range(spans) for src in range(dst + 1)]


def where_of(spans, dst, src, k):
    return CAP * pair_names(spans).index((dst, src)) + k


def middle_plan(read, own):
    edge = 2 * own - (WB - 1)
    fresh, rank, blocks = [], [], []
    count = jnp.int32(0)
    for dst in (3, 2):
        for k in range(CAP):
            b = read(dst, 1, k)
            new = (b < BIG) & (b < edge)
            for other in blocks:
                new &= b != other
            fresh.append(new)
            rank.append(count)
            blocks.append(b)
            count = count + jnp.where(new, 1, 0)
    mine = []
    for a in range(2 * CAP):
        b = jnp.int32(BIG)
        for new, r, block in zip(fresh, rank, blocks):
            b = jnp.where(new & (r == a), block, b)
        mine.append(b)
    first = [read(3, 0, k) for k in range(CAP)]
    extra = []
    for k in range(CAP):
        b = read(2, 0, k)
        new = b < BIG
        for other in first:
            new &= b != other
        extra.append(jnp.where(new, b, BIG))
    need = CAP + count + sum(jnp.where(b < BIG, 1, 0) for b in extra)
    return mine, count, first, extra, need


def prelude(spans, own, lists_in, counts, table, choice, share, theirs, sem):
    peer = {"groups": 1 - lax.axis_index("groups")}
    barrier = pltpu.get_barrier_semaphore()
    pl.semaphore_signal(barrier, inc=1, device_id=peer)
    slot = lax.broadcasted_iota(jnp.int32, lists_in.shape, 0)
    block_of = lax.broadcasted_iota(jnp.int32, lists_in.shape, 1)
    listed = jnp.where(slot < counts[...], lists_in[...], -1)
    found = {}
    for dst, src in pair_names(spans):
        inside = ((listed >= src * own) & (listed < src * own + own)
                  & (block_of >= dst * own) & (block_of < dst * own + own))
        first = jnp.min(jnp.where(inside, listed, BIG))
        second = jnp.min(jnp.where(inside & (listed > first), listed, BIG))
        for k, b in enumerate((first, second)):
            found[dst, src, k] = b
            table[where_of(spans, dst, src, k)] = b
    need = middle_plan(lambda dst, src, k: found[dst, src, k], own)[-1]
    share[...] = jnp.broadcast_to(need, share.shape)
    pl.semaphore_wait(barrier, 1)
    swap = pltpu.make_async_remote_copy(
        src_ref=share, dst_ref=theirs, send_sem=sem.at[0], recv_sem=sem.at[1], device_id=peer)
    swap.start()
    swap.wait()
    most = jnp.max(jnp.maximum(share[...], theirs[...]))
    choice[0] = jnp.clip(most - 3 * CAP, 0, CAP)


def relay_kernel(
    spans, room, lists_in, counts, table, q_in, kv_in, out,
    q_raw, raw, mine, loc, rim, relay, sendbuf, qh, acc, top, bias, scr, done, o_raw,
    in_sem, x_sem, rz_send, rz_recv, rf_send, rf_recv,
    z_send, z_recv, f_send, f_recv, out_sem,
):
    toks, heads, dh = q_in.shape
    own = toks // BLK
    me = lax.axis_index("ctx")
    side = lax.axis_index("rep")
    mate = {"rep": 1 - side}
    rims = WB - 1
    pieces = f_send.shape[0] - room + 1
    part_heads = heads // pieces
    has_next = me + 1 < spans
    ahead = {"ctx": lax.rem(me + 1, spans)}
    late, last = room - 2, room - 1

    load_kv = pltpu.make_async_copy(kv_in.at[0], raw, in_sem.at[0])
    load_q = pltpu.make_async_copy(q_in, q_raw, in_sem.at[1])
    load_kv.start()
    load_q.start()

    barrier = pltpu.get_barrier_semaphore()
    pl.semaphore_signal(barrier, inc=1, device_id=mate)

    @pl.when(me > 0)
    def _():
        pl.semaphore_signal(barrier, inc=1, device_id={"ctx": lax.rem(me + spans - 1, spans)})

    def rim_copy(j):
        return pltpu.make_async_remote_copy(
            src_ref=mine.at[own - j], dst_ref=rim.at[side, rims - j],
            send_sem=rz_send.at[j - 1], recv_sem=rz_recv.at[j - 1], device_id=ahead)

    def rim_pass(j):
        return pltpu.make_async_remote_copy(
            src_ref=rim.at[side, rims - j], dst_ref=rim.at[side, rims - j],
            send_sem=rf_send.at[j - 1], recv_sem=rf_recv.at[j - 1], device_id=mate)

    def cut(ref, piece):
        return ref if piece is None else ref.at[pl.ds(piece * part_heads, part_heads)]

    def put(src, p, piece=None):
        at = p if piece is None else p + piece
        return pltpu.make_async_remote_copy(
            src_ref=cut(src, piece), dst_ref=cut(relay.at[side, p], piece),
            send_sem=z_send.at[at], recv_sem=z_recv.at[at], device_id=ahead)

    def came(p, piece=None):
        put(relay.at[side, p], p, piece).wait_recv()

    def hand(p, piece=None):
        at = p if piece is None else p + piece
        return pltpu.make_async_remote_copy(
            src_ref=cut(relay.at[side, p], piece), dst_ref=cut(relay.at[side, p], piece),
            send_sem=f_send.at[at], recv_sem=f_recv.at[at], device_id=mate)

    def put_last(src):
        for piece in range(pieces):
            put(src, last, piece).start()

    parts = scr.shape[0]

    def spread(part, block, store):
        scr[part] = block.astype(jnp.float32).reshape(BLK * heads, dh)
        for h in range(heads):
            store(h, scr[part, pl.ds(h, BLK, stride=heads), :].astype(jnp.bfloat16))

    def spread_mine(b, part):
        def store(h, x):
            mine[b, h] = x
            loc[side, b, h] = x

        spread(part, raw[b], store)

    load_kv.wait()
    for j in range(1, WB):
        spread_mine(own - j, j % parts)
    pl.semaphore_wait(barrier, jnp.where(has_next, 2, 1))

    @pl.when(has_next)
    def _():
        for j in range(1, WB):
            rim_copy(j).start()

    def spread_rest(b, _):
        spread_mine(b, lax.rem(b, parts))
        return 0

    lax.fori_loop(0, own - rims, spread_rest, 0)

    swap = pltpu.make_async_remote_copy(
        src_ref=mine, dst_ref=loc.at[side],
        send_sem=x_sem.at[0], recv_sem=x_sem.at[1], device_id=mate)
    swap.start()

    def read(dst, src, k):
        return table[where_of(spans, dst, src, k)]

    def local_row(block):
        return jnp.clip(jnp.where(block < BIG, block - me * own, 0), 0, own - 1)

    def fill(p, block):
        sendbuf[p] = mine[local_row(block)]

    own_list, own_count, first, extra, _ = middle_plan(read, own)
    own_late, own_last = late - 2, last - 2

    @pl.when(me == 0)
    def _():
        for p, (dst, k) in zip((0, 1, 2, 3, late, last), ((3, 0), (3, 1), (2, 0), (2, 1), (1, 0), (1, 1))):
            fill(p, read(dst, 0, k))
        for p in (0, 1, 2, 3, late):
            put(sendbuf.at[p], p).start()
        put_last(sendbuf.at[last])

    early = [0, 1] + list(range(4, late))

    @pl.when(me == 1)
    def _():
        for p in early:
            fill(p, own_list[p if p < 2 else p - 2])
        for p in early:
            put(sendbuf.at[p], p).start()

    @pl.when(me == 2)
    def _():
        for k in range(CAP):
            fill(k, read(3, 2, k))
        for k in range(CAP):
            put(sendbuf.at[k], k).start()

    @pl.when(me == 0)
    def _():
        for j in range(rims):
            rim[:, j] = jnp.zeros((2,) + rim.shape[2:], rim.dtype)

    held = [0] * room
    for k in range(CAP):
        held[k] = jnp.where(me == 3, read(3, 2, k), own_list[k])
        held[2 + k] = jnp.where(me == 3, read(3, 1, k), first[k])
    for p in range(4, late):
        held[p] = jnp.where(me == 2, own_list[p - 2], BIG)
    both = (extra[0] < BIG) & (extra[1] < BIG)
    mid_late = jnp.where(both, extra[0], BIG)
    mid_last = jnp.where(extra[1] < BIG, extra[1], extra[0])
    if own_late < 2 * CAP:
        mid_late = jnp.where(own_count > own_late, own_list[own_late], mid_late)
    if own_last < 2 * CAP:
        mid_last = jnp.where(own_count > own_last, own_list[own_last], mid_last)
    held[late] = jnp.where(me == 3, read(3, 0, 0), jnp.where(me == 2, mid_late, read(1, 0, 0)))
    held[last] = jnp.where(me == 3, read(3, 0, 1), jnp.where(me == 2, mid_last, read(1, 0, 1)))
    edge = 2 * own - rims
    seen_again = []
    for k in range(CAP):
        b = read(2, 1, k)
        seen_again.append(jnp.where((b < BIG) & (b >= edge) & (me == 2), b, BIG))
    mine_far = []
    for k in range(CAP):
        b = read(0, 0, k)
        for s in range(1, spans):
            b = jnp.where(me == s, read(s, s, k), b)
        mine_far.append(b)

    slot = lax.broadcasted_iota(jnp.int32, lists_in.shape, 0)
    block_of = lax.broadcasted_iota(jnp.int32, lists_in.shape, 1)
    listed = jnp.where(slot < counts[...], lists_in[...], -1)

    for n, block in enumerate(mine_far + seen_again + held + [jnp.int32(BIG)]):
        hit = jnp.max(jnp.where(listed == block, 1.0, 0.0), axis=0, keepdims=True)
        for c in range(own):
            mark = jnp.where(block_of[:1] == me * own + c, hit, 0.0)
            mark = jnp.max(mark, axis=1, keepdims=True)
            bias[n, c] = jnp.broadcast_to(jnp.where(mark > 0.5, 0.0, MASKED), (1, BLK))

    load_q.wait()

    def spread_q(c, _):
        at = pl.ds(pl.multiple_of(c * BLK, BLK), BLK)

        def store(h, x):
            qh[h, at, :] = x

        spread(lax.rem(c, parts), q_raw[at], store)
        return 0

    lax.fori_loop(0, own, spread_q, 0)
    swap.wait_recv()

    span = WB * BLK

    def near_block(c, rows, get):
        key_pos = lax.broadcasted_iota(jnp.int32, (BLK, span), 1) - rims * BLK
        query_pos = lax.broadcasted_iota(jnp.int32, (BLK, span), 0)
        seen = key_pos <= query_pos
        if isinstance(c, int):
            seen &= (key_pos + c * BLK >= 0) | (me > 0)
        for h in range(heads):
            s = lax.dot_general(qh[h, rows, :], get(0, h), NT,
                                preferred_element_type=jnp.float32) * SCALE
            s = jnp.where(seen, s, MASKED)
            m = jnp.max(s, axis=1, keepdims=True)
            p = jnp.exp2(s - m).astype(jnp.bfloat16)
            v = jnp.concatenate([get(1, h), jnp.ones((span, LANES), jnp.bfloat16)], axis=1)
            acc[h, rows, :] = jnp.dot(p, v, preferred_element_type=jnp.float32)
            top[h, rows, :] = jnp.broadcast_to(m, (BLK, LANES))

    def near(c, _):
        keys = pl.ds(c - rims, WB)
        near_block(c, pl.ds(pl.multiple_of(c * BLK, BLK), BLK), lambda kind, h: loc[kind, keys, h].reshape(span, dh))
        return 0

    lax.fori_loop(rims, own, near, 0)

    ones = jnp.ones((BLK, LANES), jnp.bfloat16)

    tall = 2 * BLK

    def merged(h, rows, k, v, row_bias):
        s = lax.dot_general(qh[h, rows, :], k, NT, preferred_element_type=jnp.float32) * SCALE
        s = s + row_bias
        old = top[h, rows, :]
        m = jnp.maximum(old, jnp.max(s, axis=1, keepdims=True))
        spread_m = jnp.concatenate([m] * (s.shape[1] // LANES), axis=1)
        p = jnp.exp2(s - spread_m).astype(jnp.bfloat16)
        a = jnp.exp2(old - m)
        return m, acc[h, rows, :] * jnp.concatenate([a, a], axis=1) + jnp.dot(
            p, v, preferred_element_type=jnp.float32)

    def far_head(h, at, gets, keep, begin=0):
        k = jnp.concatenate([get(0, h) for get in gets], axis=0)
        v = jnp.concatenate([jnp.concatenate([get(1, h), ones], axis=1) for get in gets], axis=0)
        for low in range(begin, toks, tall):
            row_bias = jnp.concatenate([
                jnp.concatenate([jnp.broadcast_to(bias[n, low // BLK + i], (BLK, BLK)) for n in at], axis=1)
                for i in range(tall // BLK)], axis=0)
            rows = pl.ds(low, tall)
            keep(h, low, *merged(h, rows, k, v, row_bias))

    def far(at, gets, begin=0):
        def hold(h, low, m, total):
            acc[h, pl.ds(low, tall), :] = total
            top[h, pl.ds(low, tall), :] = m

        def one(h, _):
            far_head(h, at, gets, hold, begin)
            return 0

        lax.fori_loop(0, heads, one, 0)

    def relayed(p):
        return lambda kind, h: relay[kind, p, h]

    def owned(row):
        return lambda kind, h: loc[kind, row, h]

    def window(row):
        return lambda kind, h: rim[kind, row, h]

    far((0, 1), [owned(local_row(b)) for b in mine_far], WB * BLK // tall * tall)

    @pl.when(me > 0)
    def _():
        for j in range(1, WB):
            rim_copy(j).wait_recv()
            rim_pass(j).start()
        for j in range(1, WB):
            rim_pass(j).wait_recv()

    for c in range(rims):
        near_block(c, pl.ds(c * BLK, BLK), lambda kind, h: jnp.concatenate(
            [rim[kind, r, h] for r in range(c, rims)] + [loc[kind, b, h] for b in range(c + 1)], axis=0))

    base = 2 * CAP

    @pl.when(me == 1)
    def _():
        for k in range(CAP):
            came(k)
            put(relay.at[side, k], 2 + k).start()
        came(2)
        if own_late < 2 * CAP:
            sendbuf[late] = jnp.where(own_count > own_late, mine[local_row(own_list[own_late])], relay[side, 2])
            put(sendbuf.at[late], late).start()
        else:
            put(relay.at[side, 2], late).start()
        came(3)
        tail = jnp.where(extra[1] < BIG, relay[side, 3], relay[side, 2])
        if own_last < 2 * CAP:
            tail = jnp.where(own_count > own_last, mine[local_row(own_list[own_last])], tail)
        sendbuf[last] = tail
        put_last(sendbuf.at[last])

    @pl.when(me == 2)
    def _():
        far((2, 3), [window(jnp.clip(jnp.where(b < BIG, b - edge, 0), 0, rims - 1)) for b in seen_again])
        for k in range(CAP):
            came(k)
            hand(k).start()
            b = read(3, 1, k)
            pick = relay[side, 0]
            if k == 1:
                pick = jnp.where(b == own_list[1], relay[side, 1], pick)
            for j in range(1, WB):
                pick = jnp.where(b == 2 * own - j, rim[side, rims - j], pick)
            sendbuf[2 + k] = pick
            put(sendbuf.at[2 + k], 2 + k).start()

    @pl.when(me == 3)
    def _():
        for k in range(CAP):
            came(k)
            hand(k).start()

    @pl.when(me > 1)
    def _():
        for k in range(CAP):
            hand(k).wait_recv()
        far((base, base + 1), [relayed(0), relayed(1)])

    if late > 4:
        @pl.when(me == 2)
        def _():
            for p in range(4, late):
                came(p)
                hand(p).start()
            for p in range(4, late):
                hand(p).wait_recv()
            at = [base + p for p in range(4, late)]
            far((at + [base + room])[:2], [relayed(p) for p in (4, late - 1)])

    @pl.when(me == 2)
    def _():
        came(2)
        put(relay.at[side, 2], late).start()
        hand(2).start()
        came(3)
        put_last(relay.at[side, 3])
        hand(3).start()

    @pl.when(me == 3)
    def _():
        for p in (2, 3):
            came(p)
            hand(p).start()

    @pl.when(me > 1)
    def _():
        for p in (2, 3):
            hand(p).wait_recv()
        far((base + 2, base + 3), [relayed(2), relayed(3)])

    def finish(h, low, m, total):
        for i in range(tall // BLK):
            part = total[i * BLK:(i + 1) * BLK]
            done[low // BLK + i, pl.ds(h, BLK, stride=heads), :] = part[:, :dh] / part[:, dh:]

    @pl.when(me > 0)
    def _():
        came(late)
        hand(late).start()
        came(last, 0)
        hand(last, 0).start()
        hand(late).wait_recv()

        def one(piece, _):
            @pl.when(piece + 1 < pieces)
            def _():
                came(last, piece + 1)
                hand(last, piece + 1).start()

            hand(last, piece).wait_recv()
            far_head(piece, (base + late, base + last), [relayed(late), relayed(last)], finish)
            return 0

        lax.fori_loop(0, pieces, one, 0)

    @pl.when(me == 0)
    def _():
        def one(h, _):
            for low in range(0, toks, tall):
                finish(h, low, None, acc[h, pl.ds(low, tall), :])
            return 0

        lax.fori_loop(0, heads, one, 0)

    def write(c):
        rows = pl.ds(pl.multiple_of(c * BLK, BLK), BLK)
        return pltpu.make_async_copy(o_raw.at[rows], out.at[rows], out_sem.at[c])

    def pack(c, _):
        rows = pl.ds(pl.multiple_of(c * BLK, BLK), BLK)
        o_raw[rows] = done[c].reshape(BLK, heads, dh).astype(jnp.bfloat16)
        write(c).start()
        return 0

    lax.fori_loop(0, own, pack, 0)

    def drain(c, _):
        write(c).wait()
        return 0

    lax.fori_loop(0, own, drain, 0)
    swap.wait_send()

    @pl.when(has_next)
    def _():
        for j in range(1, WB):
            rim_copy(j).wait_send()
        for p in (0, 1, 2, 3, late):
            put(relay.at[side, p], p).wait_send()
        for piece in range(pieces):
            put(relay.at[side, last], last, piece).wait_send()

    @pl.when(me == 1)
    def _():
        for p in range(4, late):
            put(relay.at[side, p], p).wait_send()

    @pl.when(me > 0)
    def _():
        for j in range(1, WB):
            rim_pass(j).wait_send()
        hand(late).wait_send()
        for piece in range(pieces):
            hand(last, piece).wait_send()

    @pl.when(me > 1)
    def _():
        for p in range(4):
            hand(p).wait_send()

    @pl.when(me == 2)
    def _():
        for p in range(4, late):
            hand(p).wait_send()


def settle(src, out, buf, read_sem, write_sem):
    toks = src.shape[0]
    step = toks // read_sem.shape[0]

    def fetch(i):
        at = pl.ds(i * step, step)
        return pltpu.make_async_copy(src.at[at], buf.at[at], read_sem.at[i])

    def store(i):
        at = pl.ds(i * step, step)
        return pltpu.make_async_copy(buf.at[at], out.at[at], write_sem.at[i])

    for i in range(read_sem.shape[0]):
        fetch(i).start()
    for i in range(read_sem.shape[0]):
        fetch(i).wait()
        store(i).start()
    for i in range(read_sem.shape[0]):
        store(i).wait()


def chained(spans, room, lists, counts, table, queries, keys_values):
    toks, heads, dh = queries.shape
    own = toks // BLK
    rims = WB - 1
    bf16, f32 = jnp.bfloat16, jnp.float32
    hbm = pl.BlockSpec(memory_space=pl.ANY)
    vmem = pl.BlockSpec(memory_space=pltpu.VMEM)
    dma = pltpu.SemaphoreType.DMA
    pieces = heads
    ways = room - 1 + pieces
    return pl.pallas_call(
        functools.partial(relay_kernel, spans, room),
        out_shape=jax.ShapeDtypeStruct((toks, heads, dh), bf16),
        in_specs=[vmem, vmem, pl.BlockSpec(memory_space=pltpu.SMEM), hbm, hbm],
        out_specs=hbm,
        scratch_shapes=[
            pltpu.VMEM((toks, heads, dh), bf16),
            pltpu.VMEM((own, BLK, heads, dh), bf16),
            pltpu.VMEM((own, heads, BLK, dh), bf16),
            pltpu.VMEM((2, own, heads, BLK, dh), bf16),
            pltpu.VMEM((2, rims, heads, BLK, dh), bf16),
            pltpu.VMEM((2, room, heads, BLK, dh), bf16),
            pltpu.VMEM((room, heads, BLK, dh), bf16),
            pltpu.VMEM((heads, toks, dh), bf16),
            pltpu.VMEM((heads, toks, dh + LANES), f32),
            pltpu.VMEM((heads, toks, LANES), f32),
            pltpu.VMEM((2 * CAP + room + 1, own, 1, BLK), f32),
            pltpu.VMEM((2, BLK * heads, dh), f32),
            pltpu.VMEM((own, BLK * heads, dh), f32),
            pltpu.VMEM((toks, heads, dh), bf16),
            dma((2,)), dma((2,)),
            dma((rims,)), dma((rims,)), dma((rims,)), dma((rims,)),
            dma((ways,)), dma((ways,)), dma((ways,)), dma((ways,)),
            dma((own,)),
        ],
        compiler_params=pltpu.CompilerParams(
            collective_id=room, has_side_effects=True, vmem_limit_bytes=60 << 20),
    )(lists, counts, table, queries, keys_values)


def local(spans, groups, queries, keys_values, far_list, far_count):
    toks, heads, members, dh = queries.shape
    own = toks // BLK
    if spans != CHAIN or groups != 2 or own < WB:
        return direct(spans, queries, keys_values, far_list, far_count)
    hbm = pl.BlockSpec(memory_space=pl.ANY)
    vmem = pl.BlockSpec(memory_space=pltpu.VMEM)
    smem = pl.BlockSpec(memory_space=pltpu.SMEM)
    dma = pltpu.SemaphoreType.DMA
    lists, counts = far_list.T, far_count.reshape(1, -1)
    table, choice = pl.pallas_call(
        functools.partial(prelude, spans, own),
        out_shape=[jax.ShapeDtypeStruct((CAP * len(pair_names(spans)),), jnp.int32), jax.ShapeDtypeStruct((1,), jnp.int32)],
        in_specs=[vmem, vmem],
        out_specs=[smem, smem],
        scratch_shapes=[pltpu.VMEM((8, LANES), jnp.int32), pltpu.VMEM((8, LANES), jnp.int32), dma((2,))],
        compiler_params=pltpu.CompilerParams(collective_id=1, has_side_effects=True),
    )(lists, counts)
    args = (lists, counts, table, queries.reshape(toks, heads, dh), keys_values.reshape(-1, own, BLK, heads, dh))
    result = lax.switch(choice[0], [functools.partial(chained, spans, room) for room in (6, 7, 8)], *args)
    result = pl.pallas_call(
        settle,
        out_shape=jax.ShapeDtypeStruct(result.shape, result.dtype),
        in_specs=[hbm], out_specs=hbm,
        scratch_shapes=[pltpu.VMEM(result.shape, result.dtype), dma((own,)), dma((own,))],
        compiler_params=pltpu.CompilerParams(vmem_limit_bytes=16 << 20),
    )(result)
    return result.reshape(queries.shape)


def direct_kernel(
    spans, lists_in, counts, q_in, kv_in, out,
    q_raw, raw, mine, loc, rim_raw, rim, far, sendbuf, qh, acc, top, bias, scr, o_raw,
    in_sem, x_send, x_recv, rz_send, rz_recv, rf_send, rf_recv,
    fz_send, fz_recv, ff_send, ff_recv, out_sem,
):
    toks, heads, dh = q_in.shape
    own = toks // BLK
    me = lax.axis_index("ctx")
    side = lax.axis_index("rep")
    mate = {"rep": 1 - side}
    rims = WB - 1

    load_kv = pltpu.make_async_copy(kv_in.at[0], raw, in_sem.at[0])
    load_q = pltpu.make_async_copy(q_in, q_raw, in_sem.at[1])
    load_kv.start()
    load_q.start()

    barrier = pltpu.get_barrier_semaphore()
    pl.semaphore_signal(barrier, inc=1, device_id=mate)

    def greet(i, _):
        pl.semaphore_signal(barrier, inc=1, device_id={"ctx": lax.rem(me + i, spans)})
        return 0

    lax.fori_loop(1, spans, greet, 0)
    pl.semaphore_wait(barrier, spans)

    def raw_copy(to):
        return pltpu.make_async_remote_copy(
            src_ref=kv_in.at[0, own - 1], dst_ref=rim_raw.at[side],
            send_sem=rz_send.at[0], recv_sem=rz_recv.at[0], device_id={"ctx": to},
        )

    def raw_pass():
        return pltpu.make_async_remote_copy(
            src_ref=rim_raw.at[side], dst_ref=rim_raw.at[side],
            send_sem=rf_send.at[0], recv_sem=rf_recv.at[0], device_id=mate,
        )

    def rim_copy(j, to):
        return pltpu.make_async_remote_copy(
            src_ref=mine.at[own - j],
            dst_ref=rim.at[side, j - 1],
            send_sem=rz_send.at[j - 1], recv_sem=rz_recv.at[j - 1],
            device_id={"ctx": to},
        )

    def rim_pass(j):
        return pltpu.make_async_remote_copy(
            src_ref=rim.at[side, j - 1],
            dst_ref=rim.at[side, j - 1],
            send_sem=rf_send.at[j - 1], recv_sem=rf_recv.at[j - 1],
            device_id=mate,
        )

    def far_copy(to):
        return pltpu.make_async_remote_copy(
            src_ref=sendbuf.at[to], dst_ref=far.at[side, me],
            send_sem=fz_send.at[to], recv_sem=fz_recv.at[me],
            device_id={"ctx": to},
        )

    def far_arrival(src):
        return pltpu.make_async_remote_copy(
            src_ref=sendbuf.at[src], dst_ref=far.at[side, src],
            send_sem=fz_send.at[src], recv_sem=fz_recv.at[src],
            device_id={"ctx": src},
        )

    def far_pass(src):
        return pltpu.make_async_remote_copy(
            src_ref=far.at[side, src], dst_ref=far.at[side, src],
            send_sem=ff_send.at[src], recv_sem=ff_recv.at[src],
            device_id=mate,
        )

    ahead = lax.rem(me + 1, spans)
    has_next = me + 1 < spans

    @pl.when(has_next)
    def _():
        raw_copy(ahead).start()

    def spread(part, block, put):
        scr[part] = block.astype(jnp.float32).reshape(BLK * heads, dh)
        for h in range(heads):
            put(h, scr[part, pl.ds(h, BLK, stride=heads), :].astype(jnp.bfloat16))

    load_kv.wait()
    parts = scr.shape[0]

    def spread_mine(i, _):
        for part in range(parts):
            b = i * parts + part

            def put(h, x):
                mine[b, h] = x
                loc[side, b, h] = x

            spread(part, raw[b], put)
        return 0

    lax.fori_loop(0, own // parts, spread_mine, 0)

    swap = pltpu.make_async_remote_copy(
        src_ref=mine, dst_ref=loc.at[side],
        send_sem=x_send, recv_sem=x_recv, device_id=mate,
    )
    swap.start()

    big = jnp.int32(1 << 30)
    slot = lax.broadcasted_iota(jnp.int32, lists_in.shape, 0)
    block_of = lax.broadcasted_iota(jnp.int32, lists_in.shape, 1)
    listed = jnp.where(slot < counts[...], lists_in[...], -1)

    def slots(dst, src):
        inside = ((listed >= src * own) & (listed < src * own + own)
                  & (block_of >= dst * own) & (block_of < dst * own + own))
        first = jnp.min(jnp.where(inside, listed, big))
        second = jnp.min(jnp.where(inside & (listed > first), listed, big))
        return first, second

    def local_row(block):
        row = jnp.where(block < big, block - me * own, 0)
        return jnp.clip(row, 0, own - 1)

    def fill(i, _):
        to = spans - 1 - i
        found = slots(to, me)
        for k in range(CAP):
            sendbuf[to, k] = mine[local_row(found[k])]
        return 0

    later = spans - 1 - me
    lax.fori_loop(0, later, fill, 0)

    def push(i, _):
        far_copy(spans - 1 - i).start()
        return 0

    lax.fori_loop(0, later, push, 0)

    @pl.when(has_next)
    def _():
        for j in range(2, WB):
            rim_copy(j, ahead).start()

    ones = jnp.ones((BLK, LANES), jnp.bfloat16)

    def fill_bias(src, _):
        found = slots(me, src)
        for k in range(CAP):
            hit = jnp.max(jnp.where(listed == found[k], 1.0, 0.0), axis=0, keepdims=True)
            for c in range(own):
                mark = jnp.where(block_of[:1] == me * own + c, hit, 0.0)
                mark = jnp.max(mark, axis=1, keepdims=True)
                bias[src, c, :, k * BLK:(k + 1) * BLK] = jnp.broadcast_to(
                    jnp.where(mark > 0.5, 0.0, MASKED), (1, BLK))
        return 0

    lax.fori_loop(0, me + 1, fill_bias, 0)

    load_q.wait()

    def spread_q(i, _):
        for part in range(parts):
            at = pl.ds(pl.multiple_of((i * parts + part) * BLK, BLK), BLK)

            def put(h, x):
                qh[h, at, :] = x

            spread(part, q_raw[at], put)
        return 0

    lax.fori_loop(0, own // parts, spread_q, 0)
    swap.wait_recv()

    wide = min(WB, own)
    span = wide * BLK

    def near(c, _):
        rows = pl.ds(pl.multiple_of(c * BLK, BLK), BLK)
        low = jnp.maximum(c - (WB - 1), 0)
        keys = pl.ds(low, wide)
        key_pos = low * BLK + lax.broadcasted_iota(jnp.int32, (BLK, span), 1)
        query_pos = c * BLK + lax.broadcasted_iota(jnp.int32, (BLK, span), 0)
        seen = key_pos <= query_pos
        for h in range(heads):
            s = lax.dot_general(qh[h, rows, :], loc[0, keys, h].reshape(span, dh), NT,
                                preferred_element_type=jnp.float32) * SCALE
            s = jnp.where(seen, s, MASKED)
            m = jnp.max(s, axis=1, keepdims=True)
            p = jnp.exp2(s - m).astype(jnp.bfloat16)
            v = jnp.concatenate([loc[1, keys, h].reshape(span, dh)] + [jnp.ones((span, LANES), jnp.bfloat16)], axis=1)
            acc[h, rows, :] = jnp.dot(p, v, preferred_element_type=jnp.float32)
            top[h, rows, :] = jnp.broadcast_to(m, (BLK, LANES))
        return 0

    lax.fori_loop(0, own, near, 0)

    def merge(h, rows, k, v, row_bias):
        s = lax.dot_general(qh[h, rows, :], k, NT, preferred_element_type=jnp.float32) * SCALE
        s = s + row_bias
        old = top[h, rows, :]
        m = jnp.maximum(old, jnp.max(s, axis=1, keepdims=True))
        spread_m = jnp.concatenate([m] * (s.shape[1] // LANES), axis=1)
        p = jnp.exp2(s - spread_m).astype(jnp.bfloat16)
        a = jnp.exp2(old - m)
        acc[h, rows, :] = acc[h, rows, :] * jnp.concatenate([a, a], axis=1) + jnp.dot(
            p, v, preferred_element_type=jnp.float32)
        top[h, rows, :] = m

    def stack(get, h):
        k = jnp.concatenate([get(0, n, h) for n in range(CAP)], axis=0)
        v = jnp.concatenate(
            [jnp.concatenate([get(1, n, h), ones], axis=1) for n in range(CAP)], axis=0)
        return k, v

    def far_all(src, get):
        def one(c, _):
            rows = pl.ds(pl.multiple_of(c * BLK, BLK), BLK)
            row_bias = bias[src, c]
            for h in range(heads):
                merge(h, rows, *stack(get, h), row_bias)
            return 0

        lax.fori_loop(0, own, one, 0)

    found_mine = slots(me, me)
    at_mine = [local_row(b) for b in found_mine]
    far_all(me, lambda kind, k, h: loc[kind, at_mine[k], h])

    @pl.when(me > 0)
    def _():
        raw_copy(ahead).wait_recv()
        raw_pass().start()
        raw_pass().wait_recv()

        def put_k(h, x):
            rim[0, 0, h] = x

        def put_v(h, x):
            rim[1, 0, h] = x

        spread(0, rim_raw[0], put_k)
        spread(1, rim_raw[1], put_v)

    def far_step(src, _):
        far_arrival(src).wait_recv()
        far_pass(src).start()
        far_pass(src).wait_recv()
        far_all(src, lambda kind, k, h: far[kind, src, k, h])
        return 0

    lax.fori_loop(0, me, far_step, 0)

    def finish(c, _):
        rows = pl.ds(pl.multiple_of(c * BLK, BLK), BLK)
        part = lax.rem(c, parts)
        for h in range(heads):
            scr[part, pl.ds(h, BLK, stride=heads), :] = acc[h, rows, :dh] / acc[h, rows, dh:]
        o_raw[rows] = scr[part].reshape(BLK, heads, dh).astype(jnp.bfloat16)
        pltpu.make_async_copy(o_raw.at[rows], out.at[rows], out_sem.at[c]).start()
        return 0

    lane = lax.broadcasted_iota(jnp.int32, (1, CAP * BLK), 1)
    once = jnp.where(lane < BLK, 0.0, MASKED)

    def close(i, _):
        last = own - 1 - i
        j = WB - 1 - last

        @pl.when((me > 0) & (j > 1))
        def _():
            rim_copy(j, ahead).wait_recv()
            rim_pass(j).start()
            rim_pass(j).wait_recv()

        def one(c, _):
            rows = pl.ds(pl.multiple_of(c * BLK, BLK), BLK)
            for h in range(heads):
                merge(h, rows, *stack(lambda kind, n, h: rim[kind, j - 1, h], h), once)
            return 0

        @pl.when((me > 0) & (j > 0))
        def _():
            lax.fori_loop(0, last + 1, one, 0)

        return finish(last, 0)

    lax.fori_loop(0, own, close, 0)

    def drain(c, _):
        rows = pl.ds(pl.multiple_of(c * BLK, BLK), BLK)
        pltpu.make_async_copy(o_raw.at[rows], out.at[rows], out_sem.at[c]).wait()
        return 0

    lax.fori_loop(0, own, drain, 0)
    swap.wait_send()

    @pl.when(has_next)
    def _():
        raw_copy(ahead).wait_send()
        for j in range(2, WB):
            rim_copy(j, ahead).wait_send()

    @pl.when(me > 0)
    def _():
        raw_pass().wait_send()
        for j in range(2, WB):
            rim_pass(j).wait_send()

    def sent(i, _):
        far_copy(spans - 1 - i).wait_send()
        return 0

    lax.fori_loop(0, later, sent, 0)

    def passed(src, _):
        far_pass(src).wait_send()
        return 0

    lax.fori_loop(0, me, passed, 0)


def direct(spans, queries, keys_values, far_list, far_count):
    toks, heads, members, dh = queries.shape
    own = toks // BLK
    rims = WB - 1
    bf16, f32 = jnp.bfloat16, jnp.float32
    hbm = pl.BlockSpec(memory_space=pl.ANY)
    dma = pltpu.SemaphoreType.DMA
    result = pl.pallas_call(
        functools.partial(direct_kernel, spans),
        out_shape=jax.ShapeDtypeStruct((toks, heads, dh), bf16),
        in_specs=[pl.BlockSpec(memory_space=pltpu.VMEM)] * 2 + [hbm, hbm],
        out_specs=hbm,
        scratch_shapes=[
            pltpu.VMEM((toks, heads, dh), bf16),
            pltpu.VMEM((own, BLK, heads, dh), bf16),
            pltpu.VMEM((own, heads, BLK, dh), bf16),
            pltpu.VMEM((2, own, heads, BLK, dh), bf16),
            pltpu.VMEM((2, BLK, heads, dh), bf16),
            pltpu.VMEM((2, rims, heads, BLK, dh), bf16),
            pltpu.VMEM((2, spans, CAP, heads, BLK, dh), bf16),
            pltpu.VMEM((spans, CAP, heads, BLK, dh), bf16),
            pltpu.VMEM((heads, toks, dh), bf16),
            pltpu.VMEM((heads, toks, dh + LANES), f32),
            pltpu.VMEM((heads, toks, LANES), f32),
            pltpu.VMEM((spans, own, 1, CAP * BLK), f32),
            pltpu.VMEM((2, BLK * heads, dh), f32),
            pltpu.VMEM((toks, heads, dh), bf16),
            dma((2,)), dma, dma,
            dma((rims,)), dma((rims,)), dma((rims,)), dma((rims,)),
            dma((spans,)), dma((spans,)), dma((spans,)), dma((spans,)),
            dma((own,)),
        ],
        compiler_params=pltpu.CompilerParams(
            collective_id=0, has_side_effects=True, vmem_limit_bytes=62 << 20),
    )(far_list.T, far_count.reshape(1, -1), queries.reshape(toks, heads, dh), keys_values.reshape(-1, own, BLK, heads, dh))
    return result.reshape(queries.shape)


def solution(mesh):
    in_specs = (
        P(("groups", "ctx"), "head", "rep", None),
        P("rep", ("groups", "ctx"), "head", None),
        P("groups", None),
        P("groups"),
    )
    out_specs = P(("groups", "ctx"), "head", "rep", None)
    return jax.shard_map(
        functools.partial(local, mesh.shape["ctx"], mesh.shape["groups"]),
        mesh=mesh, in_specs=in_specs, out_specs=out_specs, check_vma=False)
```

```python
import functools
import math

import jax
import jax.numpy as jnp
from jax import lax
from jax.experimental import pallas as pl
from jax.experimental.pallas import tpu as pltpu
from jax.sharding import PartitionSpec as P

BLK = 128
WB = 4
FSEL = 16
CAP = 2

LANES = 128
MASKED = -1e30
SCALE = math.log2(math.e) / 12.0
NT = (((1,), (1,)), ((), ()))


CHAIN = 4
BIG = 1 << 30


def pair_names(spans):
    return [(dst, src) for dst in range(spans) for src in range(dst + 1)]


def where_of(spans, dst, src, k):
    return CAP * pair_names(spans).index((dst, src)) + k


def middle_plan(read, own):
    edge = 2 * own - (WB - 1)
    fresh, rank, blocks = [], [], []
    count = jnp.int32(0)
    for dst in (3, 2):
        for k in range(CAP):
            b = read(dst, 1, k)
            new = (b < BIG) & (b < edge)
            for other in blocks:
                new &= b != other
            fresh.append(new)
            rank.append(count)
            blocks.append(b)
            count = count + jnp.where(new, 1, 0)
    mine = []
    for a in range(2 * CAP):
        b = jnp.int32(BIG)
        for new, r, block in zip(fresh, rank, blocks):
            b = jnp.where(new & (r == a), block, b)
        mine.append(b)
    first = [read(3, 0, k) for k in range(CAP)]
    extra = []
    for k in range(CAP):
        b = read(2, 0, k)
        new = b < BIG
        for other in first:
            new &= b != other
        extra.append(jnp.where(new, b, BIG))
    need = CAP + count + sum(jnp.where(b < BIG, 1, 0) for b in extra)
    return mine, count, first, extra, need


def prelude(
    spans, own, lists_in, counts, kv_in, table, choice, close_by, ready,
    raw, scr, turned, share, theirs, sem, own_sem,
):
    rims, _, heads, dh = raw.shape
    me = lax.axis_index("ctx")
    peer = {"groups": 1 - lax.axis_index("groups")}
    has_next = me + 1 < spans
    load = pltpu.make_async_copy(kv_in.at[0, pl.ds(own - rims, rims)], raw, own_sem.at[0])
    load.start()
    barrier = pltpu.get_barrier_semaphore()
    pl.semaphore_signal(barrier, inc=1, device_id=peer)

    @pl.when(me > 0)
    def _():
        pl.semaphore_signal(barrier, inc=1, device_id={"ctx": lax.rem(me + spans - 1, spans)})

    load.wait()

    def turn(r):
        scr[r] = raw[r].astype(jnp.float32).reshape(BLK * heads, dh)
        for h in range(heads):
            turned[r, h] = scr[r, pl.ds(h, BLK, stride=heads), :].astype(jnp.bfloat16)

    turn(rims - 1)
    pl.semaphore_wait(barrier, jnp.where(has_next, 2, 1))
    send = pltpu.make_async_remote_copy(
        src_ref=turned.at[rims - 1], dst_ref=close_by, send_sem=sem.at[2], recv_sem=sem.at[3],
        device_id={"ctx": lax.rem(me + 1, spans)})

    @pl.when(has_next)
    def _():
        send.start()

    slot = lax.broadcasted_iota(jnp.int32, lists_in.shape, 0)
    block_of = lax.broadcasted_iota(jnp.int32, lists_in.shape, 1)
    listed = jnp.where(slot < counts[...], lists_in[...], -1)
    found = {}
    for dst, src in pair_names(spans):
        inside = ((listed >= src * own) & (listed < src * own + own)
                  & (block_of >= dst * own) & (block_of < dst * own + own))
        first = jnp.min(jnp.where(inside, listed, BIG))
        second = jnp.min(jnp.where(inside & (listed > first), listed, BIG))
        for k, b in enumerate((first, second)):
            found[dst, src, k] = b
            table[where_of(spans, dst, src, k)] = b
    need = middle_plan(lambda dst, src, k: found[dst, src, k], own)[-1]
    share[...] = jnp.broadcast_to(need, share.shape)
    swap = pltpu.make_async_remote_copy(
        src_ref=share, dst_ref=theirs, send_sem=sem.at[0], recv_sem=sem.at[1], device_id=peer)
    swap.start()
    for r in range(rims - 1):
        turn(r)
    keep = pltpu.make_async_copy(turned.at[pl.ds(0, rims - 1)], ready, own_sem.at[1])
    keep.start()
    swap.wait()
    most = jnp.max(jnp.maximum(share[...], theirs[...]))
    choice[0] = jnp.clip(most - 3 * CAP, 0, CAP)
    keep.wait()

    @pl.when(me > 0)
    def _():
        send.wait_recv()

    @pl.when(has_next)
    def _():
        send.wait_send()


def relay_kernel(
    spans, room, lists_in, counts, table, close_by, ready, q_in, kv_in, out,
    q_raw, raw, mine, loc, rim, relay, sendbuf, qh, acc, top, bias, scr, done, o_raw,
    in_sem, x_sem, rz_send, rz_recv, rf_send, rf_recv,
    z_send, z_recv, f_send, f_recv, out_sem,
):
    toks, heads, dh = q_in.shape
    own = toks // BLK
    me = lax.axis_index("ctx")
    side = lax.axis_index("rep")
    mate = {"rep": 1 - side}
    rims = WB - 1
    pieces = f_send.shape[0] - room + 1
    part_heads = heads // pieces
    has_next = me + 1 < spans
    ahead = {"ctx": lax.rem(me + 1, spans)}
    late, last = room - 2, room - 1

    load_kv = pltpu.make_async_copy(kv_in.at[0], raw, in_sem.at[0])
    load_q = pltpu.make_async_copy(q_in, q_raw, in_sem.at[1])
    load_rim = pltpu.make_async_copy(close_by, rim.at[side, rims - 1], in_sem.at[2])
    barrier = pltpu.get_barrier_semaphore()
    pl.semaphore_signal(barrier, inc=1, device_id=mate)

    @pl.when(me > 0)
    def _():
        pl.semaphore_signal(barrier, inc=1, device_id={"ctx": lax.rem(me + spans - 1, spans)})

    def rim_copy(j):
        return pltpu.make_async_remote_copy(
            src_ref=ready.at[rims - j], dst_ref=rim.at[side, rims - j],
            send_sem=rz_send.at[j - 1], recv_sem=rz_recv.at[j - 1], device_id=ahead)

    def rim_pass(j):
        return pltpu.make_async_remote_copy(
            src_ref=rim.at[side, rims - j], dst_ref=rim.at[side, rims - j],
            send_sem=rf_send.at[j - 1], recv_sem=rf_recv.at[j - 1], device_id=mate)

    def cut(ref, piece):
        return ref if piece is None else ref.at[pl.ds(piece * part_heads, part_heads)]

    def put(src, p, piece=None):
        at = p if piece is None else p + piece
        return pltpu.make_async_remote_copy(
            src_ref=cut(src, piece), dst_ref=cut(relay.at[side, p], piece),
            send_sem=z_send.at[at], recv_sem=z_recv.at[at], device_id=ahead)

    def came(p, piece=None):
        put(relay.at[side, p], p, piece).wait_recv()

    def hand(p, piece=None):
        at = p if piece is None else p + piece
        return pltpu.make_async_remote_copy(
            src_ref=cut(relay.at[side, p], piece), dst_ref=cut(relay.at[side, p], piece),
            send_sem=f_send.at[at], recv_sem=f_recv.at[at], device_id=mate)

    def put_last(src):
        for piece in range(pieces):
            put(src, last, piece).start()

    parts = scr.shape[0]

    def spread(part, block, store):
        scr[part] = block.astype(jnp.float32).reshape(BLK * heads, dh)
        for h in range(heads):
            store(h, scr[part, pl.ds(h, BLK, stride=heads), :].astype(jnp.bfloat16))

    def spread_mine(b, part):
        def store(h, x):
            mine[b, h] = x
            loc[side, b, h] = x

        spread(part, raw[b], store)

    pl.semaphore_wait(barrier, jnp.where(has_next, 2, 1))

    @pl.when(has_next)
    def _():
        for j in range(2, WB):
            rim_copy(j).start()

    load_kv.start()

    @pl.when(me > 0)
    def _():
        load_rim.start()

    load_q.start()
    load_kv.wait()

    def spread_all(b, _):
        spread_mine(b, lax.rem(b, parts))
        return 0

    lax.fori_loop(0, own, spread_all, 0)

    swap = pltpu.make_async_remote_copy(
        src_ref=mine, dst_ref=loc.at[side],
        send_sem=x_sem.at[0], recv_sem=x_sem.at[1], device_id=mate)
    swap.start()

    def read(dst, src, k):
        return table[where_of(spans, dst, src, k)]

    def local_row(block):
        return jnp.clip(jnp.where(block < BIG, block - me * own, 0), 0, own - 1)

    def fill(p, block):
        sendbuf[p] = mine[local_row(block)]

    own_list, own_count, first, extra, _ = middle_plan(read, own)
    own_late, own_last = late - 2, last - 2

    @pl.when(me == 0)
    def _():
        for p, (dst, k) in zip((0, 1, 2, 3, late, last), ((3, 0), (3, 1), (2, 0), (2, 1), (1, 0), (1, 1))):
            fill(p, read(dst, 0, k))
        for p in (0, 1, 2, 3, late):
            put(sendbuf.at[p], p).start()
        put_last(sendbuf.at[last])

    early = [0, 1] + list(range(4, late))

    @pl.when(me == 1)
    def _():
        for p in early:
            fill(p, own_list[p if p < 2 else p - 2])
        for p in early:
            put(sendbuf.at[p], p).start()

    @pl.when(me == 2)
    def _():
        for k in range(CAP):
            fill(k, read(3, 2, k))
        for k in range(CAP):
            put(sendbuf.at[k], k).start()

    @pl.when(me == 0)
    def _():
        for j in range(rims):
            rim[:, j] = jnp.zeros((2,) + rim.shape[2:], rim.dtype)

    held = [0] * room
    for k in range(CAP):
        held[k] = jnp.where(me == 3, read(3, 2, k), own_list[k])
        held[2 + k] = jnp.where(me == 3, read(3, 1, k), first[k])
    for p in range(4, late):
        held[p] = jnp.where(me == 2, own_list[p - 2], BIG)
    both = (extra[0] < BIG) & (extra[1] < BIG)
    mid_late = jnp.where(both, extra[0], BIG)
    mid_last = jnp.where(extra[1] < BIG, extra[1], extra[0])
    if own_late < 2 * CAP:
        mid_late = jnp.where(own_count > own_late, own_list[own_late], mid_late)
    if own_last < 2 * CAP:
        mid_last = jnp.where(own_count > own_last, own_list[own_last], mid_last)
    held[late] = jnp.where(me == 3, read(3, 0, 0), jnp.where(me == 2, mid_late, read(1, 0, 0)))
    held[last] = jnp.where(me == 3, read(3, 0, 1), jnp.where(me == 2, mid_last, read(1, 0, 1)))
    edge = 2 * own - rims
    seen_again = []
    for k in range(CAP):
        b = read(2, 1, k)
        seen_again.append(jnp.where((b < BIG) & (b >= edge) & (me == 2), b, BIG))
    mine_far = []
    for k in range(CAP):
        b = read(0, 0, k)
        for s in range(1, spans):
            b = jnp.where(me == s, read(s, s, k), b)
        mine_far.append(b)

    slot = lax.broadcasted_iota(jnp.int32, lists_in.shape, 0)
    block_of = lax.broadcasted_iota(jnp.int32, lists_in.shape, 1)
    listed = jnp.where(slot < counts[...], lists_in[...], -1)

    for n, block in enumerate(mine_far + seen_again + held + [jnp.int32(BIG)]):
        hit = jnp.max(jnp.where(listed == block, 1.0, 0.0), axis=0, keepdims=True)
        for c in range(own):
            mark = jnp.where(block_of[:1] == me * own + c, hit, 0.0)
            mark = jnp.max(mark, axis=1, keepdims=True)
            bias[n, c] = jnp.broadcast_to(jnp.where(mark > 0.5, 0.0, MASKED), (1, BLK))

    load_q.wait()

    def spread_q(c, _):
        at = pl.ds(pl.multiple_of(c * BLK, BLK), BLK)

        def store(h, x):
            qh[h, at, :] = x

        spread(lax.rem(c, parts), q_raw[at], store)
        return 0

    lax.fori_loop(0, own, spread_q, 0)
    swap.wait_recv()

    span = WB * BLK

    def near_block(c, rows, get):
        key_pos = lax.broadcasted_iota(jnp.int32, (BLK, span), 1) - rims * BLK
        query_pos = lax.broadcasted_iota(jnp.int32, (BLK, span), 0)
        seen = key_pos <= query_pos
        if isinstance(c, int):
            seen &= (key_pos + c * BLK >= 0) | (me > 0)
        for h in range(heads):
            s = lax.dot_general(qh[h, rows, :], get(0, h), NT,
                                preferred_element_type=jnp.float32) * SCALE
            s = jnp.where(seen, s, MASKED)
            m = jnp.max(s, axis=1, keepdims=True)
            p = jnp.exp2(s - m).astype(jnp.bfloat16)
            v = jnp.concatenate([get(1, h), jnp.ones((span, LANES), jnp.bfloat16)], axis=1)
            acc[h, rows, :] = jnp.dot(p, v, preferred_element_type=jnp.float32)
            top[h, rows, :] = jnp.broadcast_to(m, (BLK, LANES))

    def near(c, _):
        keys = pl.ds(c - rims, WB)
        near_block(c, pl.ds(pl.multiple_of(c * BLK, BLK), BLK), lambda kind, h: loc[kind, keys, h].reshape(span, dh))
        return 0

    lax.fori_loop(rims, own, near, 0)

    ones = jnp.ones((BLK, LANES), jnp.bfloat16)

    tall = 2 * BLK

    def merged(h, rows, k, v, row_bias):
        s = lax.dot_general(qh[h, rows, :], k, NT, preferred_element_type=jnp.float32) * SCALE
        s = s + row_bias
        old = top[h, rows, :]
        m = jnp.maximum(old, jnp.max(s, axis=1, keepdims=True))
        spread_m = jnp.concatenate([m] * (s.shape[1] // LANES), axis=1)
        p = jnp.exp2(s - spread_m).astype(jnp.bfloat16)
        a = jnp.exp2(old - m)
        return m, acc[h, rows, :] * jnp.concatenate([a, a], axis=1) + jnp.dot(
            p, v, preferred_element_type=jnp.float32)

    def far_head(h, at, gets, keep, begin=0):
        k = jnp.concatenate([get(0, h) for get in gets], axis=0)
        v = jnp.concatenate([jnp.concatenate([get(1, h), ones], axis=1) for get in gets], axis=0)
        for low in range(begin, toks, tall):
            row_bias = jnp.concatenate([
                jnp.concatenate([jnp.broadcast_to(bias[n, low // BLK + i], (BLK, BLK)) for n in at], axis=1)
                for i in range(tall // BLK)], axis=0)
            rows = pl.ds(low, tall)
            keep(h, low, *merged(h, rows, k, v, row_bias))

    def far(at, gets, begin=0):
        def hold(h, low, m, total):
            acc[h, pl.ds(low, tall), :] = total
            top[h, pl.ds(low, tall), :] = m

        def one(h, _):
            far_head(h, at, gets, hold, begin)
            return 0

        lax.fori_loop(0, heads, one, 0)

    def relayed(p):
        return lambda kind, h: relay[kind, p, h]

    def owned(row):
        return lambda kind, h: loc[kind, row, h]

    def window(row):
        return lambda kind, h: rim[kind, row, h]

    far((0, 1), [owned(local_row(b)) for b in mine_far], WB * BLK // tall * tall)

    @pl.when(me > 0)
    def _():
        load_rim.wait()
        rim_pass(1).start()
        for j in range(2, WB):
            rim_copy(j).wait_recv()
            rim_pass(j).start()
        for j in range(1, WB):
            rim_pass(j).wait_recv()

    for c in range(rims):
        near_block(c, pl.ds(c * BLK, BLK), lambda kind, h: jnp.concatenate(
            [rim[kind, r, h] for r in range(c, rims)] + [loc[kind, b, h] for b in range(c + 1)], axis=0))

    base = 2 * CAP

    @pl.when(me == 1)
    def _():
        for k in range(CAP):
            came(k)
            put(relay.at[side, k], 2 + k).start()
        came(2)
        if own_late < 2 * CAP:
            sendbuf[late] = jnp.where(own_count > own_late, mine[local_row(own_list[own_late])], relay[side, 2])
            put(sendbuf.at[late], late).start()
        else:
            put(relay.at[side, 2], late).start()
        came(3)
        tail = jnp.where(extra[1] < BIG, relay[side, 3], relay[side, 2])
        if own_last < 2 * CAP:
            tail = jnp.where(own_count > own_last, mine[local_row(own_list[own_last])], tail)
        sendbuf[last] = tail
        put_last(sendbuf.at[last])

    @pl.when(me == 2)
    def _():
        far((2, 3), [window(jnp.clip(jnp.where(b < BIG, b - edge, 0), 0, rims - 1)) for b in seen_again])
        for k in range(CAP):
            came(k)
            hand(k).start()
            b = read(3, 1, k)
            pick = relay[side, 0]
            if k == 1:
                pick = jnp.where(b == own_list[1], relay[side, 1], pick)
            for j in range(1, WB):
                pick = jnp.where(b == 2 * own - j, rim[side, rims - j], pick)
            sendbuf[2 + k] = pick
            put(sendbuf.at[2 + k], 2 + k).start()

    @pl.when(me == 3)
    def _():
        for k in range(CAP):
            came(k)
            hand(k).start()

    @pl.when(me > 1)
    def _():
        for k in range(CAP):
            hand(k).wait_recv()
        far((base, base + 1), [relayed(0), relayed(1)])

    if late > 4:
        @pl.when(me == 2)
        def _():
            for p in range(4, late):
                came(p)
                hand(p).start()
            for p in range(4, late):
                hand(p).wait_recv()
            at = [base + p for p in range(4, late)]
            far((at + [base + room])[:2], [relayed(p) for p in (4, late - 1)])

    @pl.when(me == 2)
    def _():
        came(2)
        put(relay.at[side, 2], late).start()
        hand(2).start()
        came(3)
        put_last(relay.at[side, 3])
        hand(3).start()

    @pl.when(me == 3)
    def _():
        for p in (2, 3):
            came(p)
            hand(p).start()

    @pl.when(me > 1)
    def _():
        for p in (2, 3):
            hand(p).wait_recv()
        far((base + 2, base + 3), [relayed(2), relayed(3)])

    def finish(h, low, m, total):
        for i in range(tall // BLK):
            part = total[i * BLK:(i + 1) * BLK]
            done[low // BLK + i, pl.ds(h, BLK, stride=heads), :] = part[:, :dh] / part[:, dh:]

    @pl.when(me > 0)
    def _():
        came(late)
        hand(late).start()
        came(last, 0)
        hand(last, 0).start()
        hand(late).wait_recv()

        def one(piece, _):
            @pl.when(piece + 1 < pieces)
            def _():
                came(last, piece + 1)
                hand(last, piece + 1).start()

            hand(last, piece).wait_recv()
            far_head(piece, (base + late, base + last), [relayed(late), relayed(last)], finish)
            return 0

        lax.fori_loop(0, pieces, one, 0)

    @pl.when(me == 0)
    def _():
        def one(h, _):
            for low in range(0, toks, tall):
                finish(h, low, None, acc[h, pl.ds(low, tall), :])
            return 0

        lax.fori_loop(0, heads, one, 0)

    def write(c):
        rows = pl.ds(pl.multiple_of(c * BLK, BLK), BLK)
        return pltpu.make_async_copy(o_raw.at[rows], out.at[rows], out_sem.at[c])

    def pack(c, _):
        rows = pl.ds(pl.multiple_of(c * BLK, BLK), BLK)
        o_raw[rows] = done[c].reshape(BLK, heads, dh).astype(jnp.bfloat16)
        write(c).start()
        return 0

    lax.fori_loop(0, own, pack, 0)

    def drain(c, _):
        write(c).wait()
        return 0

    lax.fori_loop(0, own, drain, 0)
    swap.wait_send()

    @pl.when(has_next)
    def _():
        for j in range(2, WB):
            rim_copy(j).wait_send()
        for p in (0, 1, 2, 3, late):
            put(relay.at[side, p], p).wait_send()
        for piece in range(pieces):
            put(relay.at[side, last], last, piece).wait_send()

    @pl.when(me == 1)
    def _():
        for p in range(4, late):
            put(relay.at[side, p], p).wait_send()

    @pl.when(me > 0)
    def _():
        for j in range(1, WB):
            rim_pass(j).wait_send()
        hand(late).wait_send()
        for piece in range(pieces):
            hand(last, piece).wait_send()

    @pl.when(me > 1)
    def _():
        for p in range(4):
            hand(p).wait_send()

    @pl.when(me == 2)
    def _():
        for p in range(4, late):
            hand(p).wait_send()


def settle(src, out, buf, read_sem, write_sem):
    toks = src.shape[0]
    step = toks // read_sem.shape[0]

    def fetch(i):
        at = pl.ds(i * step, step)
        return pltpu.make_async_copy(src.at[at], buf.at[at], read_sem.at[i])

    def store(i):
        at = pl.ds(i * step, step)
        return pltpu.make_async_copy(buf.at[at], out.at[at], write_sem.at[i])

    for i in range(read_sem.shape[0]):
        fetch(i).start()
    for i in range(read_sem.shape[0]):
        fetch(i).wait()
        store(i).start()
    for i in range(read_sem.shape[0]):
        store(i).wait()


def chained(spans, room, lists, counts, table, close_by, ready, queries, keys_values):
    toks, heads, dh = queries.shape
    own = toks // BLK
    rims = WB - 1
    bf16, f32 = jnp.bfloat16, jnp.float32
    hbm = pl.BlockSpec(memory_space=pl.ANY)
    vmem = pl.BlockSpec(memory_space=pltpu.VMEM)
    dma = pltpu.SemaphoreType.DMA
    pieces = heads
    ways = room - 1 + pieces
    return pl.pallas_call(
        functools.partial(relay_kernel, spans, room),
        out_shape=jax.ShapeDtypeStruct((toks, heads, dh), bf16),
        in_specs=[vmem, vmem, pl.BlockSpec(memory_space=pltpu.SMEM), hbm, hbm, hbm, hbm],
        out_specs=hbm,
        scratch_shapes=[
            pltpu.VMEM((toks, heads, dh), bf16),
            pltpu.VMEM((own, BLK, heads, dh), bf16),
            pltpu.VMEM((own, heads, BLK, dh), bf16),
            pltpu.VMEM((2, own, heads, BLK, dh), bf16),
            pltpu.VMEM((2, rims, heads, BLK, dh), bf16),
            pltpu.VMEM((2, room, heads, BLK, dh), bf16),
            pltpu.VMEM((room, heads, BLK, dh), bf16),
            pltpu.VMEM((heads, toks, dh), bf16),
            pltpu.VMEM((heads, toks, dh + LANES), f32),
            pltpu.VMEM((heads, toks, LANES), f32),
            pltpu.VMEM((2 * CAP + room + 1, own, 1, BLK), f32),
            pltpu.VMEM((2, BLK * heads, dh), f32),
            pltpu.VMEM((own, BLK * heads, dh), f32),
            pltpu.VMEM((toks, heads, dh), bf16),
            dma((3,)), dma((2,)),
            dma((rims,)), dma((rims,)), dma((rims,)), dma((rims,)),
            dma((ways,)), dma((ways,)), dma((ways,)), dma((ways,)),
            dma((own,)),
        ],
        compiler_params=pltpu.CompilerParams(
            collective_id=room, has_side_effects=True, vmem_limit_bytes=50 << 20),
    )(lists, counts, table, close_by, ready, queries, keys_values)


def local(spans, groups, queries, keys_values, far_list, far_count):
    toks, heads, members, dh = queries.shape
    own = toks // BLK
    if spans != CHAIN or groups != 2 or own < WB:
        return direct(spans, queries, keys_values, far_list, far_count)
    hbm = pl.BlockSpec(memory_space=pl.ANY)
    vmem = pl.BlockSpec(memory_space=pltpu.VMEM)
    smem = pl.BlockSpec(memory_space=pltpu.SMEM)
    dma = pltpu.SemaphoreType.DMA
    lists, counts = far_list.T, far_count.reshape(1, -1)
    rims, bf16 = WB - 1, jnp.bfloat16
    keys_values = keys_values.reshape(-1, own, BLK, heads, dh)
    table, choice, close_by, ready = pl.pallas_call(
        functools.partial(prelude, spans, own),
        out_shape=[
            jax.ShapeDtypeStruct((CAP * len(pair_names(spans)),), jnp.int32),
            jax.ShapeDtypeStruct((1,), jnp.int32),
            jax.ShapeDtypeStruct((heads, BLK, dh), bf16),
            jax.ShapeDtypeStruct((rims - 1, heads, BLK, dh), bf16),
        ],
        in_specs=[vmem, vmem, hbm],
        out_specs=[smem, smem, hbm, hbm],
        scratch_shapes=[
            pltpu.VMEM((rims, BLK, heads, dh), bf16),
            pltpu.VMEM((rims, BLK * heads, dh), jnp.float32),
            pltpu.VMEM((rims, heads, BLK, dh), bf16),
            pltpu.VMEM((8, LANES), jnp.int32), pltpu.VMEM((8, LANES), jnp.int32),
            dma((4,)), dma((2,)),
        ],
        compiler_params=pltpu.CompilerParams(collective_id=1, has_side_effects=True, vmem_limit_bytes=32 << 20),
    )(lists, counts, keys_values)
    args = (lists, counts, table, close_by, ready, queries.reshape(toks, heads, dh), keys_values)
    result = lax.switch(choice[0], [functools.partial(chained, spans, room) for room in (6, 7, 8)], *args)
    result = pl.pallas_call(
        settle,
        out_shape=jax.ShapeDtypeStruct(result.shape, result.dtype),
        in_specs=[hbm], out_specs=hbm,
        scratch_shapes=[pltpu.VMEM(result.shape, result.dtype), dma((own,)), dma((own,))],
        compiler_params=pltpu.CompilerParams(vmem_limit_bytes=16 << 20),
    )(result)
    return result.reshape(queries.shape)


def direct_kernel(
    spans, lists_in, counts, q_in, kv_in, out,
    q_raw, raw, mine, loc, rim_raw, rim, far, sendbuf, qh, acc, top, bias, scr, o_raw,
    in_sem, x_send, x_recv, rz_send, rz_recv, rf_send, rf_recv,
    fz_send, fz_recv, ff_send, ff_recv, out_sem,
):
    toks, heads, dh = q_in.shape
    own = toks // BLK
    me = lax.axis_index("ctx")
    side = lax.axis_index("rep")
    mate = {"rep": 1 - side}
    rims = WB - 1

    load_kv = pltpu.make_async_copy(kv_in.at[0], raw, in_sem.at[0])
    load_q = pltpu.make_async_copy(q_in, q_raw, in_sem.at[1])
    load_kv.start()
    load_q.start()

    barrier = pltpu.get_barrier_semaphore()
    pl.semaphore_signal(barrier, inc=1, device_id=mate)

    def greet(i, _):
        pl.semaphore_signal(barrier, inc=1, device_id={"ctx": lax.rem(me + i, spans)})
        return 0

    lax.fori_loop(1, spans, greet, 0)
    pl.semaphore_wait(barrier, spans)

    def raw_copy(to):
        return pltpu.make_async_remote_copy(
            src_ref=kv_in.at[0, own - 1], dst_ref=rim_raw.at[side],
            send_sem=rz_send.at[0], recv_sem=rz_recv.at[0], device_id={"ctx": to},
        )

    def raw_pass():
        return pltpu.make_async_remote_copy(
            src_ref=rim_raw.at[side], dst_ref=rim_raw.at[side],
            send_sem=rf_send.at[0], recv_sem=rf_recv.at[0], device_id=mate,
        )

    def rim_copy(j, to):
        return pltpu.make_async_remote_copy(
            src_ref=mine.at[own - j],
            dst_ref=rim.at[side, j - 1],
            send_sem=rz_send.at[j - 1], recv_sem=rz_recv.at[j - 1],
            device_id={"ctx": to},
        )

    def rim_pass(j):
        return pltpu.make_async_remote_copy(
            src_ref=rim.at[side, j - 1],
            dst_ref=rim.at[side, j - 1],
            send_sem=rf_send.at[j - 1], recv_sem=rf_recv.at[j - 1],
            device_id=mate,
        )

    def far_copy(to):
        return pltpu.make_async_remote_copy(
            src_ref=sendbuf.at[to], dst_ref=far.at[side, me],
            send_sem=fz_send.at[to], recv_sem=fz_recv.at[me],
            device_id={"ctx": to},
        )

    def far_arrival(src):
        return pltpu.make_async_remote_copy(
            src_ref=sendbuf.at[src], dst_ref=far.at[side, src],
            send_sem=fz_send.at[src], recv_sem=fz_recv.at[src],
            device_id={"ctx": src},
        )

    def far_pass(src):
        return pltpu.make_async_remote_copy(
            src_ref=far.at[side, src], dst_ref=far.at[side, src],
            send_sem=ff_send.at[src], recv_sem=ff_recv.at[src],
            device_id=mate,
        )

    ahead = lax.rem(me + 1, spans)
    has_next = me + 1 < spans

    @pl.when(has_next)
    def _():
        raw_copy(ahead).start()

    def spread(part, block, put):
        scr[part] = block.astype(jnp.float32).reshape(BLK * heads, dh)
        for h in range(heads):
            put(h, scr[part, pl.ds(h, BLK, stride=heads), :].astype(jnp.bfloat16))

    load_kv.wait()
    parts = scr.shape[0]

    def spread_mine(i, _):
        for part in range(parts):
            b = i * parts + part

            def put(h, x):
                mine[b, h] = x
                loc[side, b, h] = x

            spread(part, raw[b], put)
        return 0

    lax.fori_loop(0, own // parts, spread_mine, 0)

    swap = pltpu.make_async_remote_copy(
        src_ref=mine, dst_ref=loc.at[side],
        send_sem=x_send, recv_sem=x_recv, device_id=mate,
    )
    swap.start()

    big = jnp.int32(1 << 30)
    slot = lax.broadcasted_iota(jnp.int32, lists_in.shape, 0)
    block_of = lax.broadcasted_iota(jnp.int32, lists_in.shape, 1)
    listed = jnp.where(slot < counts[...], lists_in[...], -1)

    def slots(dst, src):
        inside = ((listed >= src * own) & (listed < src * own + own)
                  & (block_of >= dst * own) & (block_of < dst * own + own))
        first = jnp.min(jnp.where(inside, listed, big))
        second = jnp.min(jnp.where(inside & (listed > first), listed, big))
        return first, second

    def local_row(block):
        row = jnp.where(block < big, block - me * own, 0)
        return jnp.clip(row, 0, own - 1)

    def fill(i, _):
        to = spans - 1 - i
        found = slots(to, me)
        for k in range(CAP):
            sendbuf[to, k] = mine[local_row(found[k])]
        return 0

    later = spans - 1 - me
    lax.fori_loop(0, later, fill, 0)

    def push(i, _):
        far_copy(spans - 1 - i).start()
        return 0

    lax.fori_loop(0, later, push, 0)

    @pl.when(has_next)
    def _():
        for j in range(2, WB):
            rim_copy(j, ahead).start()

    ones = jnp.ones((BLK, LANES), jnp.bfloat16)

    def fill_bias(src, _):
        found = slots(me, src)
        for k in range(CAP):
            hit = jnp.max(jnp.where(listed == found[k], 1.0, 0.0), axis=0, keepdims=True)
            for c in range(own):
                mark = jnp.where(block_of[:1] == me * own + c, hit, 0.0)
                mark = jnp.max(mark, axis=1, keepdims=True)
                bias[src, c, :, k * BLK:(k + 1) * BLK] = jnp.broadcast_to(
                    jnp.where(mark > 0.5, 0.0, MASKED), (1, BLK))
        return 0

    lax.fori_loop(0, me + 1, fill_bias, 0)

    load_q.wait()

    def spread_q(i, _):
        for part in range(parts):
            at = pl.ds(pl.multiple_of((i * parts + part) * BLK, BLK), BLK)

            def put(h, x):
                qh[h, at, :] = x

            spread(part, q_raw[at], put)
        return 0

    lax.fori_loop(0, own // parts, spread_q, 0)
    swap.wait_recv()

    wide = min(WB, own)
    span = wide * BLK

    def near(c, _):
        rows = pl.ds(pl.multiple_of(c * BLK, BLK), BLK)
        low = jnp.maximum(c - (WB - 1), 0)
        keys = pl.ds(low, wide)
        key_pos = low * BLK + lax.broadcasted_iota(jnp.int32, (BLK, span), 1)
        query_pos = c * BLK + lax.broadcasted_iota(jnp.int32, (BLK, span), 0)
        seen = key_pos <= query_pos
        for h in range(heads):
            s = lax.dot_general(qh[h, rows, :], loc[0, keys, h].reshape(span, dh), NT,
                                preferred_element_type=jnp.float32) * SCALE
            s = jnp.where(seen, s, MASKED)
            m = jnp.max(s, axis=1, keepdims=True)
            p = jnp.exp2(s - m).astype(jnp.bfloat16)
            v = jnp.concatenate([loc[1, keys, h].reshape(span, dh)] + [jnp.ones((span, LANES), jnp.bfloat16)], axis=1)
            acc[h, rows, :] = jnp.dot(p, v, preferred_element_type=jnp.float32)
            top[h, rows, :] = jnp.broadcast_to(m, (BLK, LANES))
        return 0

    lax.fori_loop(0, own, near, 0)

    def merge(h, rows, k, v, row_bias):
        s = lax.dot_general(qh[h, rows, :], k, NT, preferred_element_type=jnp.float32) * SCALE
        s = s + row_bias
        old = top[h, rows, :]
        m = jnp.maximum(old, jnp.max(s, axis=1, keepdims=True))
        spread_m = jnp.concatenate([m] * (s.shape[1] // LANES), axis=1)
        p = jnp.exp2(s - spread_m).astype(jnp.bfloat16)
        a = jnp.exp2(old - m)
        acc[h, rows, :] = acc[h, rows, :] * jnp.concatenate([a, a], axis=1) + jnp.dot(
            p, v, preferred_element_type=jnp.float32)
        top[h, rows, :] = m

    def stack(get, h):
        k = jnp.concatenate([get(0, n, h) for n in range(CAP)], axis=0)
        v = jnp.concatenate(
            [jnp.concatenate([get(1, n, h), ones], axis=1) for n in range(CAP)], axis=0)
        return k, v

    def far_all(src, get):
        def one(c, _):
            rows = pl.ds(pl.multiple_of(c * BLK, BLK), BLK)
            row_bias = bias[src, c]
            for h in range(heads):
                merge(h, rows, *stack(get, h), row_bias)
            return 0

        lax.fori_loop(0, own, one, 0)

    found_mine = slots(me, me)
    at_mine = [local_row(b) for b in found_mine]
    far_all(me, lambda kind, k, h: loc[kind, at_mine[k], h])

    @pl.when(me > 0)
    def _():
        raw_copy(ahead).wait_recv()
        raw_pass().start()
        raw_pass().wait_recv()

        def put_k(h, x):
            rim[0, 0, h] = x

        def put_v(h, x):
            rim[1, 0, h] = x

        spread(0, rim_raw[0], put_k)
        spread(1, rim_raw[1], put_v)

    def far_step(src, _):
        far_arrival(src).wait_recv()
        far_pass(src).start()
        far_pass(src).wait_recv()
        far_all(src, lambda kind, k, h: far[kind, src, k, h])
        return 0

    lax.fori_loop(0, me, far_step, 0)

    def finish(c, _):
        rows = pl.ds(pl.multiple_of(c * BLK, BLK), BLK)
        part = lax.rem(c, parts)
        for h in range(heads):
            scr[part, pl.ds(h, BLK, stride=heads), :] = acc[h, rows, :dh] / acc[h, rows, dh:]
        o_raw[rows] = scr[part].reshape(BLK, heads, dh).astype(jnp.bfloat16)
        pltpu.make_async_copy(o_raw.at[rows], out.at[rows], out_sem.at[c]).start()
        return 0

    lane = lax.broadcasted_iota(jnp.int32, (1, CAP * BLK), 1)
    once = jnp.where(lane < BLK, 0.0, MASKED)

    def close(i, _):
        last = own - 1 - i
        j = WB - 1 - last

        @pl.when((me > 0) & (j > 1))
        def _():
            rim_copy(j, ahead).wait_recv()
            rim_pass(j).start()
            rim_pass(j).wait_recv()

        def one(c, _):
            rows = pl.ds(pl.multiple_of(c * BLK, BLK), BLK)
            for h in range(heads):
                merge(h, rows, *stack(lambda kind, n, h: rim[kind, j - 1, h], h), once)
            return 0

        @pl.when((me > 0) & (j > 0))
        def _():
            lax.fori_loop(0, last + 1, one, 0)

        return finish(last, 0)

    lax.fori_loop(0, own, close, 0)

    def drain(c, _):
        rows = pl.ds(pl.multiple_of(c * BLK, BLK), BLK)
        pltpu.make_async_copy(o_raw.at[rows], out.at[rows], out_sem.at[c]).wait()
        return 0

    lax.fori_loop(0, own, drain, 0)
    swap.wait_send()

    @pl.when(has_next)
    def _():
        raw_copy(ahead).wait_send()
        for j in range(2, WB):
            rim_copy(j, ahead).wait_send()

    @pl.when(me > 0)
    def _():
        raw_pass().wait_send()
        for j in range(2, WB):
            rim_pass(j).wait_send()

    def sent(i, _):
        far_copy(spans - 1 - i).wait_send()
        return 0

    lax.fori_loop(0, later, sent, 0)

    def passed(src, _):
        far_pass(src).wait_send()
        return 0

    lax.fori_loop(0, me, passed, 0)


def direct(spans, queries, keys_values, far_list, far_count):
    toks, heads, members, dh = queries.shape
    own = toks // BLK
    rims = WB - 1
    bf16, f32 = jnp.bfloat16, jnp.float32
    hbm = pl.BlockSpec(memory_space=pl.ANY)
    dma = pltpu.SemaphoreType.DMA
    result = pl.pallas_call(
        functools.partial(direct_kernel, spans),
        out_shape=jax.ShapeDtypeStruct((toks, heads, dh), bf16),
        in_specs=[pl.BlockSpec(memory_space=pltpu.VMEM)] * 2 + [hbm, hbm],
        out_specs=hbm,
        scratch_shapes=[
            pltpu.VMEM((toks, heads, dh), bf16),
            pltpu.VMEM((own, BLK, heads, dh), bf16),
            pltpu.VMEM((own, heads, BLK, dh), bf16),
            pltpu.VMEM((2, own, heads, BLK, dh), bf16),
            pltpu.VMEM((2, BLK, heads, dh), bf16),
            pltpu.VMEM((2, rims, heads, BLK, dh), bf16),
            pltpu.VMEM((2, spans, CAP, heads, BLK, dh), bf16),
            pltpu.VMEM((spans, CAP, heads, BLK, dh), bf16),
            pltpu.VMEM((heads, toks, dh), bf16),
            pltpu.VMEM((heads, toks, dh + LANES), f32),
            pltpu.VMEM((heads, toks, LANES), f32),
            pltpu.VMEM((spans, own, 1, CAP * BLK), f32),
            pltpu.VMEM((2, BLK * heads, dh), f32),
            pltpu.VMEM((toks, heads, dh), bf16),
            dma((2,)), dma, dma,
            dma((rims,)), dma((rims,)), dma((rims,)), dma((rims,)),
            dma((spans,)), dma((spans,)), dma((spans,)), dma((spans,)),
            dma((own,)),
        ],
        compiler_params=pltpu.CompilerParams(
            collective_id=0, has_side_effects=True, vmem_limit_bytes=62 << 20),
    )(far_list.T, far_count.reshape(1, -1), queries.reshape(toks, heads, dh), keys_values.reshape(-1, own, BLK, heads, dh))
    return result.reshape(queries.shape)


def solution(mesh):
    in_specs = (
        P(("groups", "ctx"), "head", "rep", None),
        P("rep", ("groups", "ctx"), "head", None),
        P("groups", None),
        P("groups"),
    )
    out_specs = P(("groups", "ctx"), "head", "rep", None)
    return jax.shard_map(
        functools.partial(local, mesh.shape["ctx"], mesh.shape["groups"]),
        mesh=mesh, in_specs=in_specs, out_specs=out_specs, check_vma=False)
```

```python
import functools
import math

import jax
import jax.numpy as jnp
from jax import lax
from jax.experimental import pallas as pl
from jax.experimental.pallas import tpu as pltpu
from jax.sharding import PartitionSpec as P

BLK = 128
WB = 4
FSEL = 16
CAP = 2

LANES = 128
MASKED = -1e30
SCALE = math.log2(math.e) / 12.0
NT = (((1,), (1,)), ((), ()))


CHAIN = 4
BIG = 1 << 30


def pair_names(spans):
    return [(dst, src) for dst in range(spans) for src in range(dst + 1)]


def where_of(spans, dst, src, k):
    return CAP * pair_names(spans).index((dst, src)) + k


def middle_plan(read, own):
    edge = 2 * own - (WB - 1)
    fresh, rank, blocks = [], [], []
    count = jnp.int32(0)
    for dst in (3, 2):
        for k in range(CAP):
            b = read(dst, 1, k)
            new = (b < BIG) & (b < edge)
            for other in blocks:
                new &= b != other
            fresh.append(new)
            rank.append(count)
            blocks.append(b)
            count = count + jnp.where(new, 1, 0)
    mine = []
    for a in range(2 * CAP):
        b = jnp.int32(BIG)
        for new, r, block in zip(fresh, rank, blocks):
            b = jnp.where(new & (r == a), block, b)
        mine.append(b)
    first = [read(3, 0, k) for k in range(CAP)]
    extra = []
    for k in range(CAP):
        b = read(2, 0, k)
        new = b < BIG
        for other in first:
            new &= b != other
        extra.append(jnp.where(new, b, BIG))
    need = CAP + count + sum(jnp.where(b < BIG, 1, 0) for b in extra)
    return mine, count, first, extra, need


def prelude(
    spans, own, lists_in, counts, kv_in, table, choice, close_by, ready,
    raw, scr, turned, share, theirs, sem, own_sem,
):
    rims, _, heads, dh = raw.shape
    me = lax.axis_index("ctx")
    peer = {"groups": 1 - lax.axis_index("groups")}
    has_next = me + 1 < spans
    load = pltpu.make_async_copy(kv_in.at[0, pl.ds(own - rims, rims)], raw, own_sem.at[0])
    load.start()
    barrier = pltpu.get_barrier_semaphore()
    pl.semaphore_signal(barrier, inc=1, device_id=peer)

    @pl.when(me > 0)
    def _():
        pl.semaphore_signal(barrier, inc=1, device_id={"ctx": lax.rem(me + spans - 1, spans)})

    load.wait()

    def turn(r):
        scr[r] = raw[r].astype(jnp.float32).reshape(BLK * heads, dh)
        for h in range(heads):
            turned[r, h] = scr[r, pl.ds(h, BLK, stride=heads), :].astype(jnp.bfloat16)

    turn(rims - 1)
    pl.semaphore_wait(barrier, jnp.where(has_next, 2, 1))
    send = pltpu.make_async_remote_copy(
        src_ref=turned.at[rims - 1], dst_ref=close_by, send_sem=sem.at[2], recv_sem=sem.at[3],
        device_id={"ctx": lax.rem(me + 1, spans)})

    @pl.when(has_next)
    def _():
        send.start()

    slot = lax.broadcasted_iota(jnp.int32, lists_in.shape, 0)
    block_of = lax.broadcasted_iota(jnp.int32, lists_in.shape, 1)
    listed = jnp.where(slot < counts[...], lists_in[...], -1)
    found = {}
    for dst, src in pair_names(spans):
        inside = ((listed >= src * own) & (listed < src * own + own)
                  & (block_of >= dst * own) & (block_of < dst * own + own))
        first = jnp.min(jnp.where(inside, listed, BIG))
        second = jnp.min(jnp.where(inside & (listed > first), listed, BIG))
        for k, b in enumerate((first, second)):
            found[dst, src, k] = b
            table[where_of(spans, dst, src, k)] = b
    need = middle_plan(lambda dst, src, k: found[dst, src, k], own)[-1]
    share[...] = jnp.broadcast_to(need, share.shape)
    swap = pltpu.make_async_remote_copy(
        src_ref=share, dst_ref=theirs, send_sem=sem.at[0], recv_sem=sem.at[1], device_id=peer)
    swap.start()
    for r in range(rims - 1):
        turn(r)
    keep = pltpu.make_async_copy(turned.at[pl.ds(0, rims - 1)], ready, own_sem.at[1])
    keep.start()
    swap.wait()
    most = jnp.max(jnp.maximum(share[...], theirs[...]))
    choice[0] = jnp.clip(most - 3 * CAP, 0, CAP)
    keep.wait()

    @pl.when(me > 0)
    def _():
        send.wait_recv()

    @pl.when(has_next)
    def _():
        send.wait_send()


def relay_kernel(
    spans, room, lists_in, counts, table, close_by, ready, q_in, kv_in, out,
    q_raw, raw, mine, loc, rim, relay, sendbuf, qh, acc, top, bias, scr, done, o_raw,
    in_sem, x_sem, rz_send, rz_recv, rf_send, rf_recv,
    z_send, z_recv, f_send, f_recv, out_sem,
):
    toks, heads, dh = q_in.shape
    own = toks // BLK
    me = lax.axis_index("ctx")
    side = lax.axis_index("rep")
    mate = {"rep": 1 - side}
    rims = WB - 1
    pieces = f_send.shape[0] - room + 1
    part_heads = heads // pieces
    has_next = me + 1 < spans
    ahead = {"ctx": lax.rem(me + 1, spans)}
    late, last = room - 2, room - 1

    load_kv = pltpu.make_async_copy(kv_in.at[0], raw, in_sem.at[0])
    load_q = pltpu.make_async_copy(q_in, q_raw, in_sem.at[1])
    load_rim = pltpu.make_async_copy(close_by, rim.at[side, rims - 1], in_sem.at[2])
    barrier = pltpu.get_barrier_semaphore()
    pl.semaphore_signal(barrier, inc=1, device_id=mate)

    @pl.when(me > 0)
    def _():
        pl.semaphore_signal(barrier, inc=1, device_id={"ctx": lax.rem(me + spans - 1, spans)})

    def rim_copy(j):
        return pltpu.make_async_remote_copy(
            src_ref=ready.at[rims - j], dst_ref=rim.at[side, rims - j],
            send_sem=rz_send.at[j - 1], recv_sem=rz_recv.at[j - 1], device_id=ahead)

    def rim_pass(j):
        return pltpu.make_async_remote_copy(
            src_ref=rim.at[side, rims - j], dst_ref=rim.at[side, rims - j],
            send_sem=rf_send.at[j - 1], recv_sem=rf_recv.at[j - 1], device_id=mate)

    def cut(ref, piece):
        return ref if piece is None else ref.at[pl.ds(piece * part_heads, part_heads)]

    def put(src, p, piece=None):
        at = p if piece is None else p + piece
        return pltpu.make_async_remote_copy(
            src_ref=cut(src, piece), dst_ref=cut(relay.at[side, p], piece),
            send_sem=z_send.at[at], recv_sem=z_recv.at[at], device_id=ahead)

    def came(p, piece=None):
        put(relay.at[side, p], p, piece).wait_recv()

    def hand(p, piece=None):
        at = p if piece is None else p + piece
        return pltpu.make_async_remote_copy(
            src_ref=cut(relay.at[side, p], piece), dst_ref=cut(relay.at[side, p], piece),
            send_sem=f_send.at[at], recv_sem=f_recv.at[at], device_id=mate)

    def put_last(src):
        for piece in range(pieces):
            put(src, last, piece).start()

    parts = scr.shape[0]

    def spread(part, block, store):
        scr[part] = block.astype(jnp.float32).reshape(BLK * heads, dh)
        for h in range(heads):
            store(h, scr[part, pl.ds(h, BLK, stride=heads), :].astype(jnp.bfloat16))

    def spread_mine(b, part):
        def store(h, x):
            mine[b, h] = x
            loc[side, b, h] = x

        spread(part, raw[b], store)

    pl.semaphore_wait(barrier, jnp.where(has_next, 2, 1))

    @pl.when(has_next)
    def _():
        for j in range(2, WB):
            rim_copy(j).start()

    load_kv.start()

    @pl.when(me > 0)
    def _():
        load_rim.start()

    load_q.start()
    load_kv.wait()

    def spread_all(b, _):
        spread_mine(b, lax.rem(b, parts))
        return 0

    lax.fori_loop(0, own, spread_all, 0)

    swap = pltpu.make_async_remote_copy(
        src_ref=mine, dst_ref=loc.at[side],
        send_sem=x_sem.at[0], recv_sem=x_sem.at[1], device_id=mate)
    swap.start()

    def read(dst, src, k):
        return table[where_of(spans, dst, src, k)]

    def local_row(block):
        return jnp.clip(jnp.where(block < BIG, block - me * own, 0), 0, own - 1)

    def fill(p, block):
        sendbuf[p] = mine[local_row(block)]

    own_list, own_count, first, extra, _ = middle_plan(read, own)
    own_late, own_last = late - 2, last - 2

    @pl.when(me == 0)
    def _():
        for p, (dst, k) in zip((0, 1, 2, 3, late, last), ((3, 0), (3, 1), (2, 0), (2, 1), (1, 0), (1, 1))):
            fill(p, read(dst, 0, k))
        for p in (0, 1, 2, 3, late):
            put(sendbuf.at[p], p).start()
        put_last(sendbuf.at[last])

    early = [0, 1] + list(range(4, late))

    @pl.when(me == 1)
    def _():
        for p in early:
            fill(p, own_list[p if p < 2 else p - 2])
        for p in early:
            put(sendbuf.at[p], p).start()

    @pl.when(me == 2)
    def _():
        for k in range(CAP):
            fill(k, read(3, 2, k))
        for k in range(CAP):
            put(sendbuf.at[k], k).start()

    @pl.when(me == 0)
    def _():
        for j in range(rims):
            rim[:, j] = jnp.zeros((2,) + rim.shape[2:], rim.dtype)

    held = [0] * room
    for k in range(CAP):
        held[k] = jnp.where(me == 3, read(3, 2, k), own_list[k])
        held[2 + k] = jnp.where(me == 3, read(3, 1, k), first[k])
    for p in range(4, late):
        held[p] = jnp.where(me == 2, own_list[p - 2], BIG)
    both = (extra[0] < BIG) & (extra[1] < BIG)
    mid_late = jnp.where(both, extra[0], BIG)
    mid_last = jnp.where(extra[1] < BIG, extra[1], extra[0])
    if own_late < 2 * CAP:
        mid_late = jnp.where(own_count > own_late, own_list[own_late], mid_late)
    if own_last < 2 * CAP:
        mid_last = jnp.where(own_count > own_last, own_list[own_last], mid_last)
    held[late] = jnp.where(me == 3, read(3, 0, 0), jnp.where(me == 2, mid_late, read(1, 0, 0)))
    held[last] = jnp.where(me == 3, read(3, 0, 1), jnp.where(me == 2, mid_last, read(1, 0, 1)))
    edge = 2 * own - rims
    seen_again = []
    for k in range(CAP):
        b = read(2, 1, k)
        seen_again.append(jnp.where((b < BIG) & (b >= edge) & (me == 2), b, BIG))
    mine_far = []
    for k in range(CAP):
        b = read(0, 0, k)
        for s in range(1, spans):
            b = jnp.where(me == s, read(s, s, k), b)
        mine_far.append(b)

    slot = lax.broadcasted_iota(jnp.int32, lists_in.shape, 0)
    block_of = lax.broadcasted_iota(jnp.int32, lists_in.shape, 1)
    listed = jnp.where(slot < counts[...], lists_in[...], -1)

    for n, block in enumerate(mine_far + seen_again + held + [jnp.int32(BIG)]):
        hit = jnp.max(jnp.where(listed == block, 1.0, 0.0), axis=0, keepdims=True)
        for c in range(own):
            mark = jnp.where(block_of[:1] == me * own + c, hit, 0.0)
            mark = jnp.max(mark, axis=1, keepdims=True)
            bias[n, c] = jnp.broadcast_to(jnp.where(mark > 0.5, 0.0, MASKED), (1, BLK))

    load_q.wait()

    def spread_q(c, _):
        at = pl.ds(pl.multiple_of(c * BLK, BLK), BLK)

        def store(h, x):
            qh[h, at, :] = x

        spread(lax.rem(c, parts), q_raw[at], store)
        return 0

    lax.fori_loop(0, own, spread_q, 0)
    swap.wait_recv()

    span = WB * BLK

    def near_block(c, rows, get):
        key_pos = lax.broadcasted_iota(jnp.int32, (BLK, span), 1) - rims * BLK
        query_pos = lax.broadcasted_iota(jnp.int32, (BLK, span), 0)
        seen = key_pos <= query_pos
        if isinstance(c, int):
            seen &= (key_pos + c * BLK >= 0) | (me > 0)
        for h in range(heads):
            s = lax.dot_general(qh[h, rows, :], get(0, h), NT,
                                preferred_element_type=jnp.float32) * SCALE
            s = jnp.where(seen, s, MASKED)
            m = jnp.max(s, axis=1, keepdims=True)
            p = jnp.exp2(s - m).astype(jnp.bfloat16)
            v = jnp.concatenate([get(1, h), jnp.ones((span, LANES), jnp.bfloat16)], axis=1)
            acc[h, rows, :] = jnp.dot(p, v, preferred_element_type=jnp.float32)
            top[h, rows, :] = jnp.broadcast_to(m, (BLK, LANES))

    def near(c, _):
        keys = pl.ds(c - rims, WB)
        near_block(c, pl.ds(pl.multiple_of(c * BLK, BLK), BLK), lambda kind, h: loc[kind, keys, h].reshape(span, dh))
        return 0

    lax.fori_loop(rims, own, near, 0)

    ones = jnp.ones((BLK, LANES), jnp.bfloat16)

    tall = 2 * BLK

    def merged(h, rows, k, v, row_bias):
        s = lax.dot_general(qh[h, rows, :], k, NT, preferred_element_type=jnp.float32) * SCALE
        s = s + row_bias
        old = top[h, rows, :]
        m = jnp.maximum(old, jnp.max(s, axis=1, keepdims=True))
        spread_m = jnp.concatenate([m] * (s.shape[1] // LANES), axis=1)
        p = jnp.exp2(s - spread_m).astype(jnp.bfloat16)
        a = jnp.exp2(old - m)
        return m, acc[h, rows, :] * jnp.concatenate([a, a], axis=1) + jnp.dot(
            p, v, preferred_element_type=jnp.float32)

    def far_head(h, at, gets, keep, begin=0):
        k = jnp.concatenate([get(0, h) for get in gets], axis=0)
        v = jnp.concatenate([jnp.concatenate([get(1, h), ones], axis=1) for get in gets], axis=0)
        for low in range(begin, toks, tall):
            row_bias = jnp.concatenate([
                jnp.concatenate([jnp.broadcast_to(bias[n, low // BLK + i], (BLK, BLK)) for n in at], axis=1)
                for i in range(tall // BLK)], axis=0)
            rows = pl.ds(low, tall)
            keep(h, low, *merged(h, rows, k, v, row_bias))

    def far(at, gets, begin=0):
        def hold(h, low, m, total):
            acc[h, pl.ds(low, tall), :] = total
            top[h, pl.ds(low, tall), :] = m

        def one(h, _):
            far_head(h, at, gets, hold, begin)
            return 0

        lax.fori_loop(0, heads, one, 0)

    def relayed(p):
        return lambda kind, h: relay[kind, p, h]

    def owned(row):
        return lambda kind, h: loc[kind, row, h]

    def window(row):
        return lambda kind, h: rim[kind, row, h]

    far((0, 1), [owned(local_row(b)) for b in mine_far], WB * BLK // tall * tall)

    @pl.when(me > 0)
    def _():
        load_rim.wait()
        rim_pass(1).start()
        for j in range(2, WB):
            rim_copy(j).wait_recv()
            rim_pass(j).start()
        for j in range(1, WB):
            rim_pass(j).wait_recv()

    for c in range(rims):
        near_block(c, pl.ds(c * BLK, BLK), lambda kind, h: jnp.concatenate(
            [rim[kind, r, h] for r in range(c, rims)] + [loc[kind, b, h] for b in range(c + 1)], axis=0))

    base = 2 * CAP

    @pl.when(me == 1)
    def _():
        for k in range(CAP):
            came(k)
            put(relay.at[side, k], 2 + k).start()
        came(2)
        if own_late < 2 * CAP:
            sendbuf[late] = jnp.where(own_count > own_late, mine[local_row(own_list[own_late])], relay[side, 2])
            put(sendbuf.at[late], late).start()
        else:
            put(relay.at[side, 2], late).start()
        came(3)
        tail = jnp.where(extra[1] < BIG, relay[side, 3], relay[side, 2])
        if own_last < 2 * CAP:
            tail = jnp.where(own_count > own_last, mine[local_row(own_list[own_last])], tail)
        sendbuf[last] = tail
        put_last(sendbuf.at[last])

    @pl.when(me == 2)
    def _():
        for k in range(CAP):
            came(k)
            hand(k).start()
            b = read(3, 1, k)
            pick = relay[side, 0]
            if k == 1:
                pick = jnp.where(b == own_list[1], relay[side, 1], pick)
            for j in range(1, WB):
                pick = jnp.where(b == 2 * own - j, rim[side, rims - j], pick)
            sendbuf[2 + k] = pick
            put(sendbuf.at[2 + k], 2 + k).start()
            if k == 0:
                far((2, 3), [window(jnp.clip(jnp.where(b < BIG, b - edge, 0), 0, rims - 1)) for b in seen_again])

    @pl.when(me == 3)
    def _():
        for k in range(CAP):
            came(k)
            hand(k).start()

    @pl.when(me > 1)
    def _():
        for k in range(CAP):
            hand(k).wait_recv()
        far((base, base + 1), [relayed(0), relayed(1)])

    if late > 4:
        @pl.when(me == 2)
        def _():
            for p in range(4, late):
                came(p)
                hand(p).start()
            for p in range(4, late):
                hand(p).wait_recv()
            at = [base + p for p in range(4, late)]
            far((at + [base + room])[:2], [relayed(p) for p in (4, late - 1)])

    @pl.when(me == 2)
    def _():
        came(2)
        put(relay.at[side, 2], late).start()
        hand(2).start()
        came(3)
        put_last(relay.at[side, 3])
        hand(3).start()

    @pl.when(me == 3)
    def _():
        for p in (2, 3):
            came(p)
            hand(p).start()

    @pl.when(me > 1)
    def _():
        for p in (2, 3):
            hand(p).wait_recv()
        far((base + 2, base + 3), [relayed(2), relayed(3)])

    def finish(h, low, m, total):
        for i in range(tall // BLK):
            part = total[i * BLK:(i + 1) * BLK]
            done[low // BLK + i, pl.ds(h, BLK, stride=heads), :] = part[:, :dh] / part[:, dh:]

    @pl.when(me > 0)
    def _():
        came(late)
        hand(late).start()
        came(last, 0)
        hand(last, 0).start()
        hand(late).wait_recv()

        def one(piece, _):
            @pl.when(piece + 1 < pieces)
            def _():
                came(last, piece + 1)
                hand(last, piece + 1).start()

            hand(last, piece).wait_recv()
            far_head(piece, (base + late, base + last), [relayed(late), relayed(last)], finish)
            return 0

        lax.fori_loop(0, pieces, one, 0)

    @pl.when(me == 0)
    def _():
        def one(h, _):
            for low in range(0, toks, tall):
                finish(h, low, None, acc[h, pl.ds(low, tall), :])
            return 0

        lax.fori_loop(0, heads, one, 0)

    def write(c):
        rows = pl.ds(pl.multiple_of(c * BLK, BLK), BLK)
        return pltpu.make_async_copy(o_raw.at[rows], out.at[rows], out_sem.at[c])

    def pack(c, _):
        rows = pl.ds(pl.multiple_of(c * BLK, BLK), BLK)
        o_raw[rows] = done[c].reshape(BLK, heads, dh).astype(jnp.bfloat16)
        write(c).start()
        return 0

    lax.fori_loop(0, own, pack, 0)

    def drain(c, _):
        write(c).wait()
        return 0

    lax.fori_loop(0, own, drain, 0)
    swap.wait_send()

    @pl.when(has_next)
    def _():
        for j in range(2, WB):
            rim_copy(j).wait_send()
        for p in (0, 1, 2, 3, late):
            put(relay.at[side, p], p).wait_send()
        for piece in range(pieces):
            put(relay.at[side, last], last, piece).wait_send()

    @pl.when(me == 1)
    def _():
        for p in range(4, late):
            put(relay.at[side, p], p).wait_send()

    @pl.when(me > 0)
    def _():
        for j in range(1, WB):
            rim_pass(j).wait_send()
        hand(late).wait_send()
        for piece in range(pieces):
            hand(last, piece).wait_send()

    @pl.when(me > 1)
    def _():
        for p in range(4):
            hand(p).wait_send()

    @pl.when(me == 2)
    def _():
        for p in range(4, late):
            hand(p).wait_send()


def settle(src, out, buf, read_sem, write_sem):
    toks = src.shape[0]
    step = toks // read_sem.shape[0]

    def fetch(i):
        at = pl.ds(i * step, step)
        return pltpu.make_async_copy(src.at[at], buf.at[at], read_sem.at[i])

    def store(i):
        at = pl.ds(i * step, step)
        return pltpu.make_async_copy(buf.at[at], out.at[at], write_sem.at[i])

    for i in range(read_sem.shape[0]):
        fetch(i).start()
    for i in range(read_sem.shape[0]):
        fetch(i).wait()
        store(i).start()
    for i in range(read_sem.shape[0]):
        store(i).wait()


def chained(spans, room, lists, counts, table, close_by, ready, queries, keys_values):
    toks, heads, dh = queries.shape
    own = toks // BLK
    rims = WB - 1
    bf16, f32 = jnp.bfloat16, jnp.float32
    hbm = pl.BlockSpec(memory_space=pl.ANY)
    vmem = pl.BlockSpec(memory_space=pltpu.VMEM)
    dma = pltpu.SemaphoreType.DMA
    pieces = heads
    ways = room - 1 + pieces
    return pl.pallas_call(
        functools.partial(relay_kernel, spans, room),
        out_shape=jax.ShapeDtypeStruct((toks, heads, dh), bf16),
        in_specs=[vmem, vmem, pl.BlockSpec(memory_space=pltpu.SMEM), hbm, hbm, hbm, hbm],
        out_specs=hbm,
        scratch_shapes=[
            pltpu.VMEM((toks, heads, dh), bf16),
            pltpu.VMEM((own, BLK, heads, dh), bf16),
            pltpu.VMEM((own, heads, BLK, dh), bf16),
            pltpu.VMEM((2, own, heads, BLK, dh), bf16),
            pltpu.VMEM((2, rims, heads, BLK, dh), bf16),
            pltpu.VMEM((2, room, heads, BLK, dh), bf16),
            pltpu.VMEM((room, heads, BLK, dh), bf16),
            pltpu.VMEM((heads, toks, dh), bf16),
            pltpu.VMEM((heads, toks, dh + LANES), f32),
            pltpu.VMEM((heads, toks, LANES), f32),
            pltpu.VMEM((2 * CAP + room + 1, own, 1, BLK), f32),
            pltpu.VMEM((2, BLK * heads, dh), f32),
            pltpu.VMEM((own, BLK * heads, dh), f32),
            pltpu.VMEM((toks, heads, dh), bf16),
            dma((3,)), dma((2,)),
            dma((rims,)), dma((rims,)), dma((rims,)), dma((rims,)),
            dma((ways,)), dma((ways,)), dma((ways,)), dma((ways,)),
            dma((own,)),
        ],
        compiler_params=pltpu.CompilerParams(
            collective_id=room, has_side_effects=True, vmem_limit_bytes=50 << 20),
    )(lists, counts, table, close_by, ready, queries, keys_values)


def local(spans, groups, queries, keys_values, far_list, far_count):
    toks, heads, members, dh = queries.shape
    own = toks // BLK
    if spans != CHAIN or groups != 2 or own < WB:
        return direct(spans, queries, keys_values, far_list, far_count)
    hbm = pl.BlockSpec(memory_space=pl.ANY)
    vmem = pl.BlockSpec(memory_space=pltpu.VMEM)
    smem = pl.BlockSpec(memory_space=pltpu.SMEM)
    dma = pltpu.SemaphoreType.DMA
    lists, counts = far_list.T, far_count.reshape(1, -1)
    rims, bf16 = WB - 1, jnp.bfloat16
    keys_values = keys_values.reshape(-1, own, BLK, heads, dh)
    table, choice, close_by, ready = pl.pallas_call(
        functools.partial(prelude, spans, own),
        out_shape=[
            jax.ShapeDtypeStruct((CAP * len(pair_names(spans)),), jnp.int32),
            jax.ShapeDtypeStruct((1,), jnp.int32),
            jax.ShapeDtypeStruct((heads, BLK, dh), bf16),
            jax.ShapeDtypeStruct((rims - 1, heads, BLK, dh), bf16),
        ],
        in_specs=[vmem, vmem, hbm],
        out_specs=[smem, smem, hbm, hbm],
        scratch_shapes=[
            pltpu.VMEM((rims, BLK, heads, dh), bf16),
            pltpu.VMEM((rims, BLK * heads, dh), jnp.float32),
            pltpu.VMEM((rims, heads, BLK, dh), bf16),
            pltpu.VMEM((8, LANES), jnp.int32), pltpu.VMEM((8, LANES), jnp.int32),
            dma((4,)), dma((2,)),
        ],
        compiler_params=pltpu.CompilerParams(collective_id=1, has_side_effects=True, vmem_limit_bytes=62 << 20),
    )(lists, counts, keys_values)
    args = (lists, counts, table, close_by, ready, queries.reshape(toks, heads, dh), keys_values)
    result = lax.switch(choice[0], [functools.partial(chained, spans, room) for room in (6, 7, 8)], *args)
    result = pl.pallas_call(
        settle,
        out_shape=jax.ShapeDtypeStruct(result.shape, result.dtype),
        in_specs=[hbm], out_specs=hbm,
        scratch_shapes=[pltpu.VMEM(result.shape, result.dtype), dma((own,)), dma((own,))],
        compiler_params=pltpu.CompilerParams(vmem_limit_bytes=16 << 20),
    )(result)
    return result.reshape(queries.shape)


def direct_kernel(
    spans, lists_in, counts, q_in, kv_in, out,
    q_raw, raw, mine, loc, rim_raw, rim, far, sendbuf, qh, acc, top, bias, scr, o_raw,
    in_sem, x_send, x_recv, rz_send, rz_recv, rf_send, rf_recv,
    fz_send, fz_recv, ff_send, ff_recv, out_sem,
):
    toks, heads, dh = q_in.shape
    own = toks // BLK
    me = lax.axis_index("ctx")
    side = lax.axis_index("rep")
    mate = {"rep": 1 - side}
    rims = WB - 1

    load_kv = pltpu.make_async_copy(kv_in.at[0], raw, in_sem.at[0])
    load_q = pltpu.make_async_copy(q_in, q_raw, in_sem.at[1])
    load_kv.start()
    load_q.start()

    barrier = pltpu.get_barrier_semaphore()
    pl.semaphore_signal(barrier, inc=1, device_id=mate)

    def greet(i, _):
        pl.semaphore_signal(barrier, inc=1, device_id={"ctx": lax.rem(me + i, spans)})
        return 0

    lax.fori_loop(1, spans, greet, 0)
    pl.semaphore_wait(barrier, spans)

    def raw_copy(to):
        return pltpu.make_async_remote_copy(
            src_ref=kv_in.at[0, own - 1], dst_ref=rim_raw.at[side],
            send_sem=rz_send.at[0], recv_sem=rz_recv.at[0], device_id={"ctx": to},
        )

    def raw_pass():
        return pltpu.make_async_remote_copy(
            src_ref=rim_raw.at[side], dst_ref=rim_raw.at[side],
            send_sem=rf_send.at[0], recv_sem=rf_recv.at[0], device_id=mate,
        )

    def rim_copy(j, to):
        return pltpu.make_async_remote_copy(
            src_ref=mine.at[own - j],
            dst_ref=rim.at[side, j - 1],
            send_sem=rz_send.at[j - 1], recv_sem=rz_recv.at[j - 1],
            device_id={"ctx": to},
        )

    def rim_pass(j):
        return pltpu.make_async_remote_copy(
            src_ref=rim.at[side, j - 1],
            dst_ref=rim.at[side, j - 1],
            send_sem=rf_send.at[j - 1], recv_sem=rf_recv.at[j - 1],
            device_id=mate,
        )

    def far_copy(to):
        return pltpu.make_async_remote_copy(
            src_ref=sendbuf.at[to], dst_ref=far.at[side, me],
            send_sem=fz_send.at[to], recv_sem=fz_recv.at[me],
            device_id={"ctx": to},
        )

    def far_arrival(src):
        return pltpu.make_async_remote_copy(
            src_ref=sendbuf.at[src], dst_ref=far.at[side, src],
            send_sem=fz_send.at[src], recv_sem=fz_recv.at[src],
            device_id={"ctx": src},
        )

    def far_pass(src):
        return pltpu.make_async_remote_copy(
            src_ref=far.at[side, src], dst_ref=far.at[side, src],
            send_sem=ff_send.at[src], recv_sem=ff_recv.at[src],
            device_id=mate,
        )

    ahead = lax.rem(me + 1, spans)
    has_next = me + 1 < spans

    @pl.when(has_next)
    def _():
        raw_copy(ahead).start()

    def spread(part, block, put):
        scr[part] = block.astype(jnp.float32).reshape(BLK * heads, dh)
        for h in range(heads):
            put(h, scr[part, pl.ds(h, BLK, stride=heads), :].astype(jnp.bfloat16))

    load_kv.wait()
    parts = scr.shape[0]

    def spread_mine(i, _):
        for part in range(parts):
            b = i * parts + part

            def put(h, x):
                mine[b, h] = x
                loc[side, b, h] = x

            spread(part, raw[b], put)
        return 0

    lax.fori_loop(0, own // parts, spread_mine, 0)

    swap = pltpu.make_async_remote_copy(
        src_ref=mine, dst_ref=loc.at[side],
        send_sem=x_send, recv_sem=x_recv, device_id=mate,
    )
    swap.start()

    big = jnp.int32(1 << 30)
    slot = lax.broadcasted_iota(jnp.int32, lists_in.shape, 0)
    block_of = lax.broadcasted_iota(jnp.int32, lists_in.shape, 1)
    listed = jnp.where(slot < counts[...], lists_in[...], -1)

    def slots(dst, src):
        inside = ((listed >= src * own) & (listed < src * own + own)
                  & (block_of >= dst * own) & (block_of < dst * own + own))
        first = jnp.min(jnp.where(inside, listed, big))
        second = jnp.min(jnp.where(inside & (listed > first), listed, big))
        return first, second

    def local_row(block):
        row = jnp.where(block < big, block - me * own, 0)
        return jnp.clip(row, 0, own - 1)

    def fill(i, _):
        to = spans - 1 - i
        found = slots(to, me)
        for k in range(CAP):
            sendbuf[to, k] = mine[local_row(found[k])]
        return 0

    later = spans - 1 - me
    lax.fori_loop(0, later, fill, 0)

    def push(i, _):
        far_copy(spans - 1 - i).start()
        return 0

    lax.fori_loop(0, later, push, 0)

    @pl.when(has_next)
    def _():
        for j in range(2, WB):
            rim_copy(j, ahead).start()

    ones = jnp.ones((BLK, LANES), jnp.bfloat16)

    def fill_bias(src, _):
        found = slots(me, src)
        for k in range(CAP):
            hit = jnp.max(jnp.where(listed == found[k], 1.0, 0.0), axis=0, keepdims=True)
            for c in range(own):
                mark = jnp.where(block_of[:1] == me * own + c, hit, 0.0)
                mark = jnp.max(mark, axis=1, keepdims=True)
                bias[src, c, :, k * BLK:(k + 1) * BLK] = jnp.broadcast_to(
                    jnp.where(mark > 0.5, 0.0, MASKED), (1, BLK))
        return 0

    lax.fori_loop(0, me + 1, fill_bias, 0)

    load_q.wait()

    def spread_q(i, _):
        for part in range(parts):
            at = pl.ds(pl.multiple_of((i * parts + part) * BLK, BLK), BLK)

            def put(h, x):
                qh[h, at, :] = x

            spread(part, q_raw[at], put)
        return 0

    lax.fori_loop(0, own // parts, spread_q, 0)
    swap.wait_recv()

    wide = min(WB, own)
    span = wide * BLK

    def near(c, _):
        rows = pl.ds(pl.multiple_of(c * BLK, BLK), BLK)
        low = jnp.maximum(c - (WB - 1), 0)
        keys = pl.ds(low, wide)
        key_pos = low * BLK + lax.broadcasted_iota(jnp.int32, (BLK, span), 1)
        query_pos = c * BLK + lax.broadcasted_iota(jnp.int32, (BLK, span), 0)
        seen = key_pos <= query_pos
        for h in range(heads):
            s = lax.dot_general(qh[h, rows, :], loc[0, keys, h].reshape(span, dh), NT,
                                preferred_element_type=jnp.float32) * SCALE
            s = jnp.where(seen, s, MASKED)
            m = jnp.max(s, axis=1, keepdims=True)
            p = jnp.exp2(s - m).astype(jnp.bfloat16)
            v = jnp.concatenate([loc[1, keys, h].reshape(span, dh)] + [jnp.ones((span, LANES), jnp.bfloat16)], axis=1)
            acc[h, rows, :] = jnp.dot(p, v, preferred_element_type=jnp.float32)
            top[h, rows, :] = jnp.broadcast_to(m, (BLK, LANES))
        return 0

    lax.fori_loop(0, own, near, 0)

    def merge(h, rows, k, v, row_bias):
        s = lax.dot_general(qh[h, rows, :], k, NT, preferred_element_type=jnp.float32) * SCALE
        s = s + row_bias
        old = top[h, rows, :]
        m = jnp.maximum(old, jnp.max(s, axis=1, keepdims=True))
        spread_m = jnp.concatenate([m] * (s.shape[1] // LANES), axis=1)
        p = jnp.exp2(s - spread_m).astype(jnp.bfloat16)
        a = jnp.exp2(old - m)
        acc[h, rows, :] = acc[h, rows, :] * jnp.concatenate([a, a], axis=1) + jnp.dot(
            p, v, preferred_element_type=jnp.float32)
        top[h, rows, :] = m

    def stack(get, h):
        k = jnp.concatenate([get(0, n, h) for n in range(CAP)], axis=0)
        v = jnp.concatenate(
            [jnp.concatenate([get(1, n, h), ones], axis=1) for n in range(CAP)], axis=0)
        return k, v

    def far_all(src, get):
        def one(c, _):
            rows = pl.ds(pl.multiple_of(c * BLK, BLK), BLK)
            row_bias = bias[src, c]
            for h in range(heads):
                merge(h, rows, *stack(get, h), row_bias)
            return 0

        lax.fori_loop(0, own, one, 0)

    found_mine = slots(me, me)
    at_mine = [local_row(b) for b in found_mine]
    far_all(me, lambda kind, k, h: loc[kind, at_mine[k], h])

    @pl.when(me > 0)
    def _():
        raw_copy(ahead).wait_recv()
        raw_pass().start()
        raw_pass().wait_recv()

        def put_k(h, x):
            rim[0, 0, h] = x

        def put_v(h, x):
            rim[1, 0, h] = x

        spread(0, rim_raw[0], put_k)
        spread(1, rim_raw[1], put_v)

    def far_step(src, _):
        far_arrival(src).wait_recv()
        far_pass(src).start()
        far_pass(src).wait_recv()
        far_all(src, lambda kind, k, h: far[kind, src, k, h])
        return 0

    lax.fori_loop(0, me, far_step, 0)

    def finish(c, _):
        rows = pl.ds(pl.multiple_of(c * BLK, BLK), BLK)
        part = lax.rem(c, parts)
        for h in range(heads):
            scr[part, pl.ds(h, BLK, stride=heads), :] = acc[h, rows, :dh] / acc[h, rows, dh:]
        o_raw[rows] = scr[part].reshape(BLK, heads, dh).astype(jnp.bfloat16)
        pltpu.make_async_copy(o_raw.at[rows], out.at[rows], out_sem.at[c]).start()
        return 0

    lane = lax.broadcasted_iota(jnp.int32, (1, CAP * BLK), 1)
    once = jnp.where(lane < BLK, 0.0, MASKED)

    def close(i, _):
        last = own - 1 - i
        j = WB - 1 - last

        @pl.when((me > 0) & (j > 1))
        def _():
            rim_copy(j, ahead).wait_recv()
            rim_pass(j).start()
            rim_pass(j).wait_recv()

        def one(c, _):
            rows = pl.ds(pl.multiple_of(c * BLK, BLK), BLK)
            for h in range(heads):
                merge(h, rows, *stack(lambda kind, n, h: rim[kind, j - 1, h], h), once)
            return 0

        @pl.when((me > 0) & (j > 0))
        def _():
            lax.fori_loop(0, last + 1, one, 0)

        return finish(last, 0)

    lax.fori_loop(0, own, close, 0)

    def drain(c, _):
        rows = pl.ds(pl.multiple_of(c * BLK, BLK), BLK)
        pltpu.make_async_copy(o_raw.at[rows], out.at[rows], out_sem.at[c]).wait()
        return 0

    lax.fori_loop(0, own, drain, 0)
    swap.wait_send()

    @pl.when(has_next)
    def _():
        raw_copy(ahead).wait_send()
        for j in range(2, WB):
            rim_copy(j, ahead).wait_send()

    @pl.when(me > 0)
    def _():
        raw_pass().wait_send()
        for j in range(2, WB):
            rim_pass(j).wait_send()

    def sent(i, _):
        far_copy(spans - 1 - i).wait_send()
        return 0

    lax.fori_loop(0, later, sent, 0)

    def passed(src, _):
        far_pass(src).wait_send()
        return 0

    lax.fori_loop(0, me, passed, 0)


def direct(spans, queries, keys_values, far_list, far_count):
    toks, heads, members, dh = queries.shape
    own = toks // BLK
    rims = WB - 1
    bf16, f32 = jnp.bfloat16, jnp.float32
    hbm = pl.BlockSpec(memory_space=pl.ANY)
    dma = pltpu.SemaphoreType.DMA
    result = pl.pallas_call(
        functools.partial(direct_kernel, spans),
        out_shape=jax.ShapeDtypeStruct((toks, heads, dh), bf16),
        in_specs=[pl.BlockSpec(memory_space=pltpu.VMEM)] * 2 + [hbm, hbm],
        out_specs=hbm,
        scratch_shapes=[
            pltpu.VMEM((toks, heads, dh), bf16),
            pltpu.VMEM((own, BLK, heads, dh), bf16),
            pltpu.VMEM((own, heads, BLK, dh), bf16),
            pltpu.VMEM((2, own, heads, BLK, dh), bf16),
            pltpu.VMEM((2, BLK, heads, dh), bf16),
            pltpu.VMEM((2, rims, heads, BLK, dh), bf16),
            pltpu.VMEM((2, spans, CAP, heads, BLK, dh), bf16),
            pltpu.VMEM((spans, CAP, heads, BLK, dh), bf16),
            pltpu.VMEM((heads, toks, dh), bf16),
            pltpu.VMEM((heads, toks, dh + LANES), f32),
            pltpu.VMEM((heads, toks, LANES), f32),
            pltpu.VMEM((spans, own, 1, CAP * BLK), f32),
            pltpu.VMEM((2, BLK * heads, dh), f32),
            pltpu.VMEM((toks, heads, dh), bf16),
            dma((2,)), dma, dma,
            dma((rims,)), dma((rims,)), dma((rims,)), dma((rims,)),
            dma((spans,)), dma((spans,)), dma((spans,)), dma((spans,)),
            dma((own,)),
        ],
        compiler_params=pltpu.CompilerParams(
            collective_id=0, has_side_effects=True, vmem_limit_bytes=62 << 20),
    )(far_list.T, far_count.reshape(1, -1), queries.reshape(toks, heads, dh), keys_values.reshape(-1, own, BLK, heads, dh))
    return result.reshape(queries.shape)


def solution(mesh):
    in_specs = (
        P(("groups", "ctx"), "head", "rep", None),
        P("rep", ("groups", "ctx"), "head", None),
        P("groups", None),
        P("groups"),
    )
    out_specs = P(("groups", "ctx"), "head", "rep", None)
    return jax.shard_map(
        functools.partial(local, mesh.shape["ctx"], mesh.shape["groups"]),
        mesh=mesh, in_specs=in_specs, out_specs=out_specs, check_vma=False)
```

```python
import functools
import math

import jax
import jax.numpy as jnp
from jax import lax
from jax.experimental import pallas as pl
from jax.experimental.pallas import tpu as pltpu
from jax.sharding import PartitionSpec as P

BLK = 128
WB = 4
FSEL = 16
CAP = 2

LANES = 128
MASKED = -1e30
SCALE = math.log2(math.e) / 12.0
NT = (((1,), (1,)), ((), ()))


CHAIN = 4
BIG = 1 << 30


def pair_names(spans):
    return [(dst, src) for dst in range(spans) for src in range(dst + 1)]


def where_of(spans, dst, src, k):
    return CAP * pair_names(spans).index((dst, src)) + k


def middle_plan(read, own):
    edge = 2 * own - (WB - 1)
    fresh, rank, blocks = [], [], []
    count = jnp.int32(0)
    for dst in (3, 2):
        for k in range(CAP):
            b = read(dst, 1, k)
            new = (b < BIG) & (b < edge)
            for other in blocks:
                new &= b != other
            fresh.append(new)
            rank.append(count)
            blocks.append(b)
            count = count + jnp.where(new, 1, 0)
    mine = []
    for a in range(2 * CAP):
        b = jnp.int32(BIG)
        for new, r, block in zip(fresh, rank, blocks):
            b = jnp.where(new & (r == a), block, b)
        mine.append(b)
    first = [read(3, 0, k) for k in range(CAP)]
    extra = []
    for k in range(CAP):
        b = read(2, 0, k)
        new = b < BIG
        for other in first:
            new &= b != other
        extra.append(jnp.where(new, b, BIG))
    need = CAP + count + sum(jnp.where(b < BIG, 1, 0) for b in extra)
    return mine, count, first, extra, need


def prelude(
    spans, own, lists_in, counts, kv_in, table, choice, close_by, ready,
    raw, scr, turned, share, theirs, sem, own_sem,
):
    rims, _, heads, dh = raw.shape
    me = lax.axis_index("ctx")
    peer = {"groups": 1 - lax.axis_index("groups")}
    has_next = me + 1 < spans
    load = pltpu.make_async_copy(kv_in.at[0, pl.ds(own - rims, rims)], raw, own_sem.at[0])
    load.start()
    barrier = pltpu.get_barrier_semaphore()
    pl.semaphore_signal(barrier, inc=1, device_id=peer)

    @pl.when(me > 0)
    def _():
        pl.semaphore_signal(barrier, inc=1, device_id={"ctx": lax.rem(me + spans - 1, spans)})

    load.wait()

    def turn(r):
        scr[r] = raw[r].astype(jnp.float32).reshape(BLK * heads, dh)
        for h in range(heads):
            turned[r, h] = scr[r, pl.ds(h, BLK, stride=heads), :].astype(jnp.bfloat16)

    turn(rims - 1)
    pl.semaphore_wait(barrier, jnp.where(has_next, 2, 1))
    send = pltpu.make_async_remote_copy(
        src_ref=turned.at[rims - 1], dst_ref=close_by, send_sem=sem.at[2], recv_sem=sem.at[3],
        device_id={"ctx": lax.rem(me + 1, spans)})

    @pl.when(has_next)
    def _():
        send.start()

    slot = lax.broadcasted_iota(jnp.int32, lists_in.shape, 0)
    block_of = lax.broadcasted_iota(jnp.int32, lists_in.shape, 1)
    listed = jnp.where(slot < counts[...], lists_in[...], -1)
    found = {}
    for dst, src in pair_names(spans):
        inside = ((listed >= src * own) & (listed < src * own + own)
                  & (block_of >= dst * own) & (block_of < dst * own + own))
        first = jnp.min(jnp.where(inside, listed, BIG))
        second = jnp.min(jnp.where(inside & (listed > first), listed, BIG))
        for k, b in enumerate((first, second)):
            found[dst, src, k] = b
            table[where_of(spans, dst, src, k)] = b
    need = middle_plan(lambda dst, src, k: found[dst, src, k], own)[-1]
    share[...] = jnp.broadcast_to(need, share.shape)
    swap = pltpu.make_async_remote_copy(
        src_ref=share, dst_ref=theirs, send_sem=sem.at[0], recv_sem=sem.at[1], device_id=peer)
    swap.start()
    for r in range(rims - 1):
        turn(r)
    keep = pltpu.make_async_copy(turned.at[pl.ds(0, rims - 1)], ready, own_sem.at[1])
    keep.start()
    swap.wait()
    most = jnp.max(jnp.maximum(share[...], theirs[...]))
    choice[0] = jnp.clip(most - 3 * CAP, 0, CAP)
    keep.wait()

    @pl.when(me > 0)
    def _():
        send.wait_recv()

    @pl.when(has_next)
    def _():
        send.wait_send()


def relay_kernel(
    spans, room, lists_in, counts, table, close_by, ready, q_in, kv_in, out,
    q_raw, raw, mine, loc, rim, relay, sendbuf, qh, acc, top, bias, scr, done,
    in_sem, x_sem, rz_send, rz_recv, rf_send, rf_recv,
    z_send, z_recv, f_send, f_recv,
):
    toks, heads, dh = q_in.shape
    own = toks // BLK
    me = lax.axis_index("ctx")
    side = lax.axis_index("rep")
    mate = {"rep": 1 - side}
    rims = WB - 1
    pieces = f_send.shape[0] - room + 1
    part_heads = heads // pieces
    has_next = me + 1 < spans
    ahead = {"ctx": lax.rem(me + 1, spans)}
    late, last = room - 2, room - 1

    load_kv = pltpu.make_async_copy(kv_in.at[0], raw, in_sem.at[0])
    load_q = pltpu.make_async_copy(q_in, q_raw, in_sem.at[1])
    load_rim = pltpu.make_async_copy(close_by, rim.at[side, rims - 1], in_sem.at[2])
    barrier = pltpu.get_barrier_semaphore()
    pl.semaphore_signal(barrier, inc=1, device_id=mate)

    @pl.when(me > 0)
    def _():
        pl.semaphore_signal(barrier, inc=1, device_id={"ctx": lax.rem(me + spans - 1, spans)})

    def rim_copy(j):
        return pltpu.make_async_remote_copy(
            src_ref=ready.at[rims - j], dst_ref=rim.at[side, rims - j],
            send_sem=rz_send.at[j - 1], recv_sem=rz_recv.at[j - 1], device_id=ahead)

    def rim_pass(j):
        return pltpu.make_async_remote_copy(
            src_ref=rim.at[side, rims - j], dst_ref=rim.at[side, rims - j],
            send_sem=rf_send.at[j - 1], recv_sem=rf_recv.at[j - 1], device_id=mate)

    def cut(ref, piece):
        return ref if piece is None else ref.at[pl.ds(piece * part_heads, part_heads)]

    def put(src, p, piece=None):
        at = p if piece is None else p + piece
        return pltpu.make_async_remote_copy(
            src_ref=cut(src, piece), dst_ref=cut(relay.at[side, p], piece),
            send_sem=z_send.at[at], recv_sem=z_recv.at[at], device_id=ahead)

    def came(p, piece=None):
        put(relay.at[side, p], p, piece).wait_recv()

    def hand(p, piece=None):
        at = p if piece is None else p + piece
        return pltpu.make_async_remote_copy(
            src_ref=cut(relay.at[side, p], piece), dst_ref=cut(relay.at[side, p], piece),
            send_sem=f_send.at[at], recv_sem=f_recv.at[at], device_id=mate)

    def put_last(src):
        for piece in range(pieces):
            put(src, last, piece).start()

    parts = scr.shape[0]

    def spread(part, block, store):
        scr[part] = block.astype(jnp.float32).reshape(BLK * heads, dh)
        for h in range(heads):
            store(h, scr[part, pl.ds(h, BLK, stride=heads), :].astype(jnp.bfloat16))

    def spread_mine(b, part):
        def store(h, x):
            mine[b, h] = x
            loc[side, b, h] = x

        spread(part, raw[b], store)

    pl.semaphore_wait(barrier, jnp.where(has_next, 2, 1))

    @pl.when(has_next)
    def _():
        for j in range(2, WB):
            rim_copy(j).start()

    load_kv.start()

    @pl.when(me > 0)
    def _():
        load_rim.start()

    load_q.start()
    load_kv.wait()

    def spread_all(b, _):
        spread_mine(b, lax.rem(b, parts))
        return 0

    lax.fori_loop(0, own, spread_all, 0)

    swap = pltpu.make_async_remote_copy(
        src_ref=mine, dst_ref=loc.at[side],
        send_sem=x_sem.at[0], recv_sem=x_sem.at[1], device_id=mate)
    swap.start()

    def read(dst, src, k):
        return table[where_of(spans, dst, src, k)]

    def local_row(block):
        return jnp.clip(jnp.where(block < BIG, block - me * own, 0), 0, own - 1)

    def fill(p, block):
        sendbuf[p] = mine[local_row(block)]

    own_list, own_count, first, extra, _ = middle_plan(read, own)
    own_late, own_last = late - 2, last - 2

    @pl.when(me == 0)
    def _():
        for p, (dst, k) in zip((0, 1, 2, 3, late, last), ((3, 0), (3, 1), (2, 0), (2, 1), (1, 0), (1, 1))):
            fill(p, read(dst, 0, k))
        for p in (0, 1, 2, 3, late):
            put(sendbuf.at[p], p).start()
        put_last(sendbuf.at[last])

    early = [0, 1] + list(range(4, late))

    @pl.when(me == 1)
    def _():
        for p in early:
            fill(p, own_list[p if p < 2 else p - 2])
        for p in early:
            put(sendbuf.at[p], p).start()

    @pl.when(me == 2)
    def _():
        for k in range(CAP):
            fill(k, read(3, 2, k))
        for k in range(CAP):
            put(sendbuf.at[k], k).start()

    @pl.when(me == 0)
    def _():
        for j in range(rims):
            rim[:, j] = jnp.zeros((2,) + rim.shape[2:], rim.dtype)

    held = [0] * room
    for k in range(CAP):
        held[k] = jnp.where(me == 3, read(3, 2, k), own_list[k])
        held[2 + k] = jnp.where(me == 3, read(3, 1, k), first[k])
    for p in range(4, late):
        held[p] = jnp.where(me == 2, own_list[p - 2], BIG)
    both = (extra[0] < BIG) & (extra[1] < BIG)
    mid_late = jnp.where(both, extra[0], BIG)
    mid_last = jnp.where(extra[1] < BIG, extra[1], extra[0])
    if own_late < 2 * CAP:
        mid_late = jnp.where(own_count > own_late, own_list[own_late], mid_late)
    if own_last < 2 * CAP:
        mid_last = jnp.where(own_count > own_last, own_list[own_last], mid_last)
    held[late] = jnp.where(me == 3, read(3, 0, 0), jnp.where(me == 2, mid_late, read(1, 0, 0)))
    held[last] = jnp.where(me == 3, read(3, 0, 1), jnp.where(me == 2, mid_last, read(1, 0, 1)))
    edge = 2 * own - rims
    seen_again = []
    for k in range(CAP):
        b = read(2, 1, k)
        seen_again.append(jnp.where((b < BIG) & (b >= edge) & (me == 2), b, BIG))
    mine_far = []
    for k in range(CAP):
        b = read(0, 0, k)
        for s in range(1, spans):
            b = jnp.where(me == s, read(s, s, k), b)
        mine_far.append(b)

    slot = lax.broadcasted_iota(jnp.int32, lists_in.shape, 0)
    block_of = lax.broadcasted_iota(jnp.int32, lists_in.shape, 1)
    listed = jnp.where(slot < counts[...], lists_in[...], -1)

    for n, block in enumerate(mine_far + seen_again + held + [jnp.int32(BIG)]):
        hit = jnp.max(jnp.where(listed == block, 1.0, 0.0), axis=0, keepdims=True)
        for c in range(own):
            mark = jnp.where(block_of[:1] == me * own + c, hit, 0.0)
            mark = jnp.max(mark, axis=1, keepdims=True)
            bias[n, c] = jnp.broadcast_to(jnp.where(mark > 0.5, 0.0, MASKED), (1, BLK))

    load_q.wait()

    def spread_q(c, _):
        at = pl.ds(pl.multiple_of(c * BLK, BLK), BLK)

        def store(h, x):
            qh[h, at, :] = x

        spread(lax.rem(c, parts), q_raw[at], store)
        return 0

    lax.fori_loop(0, own, spread_q, 0)
    swap.wait_recv()

    span = WB * BLK

    def near_block(c, rows, get):
        key_pos = lax.broadcasted_iota(jnp.int32, (BLK, span), 1) - rims * BLK
        query_pos = lax.broadcasted_iota(jnp.int32, (BLK, span), 0)
        seen = key_pos <= query_pos
        if isinstance(c, int):
            seen &= (key_pos + c * BLK >= 0) | (me > 0)
        for h in range(heads):
            s = lax.dot_general(qh[h, rows, :], get(0, h), NT,
                                preferred_element_type=jnp.float32) * SCALE
            s = jnp.where(seen, s, MASKED)
            m = jnp.max(s, axis=1, keepdims=True)
            p = jnp.exp2(s - m).astype(jnp.bfloat16)
            v = jnp.concatenate([get(1, h), jnp.ones((span, LANES), jnp.bfloat16)], axis=1)
            acc[h, rows, :] = jnp.dot(p, v, preferred_element_type=jnp.float32)
            top[h, rows, :] = jnp.broadcast_to(m, (BLK, LANES))

    def near(c, _):
        keys = pl.ds(c - rims, WB)
        near_block(c, pl.ds(pl.multiple_of(c * BLK, BLK), BLK), lambda kind, h: loc[kind, keys, h].reshape(span, dh))
        return 0

    lax.fori_loop(rims, own, near, 0)

    ones = jnp.ones((BLK, LANES), jnp.bfloat16)

    tall = 2 * BLK

    def merged(h, rows, k, v, row_bias):
        s = lax.dot_general(qh[h, rows, :], k, NT, preferred_element_type=jnp.float32) * SCALE
        s = s + row_bias
        old = top[h, rows, :]
        m = jnp.maximum(old, jnp.max(s, axis=1, keepdims=True))
        spread_m = jnp.concatenate([m] * (s.shape[1] // LANES), axis=1)
        p = jnp.exp2(s - spread_m).astype(jnp.bfloat16)
        a = jnp.exp2(old - m)
        return m, acc[h, rows, :] * jnp.concatenate([a, a], axis=1) + jnp.dot(
            p, v, preferred_element_type=jnp.float32)

    def far_head(h, at, gets, keep, begin=0):
        k = jnp.concatenate([get(0, h) for get in gets], axis=0)
        v = jnp.concatenate([jnp.concatenate([get(1, h), ones], axis=1) for get in gets], axis=0)
        for low in range(begin, toks, tall):
            row_bias = jnp.concatenate([
                jnp.concatenate([jnp.broadcast_to(bias[n, low // BLK + i], (BLK, BLK)) for n in at], axis=1)
                for i in range(tall // BLK)], axis=0)
            rows = pl.ds(low, tall)
            keep(h, low, *merged(h, rows, k, v, row_bias))

    def far(at, gets, begin=0):
        def hold(h, low, m, total):
            acc[h, pl.ds(low, tall), :] = total
            top[h, pl.ds(low, tall), :] = m

        def one(h, _):
            far_head(h, at, gets, hold, begin)
            return 0

        lax.fori_loop(0, heads, one, 0)

    def relayed(p):
        return lambda kind, h: relay[kind, p, h]

    def owned(row):
        return lambda kind, h: loc[kind, row, h]

    def window(row):
        return lambda kind, h: rim[kind, row, h]

    far((0, 1), [owned(local_row(b)) for b in mine_far], WB * BLK // tall * tall)

    @pl.when(me > 0)
    def _():
        load_rim.wait()
        rim_pass(1).start()
        for j in range(2, WB):
            rim_copy(j).wait_recv()
            rim_pass(j).start()
        for j in range(1, WB):
            rim_pass(j).wait_recv()

    for c in range(rims):
        near_block(c, pl.ds(c * BLK, BLK), lambda kind, h: jnp.concatenate(
            [rim[kind, r, h] for r in range(c, rims)] + [loc[kind, b, h] for b in range(c + 1)], axis=0))

    base = 2 * CAP

    @pl.when(me == 1)
    def _():
        for k in range(CAP):
            came(k)
            put(relay.at[side, k], 2 + k).start()
        came(2)
        if own_late < 2 * CAP:
            sendbuf[late] = jnp.where(own_count > own_late, mine[local_row(own_list[own_late])], relay[side, 2])
            put(sendbuf.at[late], late).start()
        else:
            put(relay.at[side, 2], late).start()
        came(3)
        tail = jnp.where(extra[1] < BIG, relay[side, 3], relay[side, 2])
        if own_last < 2 * CAP:
            tail = jnp.where(own_count > own_last, mine[local_row(own_list[own_last])], tail)
        sendbuf[last] = tail
        put_last(sendbuf.at[last])

    @pl.when(me == 2)
    def _():
        for k in range(CAP):
            came(k)
            hand(k).start()
            b = read(3, 1, k)
            pick = relay[side, 0]
            if k == 1:
                pick = jnp.where(b == own_list[1], relay[side, 1], pick)
            for j in range(1, WB):
                pick = jnp.where(b == 2 * own - j, rim[side, rims - j], pick)
            sendbuf[2 + k] = pick
            put(sendbuf.at[2 + k], 2 + k).start()
            if k == 0:
                far((2, 3), [window(jnp.clip(jnp.where(b < BIG, b - edge, 0), 0, rims - 1)) for b in seen_again])

    @pl.when(me == 3)
    def _():
        for k in range(CAP):
            came(k)
            hand(k).start()

    @pl.when(me > 1)
    def _():
        for k in range(CAP):
            hand(k).wait_recv()
        far((base, base + 1), [relayed(0), relayed(1)])

    if late > 4:
        @pl.when(me == 2)
        def _():
            for p in range(4, late):
                came(p)
                hand(p).start()
            for p in range(4, late):
                hand(p).wait_recv()
            at = [base + p for p in range(4, late)]
            far((at + [base + room])[:2], [relayed(p) for p in (4, late - 1)])

    @pl.when(me == 2)
    def _():
        came(2)
        put(relay.at[side, 2], late).start()
        hand(2).start()
        came(3)
        put_last(relay.at[side, 3])
        hand(3).start()

    @pl.when(me == 3)
    def _():
        for p in (2, 3):
            came(p)
            hand(p).start()

    @pl.when(me > 1)
    def _():
        for p in (2, 3):
            hand(p).wait_recv()
        far((base + 2, base + 3), [relayed(2), relayed(3)])

    def finish(h, low, m, total):
        for i in range(tall // BLK):
            part = total[i * BLK:(i + 1) * BLK]
            done[low // BLK + i, pl.ds(h, BLK, stride=heads), :] = part[:, :dh] / part[:, dh:]

    @pl.when(me > 0)
    def _():
        came(late)
        hand(late).start()
        came(last, 0)
        hand(last, 0).start()
        hand(late).wait_recv()

        def one(piece, _):
            @pl.when(piece + 1 < pieces)
            def _():
                came(last, piece + 1)
                hand(last, piece + 1).start()

            hand(last, piece).wait_recv()
            far_head(piece, (base + late, base + last), [relayed(late), relayed(last)], finish)
            return 0

        lax.fori_loop(0, pieces, one, 0)

    @pl.when(me == 0)
    def _():
        def one(h, _):
            for low in range(0, toks, tall):
                finish(h, low, None, acc[h, pl.ds(low, tall), :])
            return 0

        lax.fori_loop(0, heads, one, 0)

    def pack(c, _):
        rows = pl.ds(pl.multiple_of(c * BLK, BLK), BLK)
        out[rows] = done[c].reshape(BLK, heads, dh).astype(jnp.bfloat16)
        return 0

    lax.fori_loop(0, own, pack, 0)
    swap.wait_send()

    @pl.when(has_next)
    def _():
        for j in range(2, WB):
            rim_copy(j).wait_send()
        for p in (0, 1, 2, 3, late):
            put(relay.at[side, p], p).wait_send()
        for piece in range(pieces):
            put(relay.at[side, last], last, piece).wait_send()

    @pl.when(me == 1)
    def _():
        for p in range(4, late):
            put(relay.at[side, p], p).wait_send()

    @pl.when(me > 0)
    def _():
        for j in range(1, WB):
            rim_pass(j).wait_send()
        hand(late).wait_send()
        for piece in range(pieces):
            hand(last, piece).wait_send()

    @pl.when(me > 1)
    def _():
        for p in range(4):
            hand(p).wait_send()

    @pl.when(me == 2)
    def _():
        for p in range(4, late):
            hand(p).wait_send()


def settle(src, out, sem):
    step = src.shape[0] // sem.shape[0]

    def move(i):
        at = pl.ds(i * step, step)
        return pltpu.make_async_copy(src.at[at], out.at[at], sem.at[i])

    for i in range(sem.shape[0]):
        move(i).start()
    for i in range(sem.shape[0]):
        move(i).wait()


def chained(spans, room, lists, counts, table, close_by, ready, queries, keys_values):
    toks, heads, dh = queries.shape
    own = toks // BLK
    rims = WB - 1
    bf16, f32 = jnp.bfloat16, jnp.float32
    hbm = pl.BlockSpec(memory_space=pl.ANY)
    vmem = pl.BlockSpec(memory_space=pltpu.VMEM)
    dma = pltpu.SemaphoreType.DMA
    pieces = heads
    ways = room - 1 + pieces
    return pl.pallas_call(
        functools.partial(relay_kernel, spans, room),
        out_shape=jax.ShapeDtypeStruct((toks, heads, dh), bf16),
        in_specs=[vmem, vmem, pl.BlockSpec(memory_space=pltpu.SMEM), hbm, hbm, hbm, hbm],
        out_specs=vmem,
        scratch_shapes=[
            pltpu.VMEM((toks, heads, dh), bf16),
            pltpu.VMEM((own, BLK, heads, dh), bf16),
            pltpu.VMEM((own, heads, BLK, dh), bf16),
            pltpu.VMEM((2, own, heads, BLK, dh), bf16),
            pltpu.VMEM((2, rims, heads, BLK, dh), bf16),
            pltpu.VMEM((2, room, heads, BLK, dh), bf16),
            pltpu.VMEM((room, heads, BLK, dh), bf16),
            pltpu.VMEM((heads, toks, dh), bf16),
            pltpu.VMEM((heads, toks, dh + LANES), f32),
            pltpu.VMEM((heads, toks, LANES), f32),
            pltpu.VMEM((2 * CAP + room + 1, own, 1, BLK), f32),
            pltpu.VMEM((2, BLK * heads, dh), f32),
            pltpu.VMEM((own, BLK * heads, dh), f32),
            dma((3,)), dma((2,)),
            dma((rims,)), dma((rims,)), dma((rims,)), dma((rims,)),
            dma((ways,)), dma((ways,)), dma((ways,)), dma((ways,)),
        ],
        compiler_params=pltpu.CompilerParams(
            collective_id=room, has_side_effects=True, vmem_limit_bytes=50 << 20),
    )(lists, counts, table, close_by, ready, queries, keys_values)


def local(spans, groups, queries, keys_values, far_list, far_count):
    toks, heads, members, dh = queries.shape
    own = toks // BLK
    if spans != CHAIN or groups != 2 or own < WB:
        return direct(spans, queries, keys_values, far_list, far_count)
    hbm = pl.BlockSpec(memory_space=pl.ANY)
    vmem = pl.BlockSpec(memory_space=pltpu.VMEM)
    smem = pl.BlockSpec(memory_space=pltpu.SMEM)
    dma = pltpu.SemaphoreType.DMA
    lists, counts = far_list.T, far_count.reshape(1, -1)
    rims, bf16 = WB - 1, jnp.bfloat16
    keys_values = keys_values.reshape(-1, own, BLK, heads, dh)
    table, choice, close_by, ready = pl.pallas_call(
        functools.partial(prelude, spans, own),
        out_shape=[
            jax.ShapeDtypeStruct((CAP * len(pair_names(spans)),), jnp.int32),
            jax.ShapeDtypeStruct((1,), jnp.int32),
            jax.ShapeDtypeStruct((heads, BLK, dh), bf16),
            jax.ShapeDtypeStruct((rims - 1, heads, BLK, dh), bf16),
        ],
        in_specs=[vmem, vmem, hbm],
        out_specs=[smem, smem, hbm, hbm],
        scratch_shapes=[
            pltpu.VMEM((rims, BLK, heads, dh), bf16),
            pltpu.VMEM((rims, BLK * heads, dh), jnp.float32),
            pltpu.VMEM((rims, heads, BLK, dh), bf16),
            pltpu.VMEM((8, LANES), jnp.int32), pltpu.VMEM((8, LANES), jnp.int32),
            dma((4,)), dma((2,)),
        ],
        compiler_params=pltpu.CompilerParams(collective_id=1, has_side_effects=True, vmem_limit_bytes=62 << 20),
    )(lists, counts, keys_values)
    args = (lists, counts, table, close_by, ready, queries.reshape(toks, heads, dh), keys_values)
    result = lax.switch(choice[0], [functools.partial(chained, spans, room) for room in (6, 7, 8)], *args)
    result = pl.pallas_call(
        settle,
        out_shape=jax.ShapeDtypeStruct(result.shape, result.dtype),
        in_specs=[vmem], out_specs=hbm,
        scratch_shapes=[dma((own,))],
        compiler_params=pltpu.CompilerParams(vmem_limit_bytes=16 << 20),
    )(result)
    return result.reshape(queries.shape)


def direct_kernel(
    spans, lists_in, counts, q_in, kv_in, out,
    q_raw, raw, mine, loc, rim_raw, rim, far, sendbuf, qh, acc, top, bias, scr, o_raw,
    in_sem, x_send, x_recv, rz_send, rz_recv, rf_send, rf_recv,
    fz_send, fz_recv, ff_send, ff_recv, out_sem,
):
    toks, heads, dh = q_in.shape
    own = toks // BLK
    me = lax.axis_index("ctx")
    side = lax.axis_index("rep")
    mate = {"rep": 1 - side}
    rims = WB - 1

    load_kv = pltpu.make_async_copy(kv_in.at[0], raw, in_sem.at[0])
    load_q = pltpu.make_async_copy(q_in, q_raw, in_sem.at[1])
    load_kv.start()
    load_q.start()

    barrier = pltpu.get_barrier_semaphore()
    pl.semaphore_signal(barrier, inc=1, device_id=mate)

    def greet(i, _):
        pl.semaphore_signal(barrier, inc=1, device_id={"ctx": lax.rem(me + i, spans)})
        return 0

    lax.fori_loop(1, spans, greet, 0)
    pl.semaphore_wait(barrier, spans)

    def raw_copy(to):
        return pltpu.make_async_remote_copy(
            src_ref=kv_in.at[0, own - 1], dst_ref=rim_raw.at[side],
            send_sem=rz_send.at[0], recv_sem=rz_recv.at[0], device_id={"ctx": to},
        )

    def raw_pass():
        return pltpu.make_async_remote_copy(
            src_ref=rim_raw.at[side], dst_ref=rim_raw.at[side],
            send_sem=rf_send.at[0], recv_sem=rf_recv.at[0], device_id=mate,
        )

    def rim_copy(j, to):
        return pltpu.make_async_remote_copy(
            src_ref=mine.at[own - j],
            dst_ref=rim.at[side, j - 1],
            send_sem=rz_send.at[j - 1], recv_sem=rz_recv.at[j - 1],
            device_id={"ctx": to},
        )

    def rim_pass(j):
        return pltpu.make_async_remote_copy(
            src_ref=rim.at[side, j - 1],
            dst_ref=rim.at[side, j - 1],
            send_sem=rf_send.at[j - 1], recv_sem=rf_recv.at[j - 1],
            device_id=mate,
        )

    def far_copy(to):
        return pltpu.make_async_remote_copy(
            src_ref=sendbuf.at[to], dst_ref=far.at[side, me],
            send_sem=fz_send.at[to], recv_sem=fz_recv.at[me],
            device_id={"ctx": to},
        )

    def far_arrival(src):
        return pltpu.make_async_remote_copy(
            src_ref=sendbuf.at[src], dst_ref=far.at[side, src],
            send_sem=fz_send.at[src], recv_sem=fz_recv.at[src],
            device_id={"ctx": src},
        )

    def far_pass(src):
        return pltpu.make_async_remote_copy(
            src_ref=far.at[side, src], dst_ref=far.at[side, src],
            send_sem=ff_send.at[src], recv_sem=ff_recv.at[src],
            device_id=mate,
        )

    ahead = lax.rem(me + 1, spans)
    has_next = me + 1 < spans

    @pl.when(has_next)
    def _():
        raw_copy(ahead).start()

    def spread(part, block, put):
        scr[part] = block.astype(jnp.float32).reshape(BLK * heads, dh)
        for h in range(heads):
            put(h, scr[part, pl.ds(h, BLK, stride=heads), :].astype(jnp.bfloat16))

    load_kv.wait()
    parts = scr.shape[0]

    def spread_mine(i, _):
        for part in range(parts):
            b = i * parts + part

            def put(h, x):
                mine[b, h] = x
                loc[side, b, h] = x

            spread(part, raw[b], put)
        return 0

    lax.fori_loop(0, own // parts, spread_mine, 0)

    swap = pltpu.make_async_remote_copy(
        src_ref=mine, dst_ref=loc.at[side],
        send_sem=x_send, recv_sem=x_recv, device_id=mate,
    )
    swap.start()

    big = jnp.int32(1 << 30)
    slot = lax.broadcasted_iota(jnp.int32, lists_in.shape, 0)
    block_of = lax.broadcasted_iota(jnp.int32, lists_in.shape, 1)
    listed = jnp.where(slot < counts[...], lists_in[...], -1)

    def slots(dst, src):
        inside = ((listed >= src * own) & (listed < src * own + own)
                  & (block_of >= dst * own) & (block_of < dst * own + own))
        first = jnp.min(jnp.where(inside, listed, big))
        second = jnp.min(jnp.where(inside & (listed > first), listed, big))
        return first, second

    def local_row(block):
        row = jnp.where(block < big, block - me * own, 0)
        return jnp.clip(row, 0, own - 1)

    def fill(i, _):
        to = spans - 1 - i
        found = slots(to, me)
        for k in range(CAP):
            sendbuf[to, k] = mine[local_row(found[k])]
        return 0

    later = spans - 1 - me
    lax.fori_loop(0, later, fill, 0)

    def push(i, _):
        far_copy(spans - 1 - i).start()
        return 0

    lax.fori_loop(0, later, push, 0)

    @pl.when(has_next)
    def _():
        for j in range(2, WB):
            rim_copy(j, ahead).start()

    ones = jnp.ones((BLK, LANES), jnp.bfloat16)

    def fill_bias(src, _):
        found = slots(me, src)
        for k in range(CAP):
            hit = jnp.max(jnp.where(listed == found[k], 1.0, 0.0), axis=0, keepdims=True)
            for c in range(own):
                mark = jnp.where(block_of[:1] == me * own + c, hit, 0.0)
                mark = jnp.max(mark, axis=1, keepdims=True)
                bias[src, c, :, k * BLK:(k + 1) * BLK] = jnp.broadcast_to(
                    jnp.where(mark > 0.5, 0.0, MASKED), (1, BLK))
        return 0

    lax.fori_loop(0, me + 1, fill_bias, 0)

    load_q.wait()

    def spread_q(i, _):
        for part in range(parts):
            at = pl.ds(pl.multiple_of((i * parts + part) * BLK, BLK), BLK)

            def put(h, x):
                qh[h, at, :] = x

            spread(part, q_raw[at], put)
        return 0

    lax.fori_loop(0, own // parts, spread_q, 0)
    swap.wait_recv()

    wide = min(WB, own)
    span = wide * BLK

    def near(c, _):
        rows = pl.ds(pl.multiple_of(c * BLK, BLK), BLK)
        low = jnp.maximum(c - (WB - 1), 0)
        keys = pl.ds(low, wide)
        key_pos = low * BLK + lax.broadcasted_iota(jnp.int32, (BLK, span), 1)
        query_pos = c * BLK + lax.broadcasted_iota(jnp.int32, (BLK, span), 0)
        seen = key_pos <= query_pos
        for h in range(heads):
            s = lax.dot_general(qh[h, rows, :], loc[0, keys, h].reshape(span, dh), NT,
                                preferred_element_type=jnp.float32) * SCALE
            s = jnp.where(seen, s, MASKED)
            m = jnp.max(s, axis=1, keepdims=True)
            p = jnp.exp2(s - m).astype(jnp.bfloat16)
            v = jnp.concatenate([loc[1, keys, h].reshape(span, dh)] + [jnp.ones((span, LANES), jnp.bfloat16)], axis=1)
            acc[h, rows, :] = jnp.dot(p, v, preferred_element_type=jnp.float32)
            top[h, rows, :] = jnp.broadcast_to(m, (BLK, LANES))
        return 0

    lax.fori_loop(0, own, near, 0)

    def merge(h, rows, k, v, row_bias):
        s = lax.dot_general(qh[h, rows, :], k, NT, preferred_element_type=jnp.float32) * SCALE
        s = s + row_bias
        old = top[h, rows, :]
        m = jnp.maximum(old, jnp.max(s, axis=1, keepdims=True))
        spread_m = jnp.concatenate([m] * (s.shape[1] // LANES), axis=1)
        p = jnp.exp2(s - spread_m).astype(jnp.bfloat16)
        a = jnp.exp2(old - m)
        acc[h, rows, :] = acc[h, rows, :] * jnp.concatenate([a, a], axis=1) + jnp.dot(
            p, v, preferred_element_type=jnp.float32)
        top[h, rows, :] = m

    def stack(get, h):
        k = jnp.concatenate([get(0, n, h) for n in range(CAP)], axis=0)
        v = jnp.concatenate(
            [jnp.concatenate([get(1, n, h), ones], axis=1) for n in range(CAP)], axis=0)
        return k, v

    def far_all(src, get):
        def one(c, _):
            rows = pl.ds(pl.multiple_of(c * BLK, BLK), BLK)
            row_bias = bias[src, c]
            for h in range(heads):
                merge(h, rows, *stack(get, h), row_bias)
            return 0

        lax.fori_loop(0, own, one, 0)

    found_mine = slots(me, me)
    at_mine = [local_row(b) for b in found_mine]
    far_all(me, lambda kind, k, h: loc[kind, at_mine[k], h])

    @pl.when(me > 0)
    def _():
        raw_copy(ahead).wait_recv()
        raw_pass().start()
        raw_pass().wait_recv()

        def put_k(h, x):
            rim[0, 0, h] = x

        def put_v(h, x):
            rim[1, 0, h] = x

        spread(0, rim_raw[0], put_k)
        spread(1, rim_raw[1], put_v)

    def far_step(src, _):
        far_arrival(src).wait_recv()
        far_pass(src).start()
        far_pass(src).wait_recv()
        far_all(src, lambda kind, k, h: far[kind, src, k, h])
        return 0

    lax.fori_loop(0, me, far_step, 0)

    def finish(c, _):
        rows = pl.ds(pl.multiple_of(c * BLK, BLK), BLK)
        part = lax.rem(c, parts)
        for h in range(heads):
            scr[part, pl.ds(h, BLK, stride=heads), :] = acc[h, rows, :dh] / acc[h, rows, dh:]
        o_raw[rows] = scr[part].reshape(BLK, heads, dh).astype(jnp.bfloat16)
        pltpu.make_async_copy(o_raw.at[rows], out.at[rows], out_sem.at[c]).start()
        return 0

    lane = lax.broadcasted_iota(jnp.int32, (1, CAP * BLK), 1)
    once = jnp.where(lane < BLK, 0.0, MASKED)

    def close(i, _):
        last = own - 1 - i
        j = WB - 1 - last

        @pl.when((me > 0) & (j > 1))
        def _():
            rim_copy(j, ahead).wait_recv()
            rim_pass(j).start()
            rim_pass(j).wait_recv()

        def one(c, _):
            rows = pl.ds(pl.multiple_of(c * BLK, BLK), BLK)
            for h in range(heads):
                merge(h, rows, *stack(lambda kind, n, h: rim[kind, j - 1, h], h), once)
            return 0

        @pl.when((me > 0) & (j > 0))
        def _():
            lax.fori_loop(0, last + 1, one, 0)

        return finish(last, 0)

    lax.fori_loop(0, own, close, 0)

    def drain(c, _):
        rows = pl.ds(pl.multiple_of(c * BLK, BLK), BLK)
        pltpu.make_async_copy(o_raw.at[rows], out.at[rows], out_sem.at[c]).wait()
        return 0

    lax.fori_loop(0, own, drain, 0)
    swap.wait_send()

    @pl.when(has_next)
    def _():
        raw_copy(ahead).wait_send()
        for j in range(2, WB):
            rim_copy(j, ahead).wait_send()

    @pl.when(me > 0)
    def _():
        raw_pass().wait_send()
        for j in range(2, WB):
            rim_pass(j).wait_send()

    def sent(i, _):
        far_copy(spans - 1 - i).wait_send()
        return 0

    lax.fori_loop(0, later, sent, 0)

    def passed(src, _):
        far_pass(src).wait_send()
        return 0

    lax.fori_loop(0, me, passed, 0)


def direct(spans, queries, keys_values, far_list, far_count):
    toks, heads, members, dh = queries.shape
    own = toks // BLK
    rims = WB - 1
    bf16, f32 = jnp.bfloat16, jnp.float32
    hbm = pl.BlockSpec(memory_space=pl.ANY)
    dma = pltpu.SemaphoreType.DMA
    result = pl.pallas_call(
        functools.partial(direct_kernel, spans),
        out_shape=jax.ShapeDtypeStruct((toks, heads, dh), bf16),
        in_specs=[pl.BlockSpec(memory_space=pltpu.VMEM)] * 2 + [hbm, hbm],
        out_specs=hbm,
        scratch_shapes=[
            pltpu.VMEM((toks, heads, dh), bf16),
            pltpu.VMEM((own, BLK, heads, dh), bf16),
            pltpu.VMEM((own, heads, BLK, dh), bf16),
            pltpu.VMEM((2, own, heads, BLK, dh), bf16),
            pltpu.VMEM((2, BLK, heads, dh), bf16),
            pltpu.VMEM((2, rims, heads, BLK, dh), bf16),
            pltpu.VMEM((2, spans, CAP, heads, BLK, dh), bf16),
            pltpu.VMEM((spans, CAP, heads, BLK, dh), bf16),
            pltpu.VMEM((heads, toks, dh), bf16),
            pltpu.VMEM((heads, toks, dh + LANES), f32),
            pltpu.VMEM((heads, toks, LANES), f32),
            pltpu.VMEM((spans, own, 1, CAP * BLK), f32),
            pltpu.VMEM((2, BLK * heads, dh), f32),
            pltpu.VMEM((toks, heads, dh), bf16),
            dma((2,)), dma, dma,
            dma((rims,)), dma((rims,)), dma((rims,)), dma((rims,)),
            dma((spans,)), dma((spans,)), dma((spans,)), dma((spans,)),
            dma((own,)),
        ],
        compiler_params=pltpu.CompilerParams(
            collective_id=0, has_side_effects=True, vmem_limit_bytes=62 << 20),
    )(far_list.T, far_count.reshape(1, -1), queries.reshape(toks, heads, dh), keys_values.reshape(-1, own, BLK, heads, dh))
    return result.reshape(queries.shape)


def solution(mesh):
    in_specs = (
        P(("groups", "ctx"), "head", "rep", None),
        P("rep", ("groups", "ctx"), "head", None),
        P("groups", None),
        P("groups"),
    )
    out_specs = P(("groups", "ctx"), "head", "rep", None)
    return jax.shard_map(
        functools.partial(local, mesh.shape["ctx"], mesh.shape["groups"]),
        mesh=mesh, in_specs=in_specs, out_specs=out_specs, check_vma=False)
```

```python
import functools
import math

import jax
import jax.numpy as jnp
from jax import lax
from jax.experimental import pallas as pl
from jax.experimental.pallas import tpu as pltpu
from jax.sharding import PartitionSpec as P

BLK = 128
WB = 4
FSEL = 16
CAP = 2

LANES = 128
MASKED = -1e30
SCALE = math.log2(math.e) / 12.0
NT = (((1,), (1,)), ((), ()))


CHAIN = 4
BIG = 1 << 30


def pair_names(spans):
    return [(dst, src) for dst in range(spans) for src in range(dst + 1)]


def where_of(spans, dst, src, k):
    return CAP * pair_names(spans).index((dst, src)) + k


def middle_plan(read, own):
    edge = 2 * own - (WB - 1)
    fresh, rank, blocks = [], [], []
    count = jnp.int32(0)
    for dst in (3, 2):
        for k in range(CAP):
            b = read(dst, 1, k)
            new = (b < BIG) & (b < edge)
            for other in blocks:
                new &= b != other
            fresh.append(new)
            rank.append(count)
            blocks.append(b)
            count = count + jnp.where(new, 1, 0)
    mine = []
    for a in range(2 * CAP):
        b = jnp.int32(BIG)
        for new, r, block in zip(fresh, rank, blocks):
            b = jnp.where(new & (r == a), block, b)
        mine.append(b)
    first = [read(3, 0, k) for k in range(CAP)]
    extra = []
    for k in range(CAP):
        b = read(2, 0, k)
        new = b < BIG
        for other in first:
            new &= b != other
        extra.append(jnp.where(new, b, BIG))
    need = CAP + count + sum(jnp.where(b < BIG, 1, 0) for b in extra)
    return mine, count, first, extra, need


def prelude(
    spans, own, lists_in, counts, kv_in, table, choice, close_by, ready,
    raw, scr, turned, share, theirs, sem, own_sem,
):
    rims, _, heads, dh = raw.shape
    me = lax.axis_index("ctx")
    peer = {"groups": 1 - lax.axis_index("groups")}
    has_next = me + 1 < spans
    load = pltpu.make_async_copy(kv_in.at[0, pl.ds(own - rims, rims)], raw, own_sem.at[0])
    load.start()
    barrier = pltpu.get_barrier_semaphore()
    pl.semaphore_signal(barrier, inc=1, device_id=peer)

    @pl.when(me > 0)
    def _():
        pl.semaphore_signal(barrier, inc=1, device_id={"ctx": lax.rem(me + spans - 1, spans)})

    load.wait()

    def turn(r):
        scr[r] = raw[r].astype(jnp.float32).reshape(BLK * heads, dh)
        for h in range(heads):
            turned[r, h] = scr[r, pl.ds(h, BLK, stride=heads), :].astype(jnp.bfloat16)

    turn(rims - 1)
    pl.semaphore_wait(barrier, jnp.where(has_next, 2, 1))
    send = pltpu.make_async_remote_copy(
        src_ref=turned.at[rims - 1], dst_ref=close_by, send_sem=sem.at[2], recv_sem=sem.at[3],
        device_id={"ctx": lax.rem(me + 1, spans)})

    @pl.when(has_next)
    def _():
        send.start()

    slot = lax.broadcasted_iota(jnp.int32, lists_in.shape, 0)
    block_of = lax.broadcasted_iota(jnp.int32, lists_in.shape, 1)
    listed = jnp.where(slot < counts[...], lists_in[...], -1)
    found = {}
    for dst, src in pair_names(spans):
        inside = ((listed >= src * own) & (listed < src * own + own)
                  & (block_of >= dst * own) & (block_of < dst * own + own))
        first = jnp.min(jnp.where(inside, listed, BIG))
        second = jnp.min(jnp.where(inside & (listed > first), listed, BIG))
        for k, b in enumerate((first, second)):
            found[dst, src, k] = b
            table[where_of(spans, dst, src, k)] = b
    need = middle_plan(lambda dst, src, k: found[dst, src, k], own)[-1]
    share[...] = jnp.broadcast_to(need, share.shape)
    swap = pltpu.make_async_remote_copy(
        src_ref=share, dst_ref=theirs, send_sem=sem.at[0], recv_sem=sem.at[1], device_id=peer)
    swap.start()
    for r in range(rims - 1):
        turn(r)
    keep = pltpu.make_async_copy(turned.at[pl.ds(0, rims - 1)], ready, own_sem.at[1])
    keep.start()
    swap.wait()
    most = jnp.max(jnp.maximum(share[...], theirs[...]))
    choice[0] = jnp.clip(most - 3 * CAP, 0, CAP)
    keep.wait()

    @pl.when(me > 0)
    def _():
        send.wait_recv()

    @pl.when(has_next)
    def _():
        send.wait_send()


def relay_kernel(
    spans, room, lists_in, counts, table, close_by, ready, q_in, kv_in, out,
    q_raw, raw, mine, loc, rim, relay, sendbuf, qh, acc, top, bias, scr, done,
    in_sem, x_sem, rz_send, rz_recv, rf_send, rf_recv,
    z_send, z_recv, f_send, f_recv,
):
    toks, heads, dh = q_in.shape
    own = toks // BLK
    me = lax.axis_index("ctx")
    side = lax.axis_index("rep")
    mate = {"rep": 1 - side}
    rims = WB - 1
    pieces = f_send.shape[0] - room + 1
    part_heads = heads // pieces
    has_next = me + 1 < spans
    ahead = {"ctx": lax.rem(me + 1, spans)}
    late, last = room - 2, room - 1

    load_kv = pltpu.make_async_copy(kv_in.at[0], raw, in_sem.at[0])
    load_q = pltpu.make_async_copy(q_in, q_raw, in_sem.at[1])
    load_rim = pltpu.make_async_copy(close_by, rim.at[side, rims - 1], in_sem.at[2])
    barrier = pltpu.get_barrier_semaphore()
    pl.semaphore_signal(barrier, inc=1, device_id=mate)

    @pl.when(me > 0)
    def _():
        pl.semaphore_signal(barrier, inc=1, device_id={"ctx": lax.rem(me + spans - 1, spans)})

    def rim_copy(j):
        return pltpu.make_async_remote_copy(
            src_ref=ready.at[rims - j], dst_ref=rim.at[side, rims - j],
            send_sem=rz_send.at[j - 1], recv_sem=rz_recv.at[j - 1], device_id=ahead)

    def rim_pass(j):
        return pltpu.make_async_remote_copy(
            src_ref=rim.at[side, rims - j], dst_ref=rim.at[side, rims - j],
            send_sem=rf_send.at[j - 1], recv_sem=rf_recv.at[j - 1], device_id=mate)

    def cut(ref, piece):
        return ref if piece is None else ref.at[pl.ds(piece * part_heads, part_heads)]

    def put(src, p, piece=None):
        at = p if piece is None else p + piece
        return pltpu.make_async_remote_copy(
            src_ref=cut(src, piece), dst_ref=cut(relay.at[side, p], piece),
            send_sem=z_send.at[at], recv_sem=z_recv.at[at], device_id=ahead)

    def came(p, piece=None):
        put(relay.at[side, p], p, piece).wait_recv()

    def hand(p, piece=None):
        at = p if piece is None else p + piece
        return pltpu.make_async_remote_copy(
            src_ref=cut(relay.at[side, p], piece), dst_ref=cut(relay.at[side, p], piece),
            send_sem=f_send.at[at], recv_sem=f_recv.at[at], device_id=mate)

    def put_last(src):
        for piece in range(pieces):
            put(src, last, piece).start()

    parts = scr.shape[0]

    def spread(part, block, store):
        scr[part] = block.astype(jnp.float32).reshape(BLK * heads, dh)
        for h in range(heads):
            store(h, scr[part, pl.ds(h, BLK, stride=heads), :].astype(jnp.bfloat16))

    def spread_mine(b, part):
        def store(h, x):
            mine[b, h] = x
            loc[side, b, h] = x

        spread(part, raw[b], store)

    pl.semaphore_wait(barrier, jnp.where(has_next, 2, 1))

    @pl.when(has_next)
    def _():
        for j in range(2, WB):
            rim_copy(j).start()

    load_kv.start()

    @pl.when(me > 0)
    def _():
        load_rim.start()

    load_q.start()
    load_kv.wait()

    def spread_all(b, _):
        spread_mine(b, lax.rem(b, parts))
        return 0

    lax.fori_loop(0, own, spread_all, 0)

    swap = pltpu.make_async_remote_copy(
        src_ref=mine, dst_ref=loc.at[side],
        send_sem=x_sem.at[0], recv_sem=x_sem.at[1], device_id=mate)
    swap.start()

    def read(dst, src, k):
        return table[where_of(spans, dst, src, k)]

    def local_row(block):
        return jnp.clip(jnp.where(block < BIG, block - me * own, 0), 0, own - 1)

    def fill(p, block):
        sendbuf[p] = mine[local_row(block)]

    own_list, own_count, first, extra, _ = middle_plan(read, own)
    own_late, own_last = late - 2, last - 2

    @pl.when(me == 0)
    def _():
        for p, (dst, k) in zip((0, 1, 2, 3, late, last), ((3, 0), (3, 1), (2, 0), (2, 1), (1, 0), (1, 1))):
            fill(p, read(dst, 0, k))
        for p in (0, 1, 2, 3, late):
            put(sendbuf.at[p], p).start()
        put_last(sendbuf.at[last])

    early = [0, 1] + list(range(4, late))

    @pl.when(me == 1)
    def _():
        for p in early:
            fill(p, own_list[p if p < 2 else p - 2])
        for p in early:
            put(sendbuf.at[p], p).start()

    @pl.when(me == 2)
    def _():
        for k in range(CAP):
            fill(k, read(3, 2, k))
        for k in range(CAP):
            put(sendbuf.at[k], k).start()

    @pl.when(me == 0)
    def _():
        for j in range(rims):
            rim[:, j] = jnp.zeros((2,) + rim.shape[2:], rim.dtype)

    held = [0] * room
    for k in range(CAP):
        held[k] = jnp.where(me == 3, read(3, 2, k), own_list[k])
        held[2 + k] = jnp.where(me == 3, read(3, 1, k), first[k])
    for p in range(4, late):
        held[p] = jnp.where(me == 2, own_list[p - 2], BIG)
    both = (extra[0] < BIG) & (extra[1] < BIG)
    mid_late = jnp.where(both, extra[0], BIG)
    mid_last = jnp.where(extra[1] < BIG, extra[1], extra[0])
    if own_late < 2 * CAP:
        mid_late = jnp.where(own_count > own_late, own_list[own_late], mid_late)
    if own_last < 2 * CAP:
        mid_last = jnp.where(own_count > own_last, own_list[own_last], mid_last)
    held[late] = jnp.where(me == 3, read(3, 0, 0), jnp.where(me == 2, mid_late, read(1, 0, 0)))
    held[last] = jnp.where(me == 3, read(3, 0, 1), jnp.where(me == 2, mid_last, read(1, 0, 1)))
    edge = 2 * own - rims
    seen_again = []
    for k in range(CAP):
        b = read(2, 1, k)
        seen_again.append(jnp.where((b < BIG) & (b >= edge) & (me == 2), b, BIG))
    mine_far = []
    for k in range(CAP):
        b = read(0, 0, k)
        for s in range(1, spans):
            b = jnp.where(me == s, read(s, s, k), b)
        mine_far.append(b)

    slot = lax.broadcasted_iota(jnp.int32, lists_in.shape, 0)
    block_of = lax.broadcasted_iota(jnp.int32, lists_in.shape, 1)
    listed = jnp.where(slot < counts[...], lists_in[...], -1)

    for n, block in enumerate(mine_far + seen_again + held + [jnp.int32(BIG)]):
        hit = jnp.max(jnp.where(listed == block, 1.0, 0.0), axis=0, keepdims=True)
        for c in range(own):
            mark = jnp.where(block_of[:1] == me * own + c, hit, 0.0)
            mark = jnp.max(mark, axis=1, keepdims=True)
            bias[n, c] = jnp.broadcast_to(jnp.where(mark > 0.5, 0.0, MASKED), (1, BLK))

    load_q.wait()

    def spread_q(c, _):
        at = pl.ds(pl.multiple_of(c * BLK, BLK), BLK)

        def store(h, x):
            qh[h, at, :] = x

        spread(lax.rem(c, parts), q_raw[at], store)
        return 0

    lax.fori_loop(0, own, spread_q, 0)
    swap.wait_recv()

    span = WB * BLK

    def near_block(c, rows, get):
        key_pos = lax.broadcasted_iota(jnp.int32, (BLK, span), 1) - rims * BLK
        query_pos = lax.broadcasted_iota(jnp.int32, (BLK, span), 0)
        seen = key_pos <= query_pos
        if isinstance(c, int):
            seen &= (key_pos + c * BLK >= 0) | (me > 0)
        for h in range(heads):
            s = lax.dot_general(qh[h, rows, :], get(0, h), NT,
                                preferred_element_type=jnp.float32) * SCALE
            s = jnp.where(seen, s, MASKED)
            m = jnp.max(s, axis=1, keepdims=True)
            p = jnp.exp2(s - m).astype(jnp.bfloat16)
            v = jnp.concatenate([get(1, h), jnp.ones((span, LANES), jnp.bfloat16)], axis=1)
            acc[h, rows, :] = jnp.dot(p, v, preferred_element_type=jnp.float32)
            top[h, rows, :] = jnp.broadcast_to(m, (BLK, LANES))

    def near(c, _):
        keys = pl.ds(c - rims, WB)
        near_block(c, pl.ds(pl.multiple_of(c * BLK, BLK), BLK), lambda kind, h: loc[kind, keys, h].reshape(span, dh))
        return 0

    lax.fori_loop(rims, own, near, 0)

    ones = jnp.ones((BLK, LANES), jnp.bfloat16)

    tall = 2 * BLK

    def merged(h, rows, k, v, row_bias):
        s = lax.dot_general(qh[h, rows, :], k, NT, preferred_element_type=jnp.float32) * SCALE
        s = s + row_bias
        old = top[h, rows, :]
        m = jnp.maximum(old, jnp.max(s, axis=1, keepdims=True))
        spread_m = jnp.concatenate([m] * (s.shape[1] // LANES), axis=1)
        p = jnp.exp2(s - spread_m).astype(jnp.bfloat16)
        a = jnp.exp2(old - m)
        return m, acc[h, rows, :] * jnp.concatenate([a, a], axis=1) + jnp.dot(
            p, v, preferred_element_type=jnp.float32)

    def far_head(h, at, gets, keep, begin=0):
        k = jnp.concatenate([get(0, h) for get in gets], axis=0)
        v = jnp.concatenate([jnp.concatenate([get(1, h), ones], axis=1) for get in gets], axis=0)
        for low in range(begin, toks, tall):
            row_bias = jnp.concatenate([
                jnp.concatenate([jnp.broadcast_to(bias[n, low // BLK + i], (BLK, BLK)) for n in at], axis=1)
                for i in range(tall // BLK)], axis=0)
            rows = pl.ds(low, tall)
            keep(h, low, *merged(h, rows, k, v, row_bias))

    def far(at, gets, begin=0):
        def hold(h, low, m, total):
            acc[h, pl.ds(low, tall), :] = total
            top[h, pl.ds(low, tall), :] = m

        def one(h, _):
            far_head(h, at, gets, hold, begin)
            return 0

        lax.fori_loop(0, heads, one, 0)

    def relayed(p):
        return lambda kind, h: relay[kind, p, h]

    def owned(row):
        return lambda kind, h: loc[kind, row, h]

    def window(row):
        return lambda kind, h: rim[kind, row, h]

    far((0, 1), [owned(local_row(b)) for b in mine_far], WB * BLK // tall * tall)

    @pl.when(me > 0)
    def _():
        load_rim.wait()
        rim_pass(1).start()
        for j in range(2, WB):
            rim_copy(j).wait_recv()
            rim_pass(j).start()
        for j in range(1, WB):
            rim_pass(j).wait_recv()

    for c in range(rims):
        near_block(c, pl.ds(c * BLK, BLK), lambda kind, h: jnp.concatenate(
            [rim[kind, r, h] for r in range(c, rims)] + [loc[kind, b, h] for b in range(c + 1)], axis=0))

    base = 2 * CAP

    @pl.when(me == 1)
    def _():
        for k in range(CAP):
            came(k)
            put(relay.at[side, k], 2 + k).start()
        came(2)
        if own_late < 2 * CAP:
            sendbuf[late] = jnp.where(own_count > own_late, mine[local_row(own_list[own_late])], relay[side, 2])
            put(sendbuf.at[late], late).start()
        else:
            put(relay.at[side, 2], late).start()
        came(3)
        tail = jnp.where(extra[1] < BIG, relay[side, 3], relay[side, 2])
        if own_last < 2 * CAP:
            tail = jnp.where(own_count > own_last, mine[local_row(own_list[own_last])], tail)
        sendbuf[last] = tail
        put_last(sendbuf.at[last])

    @pl.when(me == 2)
    def _():
        for k in range(CAP):
            came(k)
            hand(k).start()
            b = read(3, 1, k)
            pick = relay[side, 0]
            if k == 1:
                pick = jnp.where(b == own_list[1], relay[side, 1], pick)
            for j in range(1, WB):
                pick = jnp.where(b == 2 * own - j, rim[side, rims - j], pick)
            sendbuf[2 + k] = pick
            put(sendbuf.at[2 + k], 2 + k).start()
            if k == 0:
                far((2, 3), [window(jnp.clip(jnp.where(b < BIG, b - edge, 0), 0, rims - 1)) for b in seen_again])

    @pl.when(me == 3)
    def _():
        for k in range(CAP):
            came(k)
            hand(k).start()

    @pl.when(me > 1)
    def _():
        for k in range(CAP):
            hand(k).wait_recv()
        far((base, base + 1), [relayed(0), relayed(1)])

    if late > 4:
        @pl.when(me == 2)
        def _():
            for p in range(4, late):
                came(p)
                hand(p).start()
            for p in range(4, late):
                hand(p).wait_recv()
            at = [base + p for p in range(4, late)]
            far((at + [base + room])[:2], [relayed(p) for p in (4, late - 1)])

    @pl.when(me == 2)
    def _():
        came(2)
        put(relay.at[side, 2], late).start()
        hand(2).start()
        came(3)
        put_last(relay.at[side, 3])
        hand(3).start()

    @pl.when(me == 3)
    def _():
        for p in (2, 3):
            came(p)
            hand(p).start()

    @pl.when(me > 1)
    def _():
        for p in (2, 3):
            hand(p).wait_recv()
        far((base + 2, base + 3), [relayed(2), relayed(3)])

    def finish(h, low, m, total):
        for i in range(tall // BLK):
            part = total[i * BLK:(i + 1) * BLK]
            done[low // BLK + i, pl.ds(h, BLK, stride=heads), :] = part[:, :dh] / part[:, dh:]

    @pl.when(me > 0)
    def _():
        came(late)
        hand(late).start()
        for piece in range(min(2, pieces)):
            came(last, piece)
            hand(last, piece).start()
        hand(late).wait_recv()

        def one(piece, _):
            @pl.when(piece + 2 < pieces)
            def _():
                came(last, piece + 2)
                hand(last, piece + 2).start()

            hand(last, piece).wait_recv()
            far_head(piece, (base + late, base + last), [relayed(late), relayed(last)], finish)
            return 0

        lax.fori_loop(0, pieces, one, 0)

    @pl.when(me == 0)
    def _():
        def one(h, _):
            for low in range(0, toks, tall):
                finish(h, low, None, acc[h, pl.ds(low, tall), :])
            return 0

        lax.fori_loop(0, heads, one, 0)

    def pack(c, _):
        rows = pl.ds(pl.multiple_of(c * BLK, BLK), BLK)
        out[rows] = done[c].reshape(BLK, heads, dh).astype(jnp.bfloat16)
        return 0

    lax.fori_loop(0, own, pack, 0)
    swap.wait_send()

    @pl.when(has_next)
    def _():
        for j in range(2, WB):
            rim_copy(j).wait_send()
        for p in (0, 1, 2, 3, late):
            put(relay.at[side, p], p).wait_send()
        for piece in range(pieces):
            put(relay.at[side, last], last, piece).wait_send()

    @pl.when(me == 1)
    def _():
        for p in range(4, late):
            put(relay.at[side, p], p).wait_send()

    @pl.when(me > 0)
    def _():
        for j in range(1, WB):
            rim_pass(j).wait_send()
        hand(late).wait_send()
        for piece in range(pieces):
            hand(last, piece).wait_send()

    @pl.when(me > 1)
    def _():
        for p in range(4):
            hand(p).wait_send()

    @pl.when(me == 2)
    def _():
        for p in range(4, late):
            hand(p).wait_send()


def settle(src, out, sem):
    step = src.shape[0] // sem.shape[0]

    def move(i):
        at = pl.ds(i * step, step)
        return pltpu.make_async_copy(src.at[at], out.at[at], sem.at[i])

    for i in range(sem.shape[0]):
        move(i).start()
    for i in range(sem.shape[0]):
        move(i).wait()


def chained(spans, room, lists, counts, table, close_by, ready, queries, keys_values):
    toks, heads, dh = queries.shape
    own = toks // BLK
    rims = WB - 1
    bf16, f32 = jnp.bfloat16, jnp.float32
    hbm = pl.BlockSpec(memory_space=pl.ANY)
    vmem = pl.BlockSpec(memory_space=pltpu.VMEM)
    dma = pltpu.SemaphoreType.DMA
    pieces = heads
    ways = room - 1 + pieces
    return pl.pallas_call(
        functools.partial(relay_kernel, spans, room),
        out_shape=jax.ShapeDtypeStruct((toks, heads, dh), bf16),
        in_specs=[vmem, vmem, pl.BlockSpec(memory_space=pltpu.SMEM), hbm, hbm, hbm, hbm],
        out_specs=vmem,
        scratch_shapes=[
            pltpu.VMEM((toks, heads, dh), bf16),
            pltpu.VMEM((own, BLK, heads, dh), bf16),
            pltpu.VMEM((own, heads, BLK, dh), bf16),
            pltpu.VMEM((2, own, heads, BLK, dh), bf16),
            pltpu.VMEM((2, rims, heads, BLK, dh), bf16),
            pltpu.VMEM((2, room, heads, BLK, dh), bf16),
            pltpu.VMEM((room, heads, BLK, dh), bf16),
            pltpu.VMEM((heads, toks, dh), bf16),
            pltpu.VMEM((heads, toks, dh + LANES), f32),
            pltpu.VMEM((heads, toks, LANES), f32),
            pltpu.VMEM((2 * CAP + room + 1, own, 1, BLK), f32),
            pltpu.VMEM((2, BLK * heads, dh), f32),
            pltpu.VMEM((own, BLK * heads, dh), f32),
            dma((3,)), dma((2,)),
            dma((rims,)), dma((rims,)), dma((rims,)), dma((rims,)),
            dma((ways,)), dma((ways,)), dma((ways,)), dma((ways,)),
        ],
        compiler_params=pltpu.CompilerParams(
            collective_id=room, has_side_effects=True, vmem_limit_bytes=50 << 20),
    )(lists, counts, table, close_by, ready, queries, keys_values)


def local(spans, groups, queries, keys_values, far_list, far_count):
    toks, heads, members, dh = queries.shape
    own = toks // BLK
    if spans != CHAIN or groups != 2 or own < WB:
        return direct(spans, queries, keys_values, far_list, far_count)
    hbm = pl.BlockSpec(memory_space=pl.ANY)
    vmem = pl.BlockSpec(memory_space=pltpu.VMEM)
    smem = pl.BlockSpec(memory_space=pltpu.SMEM)
    dma = pltpu.SemaphoreType.DMA
    lists, counts = far_list.T, far_count.reshape(1, -1)
    rims, bf16 = WB - 1, jnp.bfloat16
    keys_values = keys_values.reshape(-1, own, BLK, heads, dh)
    table, choice, close_by, ready = pl.pallas_call(
        functools.partial(prelude, spans, own),
        out_shape=[
            jax.ShapeDtypeStruct((CAP * len(pair_names(spans)),), jnp.int32),
            jax.ShapeDtypeStruct((1,), jnp.int32),
            jax.ShapeDtypeStruct((heads, BLK, dh), bf16),
            jax.ShapeDtypeStruct((rims - 1, heads, BLK, dh), bf16),
        ],
        in_specs=[vmem, vmem, hbm],
        out_specs=[smem, smem, hbm, hbm],
        scratch_shapes=[
            pltpu.VMEM((rims, BLK, heads, dh), bf16),
            pltpu.VMEM((rims, BLK * heads, dh), jnp.float32),
            pltpu.VMEM((rims, heads, BLK, dh), bf16),
            pltpu.VMEM((8, LANES), jnp.int32), pltpu.VMEM((8, LANES), jnp.int32),
            dma((4,)), dma((2,)),
        ],
        compiler_params=pltpu.CompilerParams(collective_id=1, has_side_effects=True, vmem_limit_bytes=62 << 20),
    )(lists, counts, keys_values)
    args = (lists, counts, table, close_by, ready, queries.reshape(toks, heads, dh), keys_values)
    result = lax.switch(choice[0], [functools.partial(chained, spans, room) for room in (6, 7, 8)], *args)
    result = pl.pallas_call(
        settle,
        out_shape=jax.ShapeDtypeStruct(result.shape, result.dtype),
        in_specs=[vmem], out_specs=hbm,
        scratch_shapes=[dma((own,))],
        compiler_params=pltpu.CompilerParams(vmem_limit_bytes=16 << 20),
    )(result)
    return result.reshape(queries.shape)


def direct_kernel(
    spans, lists_in, counts, q_in, kv_in, out,
    q_raw, raw, mine, loc, rim_raw, rim, far, sendbuf, qh, acc, top, bias, scr, o_raw,
    in_sem, x_send, x_recv, rz_send, rz_recv, rf_send, rf_recv,
    fz_send, fz_recv, ff_send, ff_recv, out_sem,
):
    toks, heads, dh = q_in.shape
    own = toks // BLK
    me = lax.axis_index("ctx")
    side = lax.axis_index("rep")
    mate = {"rep": 1 - side}
    rims = WB - 1

    load_kv = pltpu.make_async_copy(kv_in.at[0], raw, in_sem.at[0])
    load_q = pltpu.make_async_copy(q_in, q_raw, in_sem.at[1])
    load_kv.start()
    load_q.start()

    barrier = pltpu.get_barrier_semaphore()
    pl.semaphore_signal(barrier, inc=1, device_id=mate)

    def greet(i, _):
        pl.semaphore_signal(barrier, inc=1, device_id={"ctx": lax.rem(me + i, spans)})
        return 0

    lax.fori_loop(1, spans, greet, 0)
    pl.semaphore_wait(barrier, spans)

    def raw_copy(to):
        return pltpu.make_async_remote_copy(
            src_ref=kv_in.at[0, own - 1], dst_ref=rim_raw.at[side],
            send_sem=rz_send.at[0], recv_sem=rz_recv.at[0], device_id={"ctx": to},
        )

    def raw_pass():
        return pltpu.make_async_remote_copy(
            src_ref=rim_raw.at[side], dst_ref=rim_raw.at[side],
            send_sem=rf_send.at[0], recv_sem=rf_recv.at[0], device_id=mate,
        )

    def rim_copy(j, to):
        return pltpu.make_async_remote_copy(
            src_ref=mine.at[own - j],
            dst_ref=rim.at[side, j - 1],
            send_sem=rz_send.at[j - 1], recv_sem=rz_recv.at[j - 1],
            device_id={"ctx": to},
        )

    def rim_pass(j):
        return pltpu.make_async_remote_copy(
            src_ref=rim.at[side, j - 1],
            dst_ref=rim.at[side, j - 1],
            send_sem=rf_send.at[j - 1], recv_sem=rf_recv.at[j - 1],
            device_id=mate,
        )

    def far_copy(to):
        return pltpu.make_async_remote_copy(
            src_ref=sendbuf.at[to], dst_ref=far.at[side, me],
            send_sem=fz_send.at[to], recv_sem=fz_recv.at[me],
            device_id={"ctx": to},
        )

    def far_arrival(src):
        return pltpu.make_async_remote_copy(
            src_ref=sendbuf.at[src], dst_ref=far.at[side, src],
            send_sem=fz_send.at[src], recv_sem=fz_recv.at[src],
            device_id={"ctx": src},
        )

    def far_pass(src):
        return pltpu.make_async_remote_copy(
            src_ref=far.at[side, src], dst_ref=far.at[side, src],
            send_sem=ff_send.at[src], recv_sem=ff_recv.at[src],
            device_id=mate,
        )

    ahead = lax.rem(me + 1, spans)
    has_next = me + 1 < spans

    @pl.when(has_next)
    def _():
        raw_copy(ahead).start()

    def spread(part, block, put):
        scr[part] = block.astype(jnp.float32).reshape(BLK * heads, dh)
        for h in range(heads):
            put(h, scr[part, pl.ds(h, BLK, stride=heads), :].astype(jnp.bfloat16))

    load_kv.wait()
    parts = scr.shape[0]

    def spread_mine(i, _):
        for part in range(parts):
            b = i * parts + part

            def put(h, x):
                mine[b, h] = x
                loc[side, b, h] = x

            spread(part, raw[b], put)
        return 0

    lax.fori_loop(0, own // parts, spread_mine, 0)

    swap = pltpu.make_async_remote_copy(
        src_ref=mine, dst_ref=loc.at[side],
        send_sem=x_send, recv_sem=x_recv, device_id=mate,
    )
    swap.start()

    big = jnp.int32(1 << 30)
    slot = lax.broadcasted_iota(jnp.int32, lists_in.shape, 0)
    block_of = lax.broadcasted_iota(jnp.int32, lists_in.shape, 1)
    listed = jnp.where(slot < counts[...], lists_in[...], -1)

    def slots(dst, src):
        inside = ((listed >= src * own) & (listed < src * own + own)
                  & (block_of >= dst * own) & (block_of < dst * own + own))
        first = jnp.min(jnp.where(inside, listed, big))
        second = jnp.min(jnp.where(inside & (listed > first), listed, big))
        return first, second

    def local_row(block):
        row = jnp.where(block < big, block - me * own, 0)
        return jnp.clip(row, 0, own - 1)

    def fill(i, _):
        to = spans - 1 - i
        found = slots(to, me)
        for k in range(CAP):
            sendbuf[to, k] = mine[local_row(found[k])]
        return 0

    later = spans - 1 - me
    lax.fori_loop(0, later, fill, 0)

    def push(i, _):
        far_copy(spans - 1 - i).start()
        return 0

    lax.fori_loop(0, later, push, 0)

    @pl.when(has_next)
    def _():
        for j in range(2, WB):
            rim_copy(j, ahead).start()

    ones = jnp.ones((BLK, LANES), jnp.bfloat16)

    def fill_bias(src, _):
        found = slots(me, src)
        for k in range(CAP):
            hit = jnp.max(jnp.where(listed == found[k], 1.0, 0.0), axis=0, keepdims=True)
            for c in range(own):
                mark = jnp.where(block_of[:1] == me * own + c, hit, 0.0)
                mark = jnp.max(mark, axis=1, keepdims=True)
                bias[src, c, :, k * BLK:(k + 1) * BLK] = jnp.broadcast_to(
                    jnp.where(mark > 0.5, 0.0, MASKED), (1, BLK))
        return 0

    lax.fori_loop(0, me + 1, fill_bias, 0)

    load_q.wait()

    def spread_q(i, _):
        for part in range(parts):
            at = pl.ds(pl.multiple_of((i * parts + part) * BLK, BLK), BLK)

            def put(h, x):
                qh[h, at, :] = x

            spread(part, q_raw[at], put)
        return 0

    lax.fori_loop(0, own // parts, spread_q, 0)
    swap.wait_recv()

    wide = min(WB, own)
    span = wide * BLK

    def near(c, _):
        rows = pl.ds(pl.multiple_of(c * BLK, BLK), BLK)
        low = jnp.maximum(c - (WB - 1), 0)
        keys = pl.ds(low, wide)
        key_pos = low * BLK + lax.broadcasted_iota(jnp.int32, (BLK, span), 1)
        query_pos = c * BLK + lax.broadcasted_iota(jnp.int32, (BLK, span), 0)
        seen = key_pos <= query_pos
        for h in range(heads):
            s = lax.dot_general(qh[h, rows, :], loc[0, keys, h].reshape(span, dh), NT,
                                preferred_element_type=jnp.float32) * SCALE
            s = jnp.where(seen, s, MASKED)
            m = jnp.max(s, axis=1, keepdims=True)
            p = jnp.exp2(s - m).astype(jnp.bfloat16)
            v = jnp.concatenate([loc[1, keys, h].reshape(span, dh)] + [jnp.ones((span, LANES), jnp.bfloat16)], axis=1)
            acc[h, rows, :] = jnp.dot(p, v, preferred_element_type=jnp.float32)
            top[h, rows, :] = jnp.broadcast_to(m, (BLK, LANES))
        return 0

    lax.fori_loop(0, own, near, 0)

    def merge(h, rows, k, v, row_bias):
        s = lax.dot_general(qh[h, rows, :], k, NT, preferred_element_type=jnp.float32) * SCALE
        s = s + row_bias
        old = top[h, rows, :]
        m = jnp.maximum(old, jnp.max(s, axis=1, keepdims=True))
        spread_m = jnp.concatenate([m] * (s.shape[1] // LANES), axis=1)
        p = jnp.exp2(s - spread_m).astype(jnp.bfloat16)
        a = jnp.exp2(old - m)
        acc[h, rows, :] = acc[h, rows, :] * jnp.concatenate([a, a], axis=1) + jnp.dot(
            p, v, preferred_element_type=jnp.float32)
        top[h, rows, :] = m

    def stack(get, h):
        k = jnp.concatenate([get(0, n, h) for n in range(CAP)], axis=0)
        v = jnp.concatenate(
            [jnp.concatenate([get(1, n, h), ones], axis=1) for n in range(CAP)], axis=0)
        return k, v

    def far_all(src, get):
        def one(c, _):
            rows = pl.ds(pl.multiple_of(c * BLK, BLK), BLK)
            row_bias = bias[src, c]
            for h in range(heads):
                merge(h, rows, *stack(get, h), row_bias)
            return 0

        lax.fori_loop(0, own, one, 0)

    found_mine = slots(me, me)
    at_mine = [local_row(b) for b in found_mine]
    far_all(me, lambda kind, k, h: loc[kind, at_mine[k], h])

    @pl.when(me > 0)
    def _():
        raw_copy(ahead).wait_recv()
        raw_pass().start()
        raw_pass().wait_recv()

        def put_k(h, x):
            rim[0, 0, h] = x

        def put_v(h, x):
            rim[1, 0, h] = x

        spread(0, rim_raw[0], put_k)
        spread(1, rim_raw[1], put_v)

    def far_step(src, _):
        far_arrival(src).wait_recv()
        far_pass(src).start()
        far_pass(src).wait_recv()
        far_all(src, lambda kind, k, h: far[kind, src, k, h])
        return 0

    lax.fori_loop(0, me, far_step, 0)

    def finish(c, _):
        rows = pl.ds(pl.multiple_of(c * BLK, BLK), BLK)
        part = lax.rem(c, parts)
        for h in range(heads):
            scr[part, pl.ds(h, BLK, stride=heads), :] = acc[h, rows, :dh] / acc[h, rows, dh:]
        o_raw[rows] = scr[part].reshape(BLK, heads, dh).astype(jnp.bfloat16)
        pltpu.make_async_copy(o_raw.at[rows], out.at[rows], out_sem.at[c]).start()
        return 0

    lane = lax.broadcasted_iota(jnp.int32, (1, CAP * BLK), 1)
    once = jnp.where(lane < BLK, 0.0, MASKED)

    def close(i, _):
        last = own - 1 - i
        j = WB - 1 - last

        @pl.when((me > 0) & (j > 1))
        def _():
            rim_copy(j, ahead).wait_recv()
            rim_pass(j).start()
            rim_pass(j).wait_recv()

        def one(c, _):
            rows = pl.ds(pl.multiple_of(c * BLK, BLK), BLK)
            for h in range(heads):
                merge(h, rows, *stack(lambda kind, n, h: rim[kind, j - 1, h], h), once)
            return 0

        @pl.when((me > 0) & (j > 0))
        def _():
            lax.fori_loop(0, last + 1, one, 0)

        return finish(last, 0)

    lax.fori_loop(0, own, close, 0)

    def drain(c, _):
        rows = pl.ds(pl.multiple_of(c * BLK, BLK), BLK)
        pltpu.make_async_copy(o_raw.at[rows], out.at[rows], out_sem.at[c]).wait()
        return 0

    lax.fori_loop(0, own, drain, 0)
    swap.wait_send()

    @pl.when(has_next)
    def _():
        raw_copy(ahead).wait_send()
        for j in range(2, WB):
            rim_copy(j, ahead).wait_send()

    @pl.when(me > 0)
    def _():
        raw_pass().wait_send()
        for j in range(2, WB):
            rim_pass(j).wait_send()

    def sent(i, _):
        far_copy(spans - 1 - i).wait_send()
        return 0

    lax.fori_loop(0, later, sent, 0)

    def passed(src, _):
        far_pass(src).wait_send()
        return 0

    lax.fori_loop(0, me, passed, 0)


def direct(spans, queries, keys_values, far_list, far_count):
    toks, heads, members, dh = queries.shape
    own = toks // BLK
    rims = WB - 1
    bf16, f32 = jnp.bfloat16, jnp.float32
    hbm = pl.BlockSpec(memory_space=pl.ANY)
    dma = pltpu.SemaphoreType.DMA
    result = pl.pallas_call(
        functools.partial(direct_kernel, spans),
        out_shape=jax.ShapeDtypeStruct((toks, heads, dh), bf16),
        in_specs=[pl.BlockSpec(memory_space=pltpu.VMEM)] * 2 + [hbm, hbm],
        out_specs=hbm,
        scratch_shapes=[
            pltpu.VMEM((toks, heads, dh), bf16),
            pltpu.VMEM((own, BLK, heads, dh), bf16),
            pltpu.VMEM((own, heads, BLK, dh), bf16),
            pltpu.VMEM((2, own, heads, BLK, dh), bf16),
            pltpu.VMEM((2, BLK, heads, dh), bf16),
            pltpu.VMEM((2, rims, heads, BLK, dh), bf16),
            pltpu.VMEM((2, spans, CAP, heads, BLK, dh), bf16),
            pltpu.VMEM((spans, CAP, heads, BLK, dh), bf16),
            pltpu.VMEM((heads, toks, dh), bf16),
            pltpu.VMEM((heads, toks, dh + LANES), f32),
            pltpu.VMEM((heads, toks, LANES), f32),
            pltpu.VMEM((spans, own, 1, CAP * BLK), f32),
            pltpu.VMEM((2, BLK * heads, dh), f32),
            pltpu.VMEM((toks, heads, dh), bf16),
            dma((2,)), dma, dma,
            dma((rims,)), dma((rims,)), dma((rims,)), dma((rims,)),
            dma((spans,)), dma((spans,)), dma((spans,)), dma((spans,)),
            dma((own,)),
        ],
        compiler_params=pltpu.CompilerParams(
            collective_id=0, has_side_effects=True, vmem_limit_bytes=62 << 20),
    )(far_list.T, far_count.reshape(1, -1), queries.reshape(toks, heads, dh), keys_values.reshape(-1, own, BLK, heads, dh))
    return result.reshape(queries.shape)


def solution(mesh):
    in_specs = (
        P(("groups", "ctx"), "head", "rep", None),
        P("rep", ("groups", "ctx"), "head", None),
        P("groups", None),
        P("groups"),
    )
    out_specs = P(("groups", "ctx"), "head", "rep", None)
    return jax.shard_map(
        functools.partial(local, mesh.shape["ctx"], mesh.shape["groups"]),
        mesh=mesh, in_specs=in_specs, out_specs=out_specs, check_vma=False)
```

```python
import functools
import math

import jax
import jax.numpy as jnp
from jax import lax
from jax.experimental import pallas as pl
from jax.experimental.pallas import tpu as pltpu
from jax.sharding import PartitionSpec as P

BLK = 128
WB = 4
FSEL = 16
CAP = 2

LANES = 128
MASKED = -1e30
SCALE = math.log2(math.e) / 12.0
NT = (((1,), (1,)), ((), ()))


CHAIN = 4
BIG = 1 << 30


def pair_names(spans):
    return [(dst, src) for dst in range(spans) for src in range(dst + 1)]


def where_of(spans, dst, src, k):
    return CAP * pair_names(spans).index((dst, src)) + k


def middle_plan(read, own):
    edge = 2 * own - (WB - 1)
    fresh, rank, blocks = [], [], []
    count = jnp.int32(0)
    for dst in (3, 2):
        for k in range(CAP):
            b = read(dst, 1, k)
            new = (b < BIG) & (b < edge)
            for other in blocks:
                new &= b != other
            fresh.append(new)
            rank.append(count)
            blocks.append(b)
            count = count + jnp.where(new, 1, 0)
    mine = []
    for a in range(2 * CAP):
        b = jnp.int32(BIG)
        for new, r, block in zip(fresh, rank, blocks):
            b = jnp.where(new & (r == a), block, b)
        mine.append(b)
    first = [read(3, 0, k) for k in range(CAP)]
    extra = []
    for k in range(CAP):
        b = read(2, 0, k)
        new = b < BIG
        for other in first:
            new &= b != other
        extra.append(jnp.where(new, b, BIG))
    need = CAP + count + sum(jnp.where(b < BIG, 1, 0) for b in extra)
    return mine, count, first, extra, need


def prelude(
    spans, own, lists_in, counts, kv_in, table, choice, close_by, ready,
    raw, scr, turned, share, theirs, sem, own_sem,
):
    rims, _, heads, dh = raw.shape
    me = lax.axis_index("ctx")
    peer = {"groups": 1 - lax.axis_index("groups")}
    has_next = me + 1 < spans
    load = pltpu.make_async_copy(kv_in.at[0, pl.ds(own - rims, rims)], raw, own_sem.at[0])
    load.start()
    barrier = pltpu.get_barrier_semaphore()
    pl.semaphore_signal(barrier, inc=1, device_id=peer)

    @pl.when(me > 0)
    def _():
        pl.semaphore_signal(barrier, inc=1, device_id={"ctx": lax.rem(me + spans - 1, spans)})

    load.wait()

    def turn(r):
        scr[r] = raw[r].astype(jnp.float32).reshape(BLK * heads, dh)
        for h in range(heads):
            turned[r, h] = scr[r, pl.ds(h, BLK, stride=heads), :].astype(jnp.bfloat16)

    turn(rims - 1)
    pl.semaphore_wait(barrier, jnp.where(has_next, 2, 1))
    send = pltpu.make_async_remote_copy(
        src_ref=turned.at[rims - 1], dst_ref=close_by, send_sem=sem.at[2], recv_sem=sem.at[3],
        device_id={"ctx": lax.rem(me + 1, spans)})

    @pl.when(has_next)
    def _():
        send.start()

    slot = lax.broadcasted_iota(jnp.int32, lists_in.shape, 0)
    block_of = lax.broadcasted_iota(jnp.int32, lists_in.shape, 1)
    listed = jnp.where(slot < counts[...], lists_in[...], -1)
    found = {}
    for dst, src in pair_names(spans):
        inside = ((listed >= src * own) & (listed < src * own + own)
                  & (block_of >= dst * own) & (block_of < dst * own + own))
        first = jnp.min(jnp.where(inside, listed, BIG))
        second = jnp.min(jnp.where(inside & (listed > first), listed, BIG))
        for k, b in enumerate((first, second)):
            found[dst, src, k] = b
            table[where_of(spans, dst, src, k)] = b
    need = middle_plan(lambda dst, src, k: found[dst, src, k], own)[-1]
    share[...] = jnp.broadcast_to(need, share.shape)
    swap = pltpu.make_async_remote_copy(
        src_ref=share, dst_ref=theirs, send_sem=sem.at[0], recv_sem=sem.at[1], device_id=peer)
    swap.start()
    for r in range(rims - 1):
        turn(r)
    keep = pltpu.make_async_copy(turned.at[pl.ds(0, rims - 1)], ready, own_sem.at[1])
    keep.start()
    swap.wait()
    most = jnp.max(jnp.maximum(share[...], theirs[...]))
    choice[0] = jnp.clip(most - 3 * CAP, 0, CAP)
    keep.wait()

    @pl.when(me > 0)
    def _():
        send.wait_recv()

    @pl.when(has_next)
    def _():
        send.wait_send()


def relay_kernel(
    spans, room, lists_in, counts, table, close_by, ready, q_in, kv_in, out,
    q_raw, raw, mine, loc, rim, relay, sendbuf, qh, acc, top, bias, scr, done,
    in_sem, x_sem, rz_send, rz_recv, rf_send, rf_recv,
    z_send, z_recv, f_send, f_recv,
):
    toks, heads, dh = q_in.shape
    own = toks // BLK
    me = lax.axis_index("ctx")
    side = lax.axis_index("rep")
    mate = {"rep": 1 - side}
    rims = WB - 1
    pieces = f_send.shape[0] - room + 1
    part_heads = heads // pieces
    has_next = me + 1 < spans
    ahead = {"ctx": lax.rem(me + 1, spans)}
    late, last = room - 2, room - 1

    load_kv = pltpu.make_async_copy(kv_in.at[0], raw, in_sem.at[0])
    load_q = pltpu.make_async_copy(q_in, q_raw, in_sem.at[1])
    load_rim = pltpu.make_async_copy(close_by, rim.at[side, rims - 1], in_sem.at[2])
    barrier = pltpu.get_barrier_semaphore()
    pl.semaphore_signal(barrier, inc=1, device_id=mate)

    @pl.when(me > 0)
    def _():
        pl.semaphore_signal(barrier, inc=1, device_id={"ctx": lax.rem(me + spans - 1, spans)})

    def rim_copy(j):
        return pltpu.make_async_remote_copy(
            src_ref=ready.at[rims - j], dst_ref=rim.at[side, rims - j],
            send_sem=rz_send.at[j - 1], recv_sem=rz_recv.at[j - 1], device_id=ahead)

    def rim_pass(j):
        return pltpu.make_async_remote_copy(
            src_ref=rim.at[side, rims - j], dst_ref=rim.at[side, rims - j],
            send_sem=rf_send.at[j - 1], recv_sem=rf_recv.at[j - 1], device_id=mate)

    def cut(ref, piece):
        return ref if piece is None else ref.at[pl.ds(piece * part_heads, part_heads)]

    def put(src, p, piece=None):
        at = p if piece is None else p + piece
        return pltpu.make_async_remote_copy(
            src_ref=cut(src, piece), dst_ref=cut(relay.at[side, p], piece),
            send_sem=z_send.at[at], recv_sem=z_recv.at[at], device_id=ahead)

    def came(p, piece=None):
        put(relay.at[side, p], p, piece).wait_recv()

    def hand(p, piece=None):
        at = p if piece is None else p + piece
        return pltpu.make_async_remote_copy(
            src_ref=cut(relay.at[side, p], piece), dst_ref=cut(relay.at[side, p], piece),
            send_sem=f_send.at[at], recv_sem=f_recv.at[at], device_id=mate)

    def put_last(src):
        for piece in range(pieces):
            put(src, last, piece).start()

    parts = scr.shape[0]

    def spread(part, block, store):
        scr[part] = block.astype(jnp.float32).reshape(BLK * heads, dh)
        for h in range(heads):
            store(h, scr[part, pl.ds(h, BLK, stride=heads), :].astype(jnp.bfloat16))

    def spread_mine(b, part):
        def store(h, x):
            mine[b, h] = x
            loc[side, b, h] = x

        spread(part, raw[b], store)

    pl.semaphore_wait(barrier, jnp.where(has_next, 2, 1))

    @pl.when(has_next)
    def _():
        for j in range(2, WB):
            rim_copy(j).start()

    load_kv.start()

    @pl.when(me > 0)
    def _():
        load_rim.start()

    load_q.start()
    load_kv.wait()

    def spread_all(b, _):
        spread_mine(b, lax.rem(b, parts))
        return 0

    lax.fori_loop(0, own, spread_all, 0)

    swap = pltpu.make_async_remote_copy(
        src_ref=mine, dst_ref=loc.at[side],
        send_sem=x_sem.at[0], recv_sem=x_sem.at[1], device_id=mate)
    swap.start()

    def read(dst, src, k):
        return table[where_of(spans, dst, src, k)]

    def local_row(block):
        return jnp.clip(jnp.where(block < BIG, block - me * own, 0), 0, own - 1)

    def fill(p, block):
        sendbuf[p] = mine[local_row(block)]

    own_list, own_count, first, extra, _ = middle_plan(read, own)
    own_late, own_last = late - 2, last - 2

    @pl.when(me == 0)
    def _():
        for p, (dst, k) in zip((0, 1, 2, 3, late, last), ((3, 0), (3, 1), (2, 0), (2, 1), (1, 0), (1, 1))):
            fill(p, read(dst, 0, k))
        for p in (0, 1, 2, 3, late):
            put(sendbuf.at[p], p).start()
        put_last(sendbuf.at[last])

    early = [0, 1] + list(range(4, late))

    @pl.when(me == 1)
    def _():
        for p in early:
            fill(p, own_list[p if p < 2 else p - 2])
        for p in early:
            put(sendbuf.at[p], p).start()

    @pl.when(me == 2)
    def _():
        for k in range(CAP):
            fill(k, read(3, 2, k))
        for k in range(CAP):
            put(sendbuf.at[k], k).start()

    @pl.when(me == 0)
    def _():
        for j in range(rims):
            rim[:, j] = jnp.zeros((2,) + rim.shape[2:], rim.dtype)

    held = [0] * room
    for k in range(CAP):
        held[k] = jnp.where(me == 3, read(3, 2, k), own_list[k])
        held[2 + k] = jnp.where(me == 3, read(3, 1, k), first[k])
    for p in range(4, late):
        held[p] = jnp.where(me == 2, own_list[p - 2], BIG)
    both = (extra[0] < BIG) & (extra[1] < BIG)
    mid_late = jnp.where(both, extra[0], BIG)
    mid_last = jnp.where(extra[1] < BIG, extra[1], extra[0])
    if own_late < 2 * CAP:
        mid_late = jnp.where(own_count > own_late, own_list[own_late], mid_late)
    if own_last < 2 * CAP:
        mid_last = jnp.where(own_count > own_last, own_list[own_last], mid_last)
    held[late] = jnp.where(me == 3, read(3, 0, 0), jnp.where(me == 2, mid_late, read(1, 0, 0)))
    held[last] = jnp.where(me == 3, read(3, 0, 1), jnp.where(me == 2, mid_last, read(1, 0, 1)))
    edge = 2 * own - rims
    seen_again = []
    for k in range(CAP):
        b = read(2, 1, k)
        seen_again.append(jnp.where((b < BIG) & (b >= edge) & (me == 2), b, BIG))
    mine_far = []
    for k in range(CAP):
        b = read(0, 0, k)
        for s in range(1, spans):
            b = jnp.where(me == s, read(s, s, k), b)
        mine_far.append(b)

    slot = lax.broadcasted_iota(jnp.int32, lists_in.shape, 0)
    block_of = lax.broadcasted_iota(jnp.int32, lists_in.shape, 1)
    listed = jnp.where(slot < counts[...], lists_in[...], -1)

    for n, block in enumerate(mine_far + seen_again + held + [jnp.int32(BIG)]):
        hit = jnp.max(jnp.where(listed == block, 1.0, 0.0), axis=0, keepdims=True)
        for c in range(own):
            mark = jnp.where(block_of[:1] == me * own + c, hit, 0.0)
            mark = jnp.max(mark, axis=1, keepdims=True)
            bias[n, c] = jnp.broadcast_to(jnp.where(mark > 0.5, 0.0, MASKED), (1, BLK))

    load_q.wait()

    def spread_q(c, _):
        at = pl.ds(pl.multiple_of(c * BLK, BLK), BLK)

        def store(h, x):
            qh[h, at, :] = x

        spread(lax.rem(c, parts), q_raw[at], store)
        return 0

    lax.fori_loop(0, own, spread_q, 0)
    swap.wait_recv()

    span = WB * BLK

    def near_block(c, rows, get):
        key_pos = lax.broadcasted_iota(jnp.int32, (BLK, span), 1) - rims * BLK
        query_pos = lax.broadcasted_iota(jnp.int32, (BLK, span), 0)
        seen = key_pos <= query_pos
        if isinstance(c, int):
            seen &= (key_pos + c * BLK >= 0) | (me > 0)
        for h in range(heads):
            s = lax.dot_general(qh[h, rows, :], get(0, h), NT,
                                preferred_element_type=jnp.float32) * SCALE
            s = jnp.where(seen, s, MASKED)
            m = jnp.max(s, axis=1, keepdims=True)
            p = jnp.exp2(s - m).astype(jnp.bfloat16)
            v = jnp.concatenate([get(1, h), jnp.ones((span, LANES), jnp.bfloat16)], axis=1)
            acc[h, rows, :] = jnp.dot(p, v, preferred_element_type=jnp.float32)
            top[h, rows, :] = jnp.broadcast_to(m, (BLK, LANES))

    def near(c, _):
        keys = pl.ds(c - rims, WB)
        near_block(c, pl.ds(pl.multiple_of(c * BLK, BLK), BLK), lambda kind, h: loc[kind, keys, h].reshape(span, dh))
        return 0

    lax.fori_loop(rims, own, near, 0)

    ones = jnp.ones((BLK, LANES), jnp.bfloat16)

    tall = 4 * BLK

    def merged(h, rows, k, v, row_bias):
        s = lax.dot_general(qh[h, rows, :], k, NT, preferred_element_type=jnp.float32) * SCALE
        s = s + row_bias
        old = top[h, rows, :]
        m = jnp.maximum(old, jnp.max(s, axis=1, keepdims=True))
        spread_m = jnp.concatenate([m] * (s.shape[1] // LANES), axis=1)
        p = jnp.exp2(s - spread_m).astype(jnp.bfloat16)
        a = jnp.exp2(old - m)
        return m, acc[h, rows, :] * jnp.concatenate([a, a], axis=1) + jnp.dot(
            p, v, preferred_element_type=jnp.float32)

    def far_head(h, at, gets, keep, begin=0):
        k = jnp.concatenate([get(0, h) for get in gets], axis=0)
        v = jnp.concatenate([jnp.concatenate([get(1, h), ones], axis=1) for get in gets], axis=0)
        for low in range(begin, toks, tall):
            row_bias = jnp.concatenate([
                jnp.concatenate([jnp.broadcast_to(bias[n, low // BLK + i], (BLK, BLK)) for n in at], axis=1)
                for i in range(tall // BLK)], axis=0)
            rows = pl.ds(low, tall)
            keep(h, low, *merged(h, rows, k, v, row_bias))

    def far(at, gets, begin=0):
        def hold(h, low, m, total):
            acc[h, pl.ds(low, tall), :] = total
            top[h, pl.ds(low, tall), :] = m

        def one(h, _):
            far_head(h, at, gets, hold, begin)
            return 0

        lax.fori_loop(0, heads, one, 0)

    def relayed(p):
        return lambda kind, h: relay[kind, p, h]

    def owned(row):
        return lambda kind, h: loc[kind, row, h]

    def window(row):
        return lambda kind, h: rim[kind, row, h]

    far((0, 1), [owned(local_row(b)) for b in mine_far], WB * BLK // tall * tall)

    @pl.when(me > 0)
    def _():
        load_rim.wait()
        rim_pass(1).start()
        for j in range(2, WB):
            rim_copy(j).wait_recv()
            rim_pass(j).start()
        for j in range(1, WB):
            rim_pass(j).wait_recv()

    for c in range(rims):
        near_block(c, pl.ds(c * BLK, BLK), lambda kind, h: jnp.concatenate(
            [rim[kind, r, h] for r in range(c, rims)] + [loc[kind, b, h] for b in range(c + 1)], axis=0))

    base = 2 * CAP

    @pl.when(me == 1)
    def _():
        for k in range(CAP):
            came(k)
            put(relay.at[side, k], 2 + k).start()
        came(2)
        if own_late < 2 * CAP:
            sendbuf[late] = jnp.where(own_count > own_late, mine[local_row(own_list[own_late])], relay[side, 2])
            put(sendbuf.at[late], late).start()
        else:
            put(relay.at[side, 2], late).start()
        came(3)
        tail = jnp.where(extra[1] < BIG, relay[side, 3], relay[side, 2])
        if own_last < 2 * CAP:
            tail = jnp.where(own_count > own_last, mine[local_row(own_list[own_last])], tail)
        sendbuf[last] = tail
        put_last(sendbuf.at[last])

    @pl.when(me == 2)
    def _():
        for k in range(CAP):
            came(k)
            hand(k).start()
            b = read(3, 1, k)
            pick = relay[side, 0]
            if k == 1:
                pick = jnp.where(b == own_list[1], relay[side, 1], pick)
            for j in range(1, WB):
                pick = jnp.where(b == 2 * own - j, rim[side, rims - j], pick)
            sendbuf[2 + k] = pick
            put(sendbuf.at[2 + k], 2 + k).start()
            if k == 0:
                far((2, 3), [window(jnp.clip(jnp.where(b < BIG, b - edge, 0), 0, rims - 1)) for b in seen_again])

    @pl.when(me == 3)
    def _():
        for k in range(CAP):
            came(k)
            hand(k).start()

    @pl.when(me > 1)
    def _():
        for k in range(CAP):
            hand(k).wait_recv()
        far((base, base + 1), [relayed(0), relayed(1)])

    if late > 4:
        @pl.when(me == 2)
        def _():
            for p in range(4, late):
                came(p)
                hand(p).start()
            for p in range(4, late):
                hand(p).wait_recv()
            at = [base + p for p in range(4, late)]
            far((at + [base + room])[:2], [relayed(p) for p in (4, late - 1)])

    @pl.when(me == 2)
    def _():
        came(2)
        put(relay.at[side, 2], late).start()
        hand(2).start()
        came(3)
        put_last(relay.at[side, 3])
        hand(3).start()

    @pl.when(me == 3)
    def _():
        for p in (2, 3):
            came(p)
            hand(p).start()

    @pl.when(me > 1)
    def _():
        for p in (2, 3):
            hand(p).wait_recv()
        far((base + 2, base + 3), [relayed(2), relayed(3)])

    def finish(h, low, m, total):
        for i in range(tall // BLK):
            part = total[i * BLK:(i + 1) * BLK]
            done[low // BLK + i, pl.ds(h, BLK, stride=heads), :] = part[:, :dh] / part[:, dh:]

    @pl.when(me > 0)
    def _():
        came(late)
        hand(late).start()
        for piece in range(min(2, pieces)):
            came(last, piece)
            hand(last, piece).start()
        hand(late).wait_recv()

        def one(piece, _):
            @pl.when(piece + 2 < pieces)
            def _():
                came(last, piece + 2)
                hand(last, piece + 2).start()

            hand(last, piece).wait_recv()
            far_head(piece, (base + late, base + last), [relayed(late), relayed(last)], finish)
            return 0

        lax.fori_loop(0, pieces, one, 0)

    @pl.when(me == 0)
    def _():
        def one(h, _):
            for low in range(0, toks, tall):
                finish(h, low, None, acc[h, pl.ds(low, tall), :])
            return 0

        lax.fori_loop(0, heads, one, 0)

    def pack(c, _):
        rows = pl.ds(pl.multiple_of(c * BLK, BLK), BLK)
        out[rows] = done[c].reshape(BLK, heads, dh).astype(jnp.bfloat16)
        return 0

    lax.fori_loop(0, own, pack, 0)
    swap.wait_send()

    @pl.when(has_next)
    def _():
        for j in range(2, WB):
            rim_copy(j).wait_send()
        for p in (0, 1, 2, 3, late):
            put(relay.at[side, p], p).wait_send()
        for piece in range(pieces):
            put(relay.at[side, last], last, piece).wait_send()

    @pl.when(me == 1)
    def _():
        for p in range(4, late):
            put(relay.at[side, p], p).wait_send()

    @pl.when(me > 0)
    def _():
        for j in range(1, WB):
            rim_pass(j).wait_send()
        hand(late).wait_send()
        for piece in range(pieces):
            hand(last, piece).wait_send()

    @pl.when(me > 1)
    def _():
        for p in range(4):
            hand(p).wait_send()

    @pl.when(me == 2)
    def _():
        for p in range(4, late):
            hand(p).wait_send()


def settle(src, out, sem):
    step = src.shape[0] // sem.shape[0]

    def move(i):
        at = pl.ds(i * step, step)
        return pltpu.make_async_copy(src.at[at], out.at[at], sem.at[i])

    for i in range(sem.shape[0]):
        move(i).start()
    for i in range(sem.shape[0]):
        move(i).wait()


def chained(spans, room, lists, counts, table, close_by, ready, queries, keys_values):
    toks, heads, dh = queries.shape
    own = toks // BLK
    rims = WB - 1
    bf16, f32 = jnp.bfloat16, jnp.float32
    hbm = pl.BlockSpec(memory_space=pl.ANY)
    vmem = pl.BlockSpec(memory_space=pltpu.VMEM)
    dma = pltpu.SemaphoreType.DMA
    pieces = heads
    ways = room - 1 + pieces
    return pl.pallas_call(
        functools.partial(relay_kernel, spans, room),
        out_shape=jax.ShapeDtypeStruct((toks, heads, dh), bf16),
        in_specs=[vmem, vmem, pl.BlockSpec(memory_space=pltpu.SMEM), hbm, hbm, hbm, hbm],
        out_specs=vmem,
        scratch_shapes=[
            pltpu.VMEM((toks, heads, dh), bf16),
            pltpu.VMEM((own, BLK, heads, dh), bf16),
            pltpu.VMEM((own, heads, BLK, dh), bf16),
            pltpu.VMEM((2, own, heads, BLK, dh), bf16),
            pltpu.VMEM((2, rims, heads, BLK, dh), bf16),
            pltpu.VMEM((2, room, heads, BLK, dh), bf16),
            pltpu.VMEM((room, heads, BLK, dh), bf16),
            pltpu.VMEM((heads, toks, dh), bf16),
            pltpu.VMEM((heads, toks, dh + LANES), f32),
            pltpu.VMEM((heads, toks, LANES), f32),
            pltpu.VMEM((2 * CAP + room + 1, own, 1, BLK), f32),
            pltpu.VMEM((2, BLK * heads, dh), f32),
            pltpu.VMEM((own, BLK * heads, dh), f32),
            dma((3,)), dma((2,)),
            dma((rims,)), dma((rims,)), dma((rims,)), dma((rims,)),
            dma((ways,)), dma((ways,)), dma((ways,)), dma((ways,)),
        ],
        compiler_params=pltpu.CompilerParams(
            collective_id=room, has_side_effects=True, vmem_limit_bytes=50 << 20),
    )(lists, counts, table, close_by, ready, queries, keys_values)


def local(spans, groups, queries, keys_values, far_list, far_count):
    toks, heads, members, dh = queries.shape
    own = toks // BLK
    if spans != CHAIN or groups != 2 or own < WB:
        return direct(spans, queries, keys_values, far_list, far_count)
    hbm = pl.BlockSpec(memory_space=pl.ANY)
    vmem = pl.BlockSpec(memory_space=pltpu.VMEM)
    smem = pl.BlockSpec(memory_space=pltpu.SMEM)
    dma = pltpu.SemaphoreType.DMA
    lists, counts = far_list.T, far_count.reshape(1, -1)
    rims, bf16 = WB - 1, jnp.bfloat16
    keys_values = keys_values.reshape(-1, own, BLK, heads, dh)
    table, choice, close_by, ready = pl.pallas_call(
        functools.partial(prelude, spans, own),
        out_shape=[
            jax.ShapeDtypeStruct((CAP * len(pair_names(spans)),), jnp.int32),
            jax.ShapeDtypeStruct((1,), jnp.int32),
            jax.ShapeDtypeStruct((heads, BLK, dh), bf16),
            jax.ShapeDtypeStruct((rims - 1, heads, BLK, dh), bf16),
        ],
        in_specs=[vmem, vmem, hbm],
        out_specs=[smem, smem, hbm, hbm],
        scratch_shapes=[
            pltpu.VMEM((rims, BLK, heads, dh), bf16),
            pltpu.VMEM((rims, BLK * heads, dh), jnp.float32),
            pltpu.VMEM((rims, heads, BLK, dh), bf16),
            pltpu.VMEM((8, LANES), jnp.int32), pltpu.VMEM((8, LANES), jnp.int32),
            dma((4,)), dma((2,)),
        ],
        compiler_params=pltpu.CompilerParams(collective_id=1, has_side_effects=True, vmem_limit_bytes=62 << 20),
    )(lists, counts, keys_values)
    args = (lists, counts, table, close_by, ready, queries.reshape(toks, heads, dh), keys_values)
    result = lax.switch(choice[0], [functools.partial(chained, spans, room) for room in (6, 7, 8)], *args)
    result = pl.pallas_call(
        settle,
        out_shape=jax.ShapeDtypeStruct(result.shape, result.dtype),
        in_specs=[vmem], out_specs=hbm,
        scratch_shapes=[dma((own,))],
        compiler_params=pltpu.CompilerParams(vmem_limit_bytes=16 << 20),
    )(result)
    return result.reshape(queries.shape)


def direct_kernel(
    spans, lists_in, counts, q_in, kv_in, out,
    q_raw, raw, mine, loc, rim_raw, rim, far, sendbuf, qh, acc, top, bias, scr, o_raw,
    in_sem, x_send, x_recv, rz_send, rz_recv, rf_send, rf_recv,
    fz_send, fz_recv, ff_send, ff_recv, out_sem,
):
    toks, heads, dh = q_in.shape
    own = toks // BLK
    me = lax.axis_index("ctx")
    side = lax.axis_index("rep")
    mate = {"rep": 1 - side}
    rims = WB - 1

    load_kv = pltpu.make_async_copy(kv_in.at[0], raw, in_sem.at[0])
    load_q = pltpu.make_async_copy(q_in, q_raw, in_sem.at[1])
    load_kv.start()
    load_q.start()

    barrier = pltpu.get_barrier_semaphore()
    pl.semaphore_signal(barrier, inc=1, device_id=mate)

    def greet(i, _):
        pl.semaphore_signal(barrier, inc=1, device_id={"ctx": lax.rem(me + i, spans)})
        return 0

    lax.fori_loop(1, spans, greet, 0)
    pl.semaphore_wait(barrier, spans)

    def raw_copy(to):
        return pltpu.make_async_remote_copy(
            src_ref=kv_in.at[0, own - 1], dst_ref=rim_raw.at[side],
            send_sem=rz_send.at[0], recv_sem=rz_recv.at[0], device_id={"ctx": to},
        )

    def raw_pass():
        return pltpu.make_async_remote_copy(
            src_ref=rim_raw.at[side], dst_ref=rim_raw.at[side],
            send_sem=rf_send.at[0], recv_sem=rf_recv.at[0], device_id=mate,
        )

    def rim_copy(j, to):
        return pltpu.make_async_remote_copy(
            src_ref=mine.at[own - j],
            dst_ref=rim.at[side, j - 1],
            send_sem=rz_send.at[j - 1], recv_sem=rz_recv.at[j - 1],
            device_id={"ctx": to},
        )

    def rim_pass(j):
        return pltpu.make_async_remote_copy(
            src_ref=rim.at[side, j - 1],
            dst_ref=rim.at[side, j - 1],
            send_sem=rf_send.at[j - 1], recv_sem=rf_recv.at[j - 1],
            device_id=mate,
        )

    def far_copy(to):
        return pltpu.make_async_remote_copy(
            src_ref=sendbuf.at[to], dst_ref=far.at[side, me],
            send_sem=fz_send.at[to], recv_sem=fz_recv.at[me],
            device_id={"ctx": to},
        )

    def far_arrival(src):
        return pltpu.make_async_remote_copy(
            src_ref=sendbuf.at[src], dst_ref=far.at[side, src],
            send_sem=fz_send.at[src], recv_sem=fz_recv.at[src],
            device_id={"ctx": src},
        )

    def far_pass(src):
        return pltpu.make_async_remote_copy(
            src_ref=far.at[side, src], dst_ref=far.at[side, src],
            send_sem=ff_send.at[src], recv_sem=ff_recv.at[src],
            device_id=mate,
        )

    ahead = lax.rem(me + 1, spans)
    has_next = me + 1 < spans

    @pl.when(has_next)
    def _():
        raw_copy(ahead).start()

    def spread(part, block, put):
        scr[part] = block.astype(jnp.float32).reshape(BLK * heads, dh)
        for h in range(heads):
            put(h, scr[part, pl.ds(h, BLK, stride=heads), :].astype(jnp.bfloat16))

    load_kv.wait()
    parts = scr.shape[0]

    def spread_mine(i, _):
        for part in range(parts):
            b = i * parts + part

            def put(h, x):
                mine[b, h] = x
                loc[side, b, h] = x

            spread(part, raw[b], put)
        return 0

    lax.fori_loop(0, own // parts, spread_mine, 0)

    swap = pltpu.make_async_remote_copy(
        src_ref=mine, dst_ref=loc.at[side],
        send_sem=x_send, recv_sem=x_recv, device_id=mate,
    )
    swap.start()

    big = jnp.int32(1 << 30)
    slot = lax.broadcasted_iota(jnp.int32, lists_in.shape, 0)
    block_of = lax.broadcasted_iota(jnp.int32, lists_in.shape, 1)
    listed = jnp.where(slot < counts[...], lists_in[...], -1)

    def slots(dst, src):
        inside = ((listed >= src * own) & (listed < src * own + own)
                  & (block_of >= dst * own) & (block_of < dst * own + own))
        first = jnp.min(jnp.where(inside, listed, big))
        second = jnp.min(jnp.where(inside & (listed > first), listed, big))
        return first, second

    def local_row(block):
        row = jnp.where(block < big, block - me * own, 0)
        return jnp.clip(row, 0, own - 1)

    def fill(i, _):
        to = spans - 1 - i
        found = slots(to, me)
        for k in range(CAP):
            sendbuf[to, k] = mine[local_row(found[k])]
        return 0

    later = spans - 1 - me
    lax.fori_loop(0, later, fill, 0)

    def push(i, _):
        far_copy(spans - 1 - i).start()
        return 0

    lax.fori_loop(0, later, push, 0)

    @pl.when(has_next)
    def _():
        for j in range(2, WB):
            rim_copy(j, ahead).start()

    ones = jnp.ones((BLK, LANES), jnp.bfloat16)

    def fill_bias(src, _):
        found = slots(me, src)
        for k in range(CAP):
            hit = jnp.max(jnp.where(listed == found[k], 1.0, 0.0), axis=0, keepdims=True)
            for c in range(own):
                mark = jnp.where(block_of[:1] == me * own + c, hit, 0.0)
                mark = jnp.max(mark, axis=1, keepdims=True)
                bias[src, c, :, k * BLK:(k + 1) * BLK] = jnp.broadcast_to(
                    jnp.where(mark > 0.5, 0.0, MASKED), (1, BLK))
        return 0

    lax.fori_loop(0, me + 1, fill_bias, 0)

    load_q.wait()

    def spread_q(i, _):
        for part in range(parts):
            at = pl.ds(pl.multiple_of((i * parts + part) * BLK, BLK), BLK)

            def put(h, x):
                qh[h, at, :] = x

            spread(part, q_raw[at], put)
        return 0

    lax.fori_loop(0, own // parts, spread_q, 0)
    swap.wait_recv()

    wide = min(WB, own)
    span = wide * BLK

    def near(c, _):
        rows = pl.ds(pl.multiple_of(c * BLK, BLK), BLK)
        low = jnp.maximum(c - (WB - 1), 0)
        keys = pl.ds(low, wide)
        key_pos = low * BLK + lax.broadcasted_iota(jnp.int32, (BLK, span), 1)
        query_pos = c * BLK + lax.broadcasted_iota(jnp.int32, (BLK, span), 0)
        seen = key_pos <= query_pos
        for h in range(heads):
            s = lax.dot_general(qh[h, rows, :], loc[0, keys, h].reshape(span, dh), NT,
                                preferred_element_type=jnp.float32) * SCALE
            s = jnp.where(seen, s, MASKED)
            m = jnp.max(s, axis=1, keepdims=True)
            p = jnp.exp2(s - m).astype(jnp.bfloat16)
            v = jnp.concatenate([loc[1, keys, h].reshape(span, dh)] + [jnp.ones((span, LANES), jnp.bfloat16)], axis=1)
            acc[h, rows, :] = jnp.dot(p, v, preferred_element_type=jnp.float32)
            top[h, rows, :] = jnp.broadcast_to(m, (BLK, LANES))
        return 0

    lax.fori_loop(0, own, near, 0)

    def merge(h, rows, k, v, row_bias):
        s = lax.dot_general(qh[h, rows, :], k, NT, preferred_element_type=jnp.float32) * SCALE
        s = s + row_bias
        old = top[h, rows, :]
        m = jnp.maximum(old, jnp.max(s, axis=1, keepdims=True))
        spread_m = jnp.concatenate([m] * (s.shape[1] // LANES), axis=1)
        p = jnp.exp2(s - spread_m).astype(jnp.bfloat16)
        a = jnp.exp2(old - m)
        acc[h, rows, :] = acc[h, rows, :] * jnp.concatenate([a, a], axis=1) + jnp.dot(
            p, v, preferred_element_type=jnp.float32)
        top[h, rows, :] = m

    def stack(get, h):
        k = jnp.concatenate([get(0, n, h) for n in range(CAP)], axis=0)
        v = jnp.concatenate(
            [jnp.concatenate([get(1, n, h), ones], axis=1) for n in range(CAP)], axis=0)
        return k, v

    def far_all(src, get):
        def one(c, _):
            rows = pl.ds(pl.multiple_of(c * BLK, BLK), BLK)
            row_bias = bias[src, c]
            for h in range(heads):
                merge(h, rows, *stack(get, h), row_bias)
            return 0

        lax.fori_loop(0, own, one, 0)

    found_mine = slots(me, me)
    at_mine = [local_row(b) for b in found_mine]
    far_all(me, lambda kind, k, h: loc[kind, at_mine[k], h])

    @pl.when(me > 0)
    def _():
        raw_copy(ahead).wait_recv()
        raw_pass().start()
        raw_pass().wait_recv()

        def put_k(h, x):
            rim[0, 0, h] = x

        def put_v(h, x):
            rim[1, 0, h] = x

        spread(0, rim_raw[0], put_k)
        spread(1, rim_raw[1], put_v)

    def far_step(src, _):
        far_arrival(src).wait_recv()
        far_pass(src).start()
        far_pass(src).wait_recv()
        far_all(src, lambda kind, k, h: far[kind, src, k, h])
        return 0

    lax.fori_loop(0, me, far_step, 0)

    def finish(c, _):
        rows = pl.ds(pl.multiple_of(c * BLK, BLK), BLK)
        part = lax.rem(c, parts)
        for h in range(heads):
            scr[part, pl.ds(h, BLK, stride=heads), :] = acc[h, rows, :dh] / acc[h, rows, dh:]
        o_raw[rows] = scr[part].reshape(BLK, heads, dh).astype(jnp.bfloat16)
        pltpu.make_async_copy(o_raw.at[rows], out.at[rows], out_sem.at[c]).start()
        return 0

    lane = lax.broadcasted_iota(jnp.int32, (1, CAP * BLK), 1)
    once = jnp.where(lane < BLK, 0.0, MASKED)

    def close(i, _):
        last = own - 1 - i
        j = WB - 1 - last

        @pl.when((me > 0) & (j > 1))
        def _():
            rim_copy(j, ahead).wait_recv()
            rim_pass(j).start()
            rim_pass(j).wait_recv()

        def one(c, _):
            rows = pl.ds(pl.multiple_of(c * BLK, BLK), BLK)
            for h in range(heads):
                merge(h, rows, *stack(lambda kind, n, h: rim[kind, j - 1, h], h), once)
            return 0

        @pl.when((me > 0) & (j > 0))
        def _():
            lax.fori_loop(0, last + 1, one, 0)

        return finish(last, 0)

    lax.fori_loop(0, own, close, 0)

    def drain(c, _):
        rows = pl.ds(pl.multiple_of(c * BLK, BLK), BLK)
        pltpu.make_async_copy(o_raw.at[rows], out.at[rows], out_sem.at[c]).wait()
        return 0

    lax.fori_loop(0, own, drain, 0)
    swap.wait_send()

    @pl.when(has_next)
    def _():
        raw_copy(ahead).wait_send()
        for j in range(2, WB):
            rim_copy(j, ahead).wait_send()

    @pl.when(me > 0)
    def _():
        raw_pass().wait_send()
        for j in range(2, WB):
            rim_pass(j).wait_send()

    def sent(i, _):
        far_copy(spans - 1 - i).wait_send()
        return 0

    lax.fori_loop(0, later, sent, 0)

    def passed(src, _):
        far_pass(src).wait_send()
        return 0

    lax.fori_loop(0, me, passed, 0)


def direct(spans, queries, keys_values, far_list, far_count):
    toks, heads, members, dh = queries.shape
    own = toks // BLK
    rims = WB - 1
    bf16, f32 = jnp.bfloat16, jnp.float32
    hbm = pl.BlockSpec(memory_space=pl.ANY)
    dma = pltpu.SemaphoreType.DMA
    result = pl.pallas_call(
        functools.partial(direct_kernel, spans),
        out_shape=jax.ShapeDtypeStruct((toks, heads, dh), bf16),
        in_specs=[pl.BlockSpec(memory_space=pltpu.VMEM)] * 2 + [hbm, hbm],
        out_specs=hbm,
        scratch_shapes=[
            pltpu.VMEM((toks, heads, dh), bf16),
            pltpu.VMEM((own, BLK, heads, dh), bf16),
            pltpu.VMEM((own, heads, BLK, dh), bf16),
            pltpu.VMEM((2, own, heads, BLK, dh), bf16),
            pltpu.VMEM((2, BLK, heads, dh), bf16),
            pltpu.VMEM((2, rims, heads, BLK, dh), bf16),
            pltpu.VMEM((2, spans, CAP, heads, BLK, dh), bf16),
            pltpu.VMEM((spans, CAP, heads, BLK, dh), bf16),
            pltpu.VMEM((heads, toks, dh), bf16),
            pltpu.VMEM((heads, toks, dh + LANES), f32),
            pltpu.VMEM((heads, toks, LANES), f32),
            pltpu.VMEM((spans, own, 1, CAP * BLK), f32),
            pltpu.VMEM((2, BLK * heads, dh), f32),
            pltpu.VMEM((toks, heads, dh), bf16),
            dma((2,)), dma, dma,
            dma((rims,)), dma((rims,)), dma((rims,)), dma((rims,)),
            dma((spans,)), dma((spans,)), dma((spans,)), dma((spans,)),
            dma((own,)),
        ],
        compiler_params=pltpu.CompilerParams(
            collective_id=0, has_side_effects=True, vmem_limit_bytes=62 << 20),
    )(far_list.T, far_count.reshape(1, -1), queries.reshape(toks, heads, dh), keys_values.reshape(-1, own, BLK, heads, dh))
    return result.reshape(queries.shape)


def solution(mesh):
    in_specs = (
        P(("groups", "ctx"), "head", "rep", None),
        P("rep", ("groups", "ctx"), "head", None),
        P("groups", None),
        P("groups"),
    )
    out_specs = P(("groups", "ctx"), "head", "rep", None)
    return jax.shard_map(
        functools.partial(local, mesh.shape["ctx"], mesh.shape["groups"]),
        mesh=mesh, in_specs=in_specs, out_specs=out_specs, check_vma=False)
```
